32 devices in a mesh: dp: 8 (over z, x), tensor: 4 (over y, core).
Axes of the slice: x: 2, y: 2, z: 4, core: 2. Of those that a mesh axis runs over, the one named last changes fastest.
Arguments:
- inputs: bfloat16 [6304, 512], P(('dp', 'tensor')), may hold values from -6 to 6
- norm_gains: float32 [2, 2, 512], replicated, may hold values from 0.5 to 1.5
- qkv_weight: bfloat16 [2, 512, 3, 512], P(None, 'dp', None, 'tensor'), may hold values from -0.25 to 0.25
- out_weight: bfloat16 [2, 512, 512], P(None, 'tensor', 'dp'), may hold values from -1 to 1
- router_weight: bfloat16 [2, 512, 8], replicated, may hold values from -0.1875 to 0.1875
- expert_in: bfloat16 [2, 8, 512, 2048], P(None, None, 'dp', 'tensor'), may hold values from -0.25 to 0.25
- expert_out: bfloat16 [2, 8, 2048, 512], P(None, None, 'tensor', 'dp'), may hold values from -0.75 to 0.75
- routes: int32 [2, 6304, 2], P(None, 'dp'), may hold values from 0 to 7, all different within a row
- priority: int32 [2, 8, 788], P(None, 'dp'), may hold values from 0 to 787, each once within a row
- cotangent: float32 [6304, 512], P(('dp', 'tensor')), may hold values from -6 to 6
Outputs:
- outputs: bfloat16 [6304, 512], P(('dp', 'tensor'))
- input_grad: float32 [6304, 512], P(('dp', 'tensor'))
- gains_grad: float32 [2, 2, 512], replicated
- qkv_grad: float32 [2, 512, 3, 512], P(None, 'dp', None, 'tensor')
- out_proj_grad: float32 [2, 512, 512], P(None, 'tensor', 'dp')
- router_grad: float32 [2, 512, 8], replicated
- expert_in_grad: float32 [2, 8, 512, 2048], P(None, None, 'dp', 'tensor')
- expert_out_grad: float32 [2, 8, 2048, 512], P(None, None, 'tensor', 'dp')
The draws below stay inside these ranges and needn't reach their ends.
Inputs may be any that keep to these rules, and one draw needn't show every extreme that they name: `routes`: the two experts of a token differ. For each layer and shard, priority lists each of the 788 tokens' ranks once; rank 0 is served first.
All inputs are finite; a program needn't handle non-finite values.
Results may differ from the reference program's by a relative error of at most 0.035.
Values may be sent and summed in bfloat16 or wider, within the bound.
No kernel may reach another device: no remote copies, remote signals or barrier semaphores. Data moves between devices by JAX's collectives and lax.ppermute only.
A program may use at most 192 MiB of HBM per device.

```python
import jax
import jax.numpy as jnp
from jax import lax

D = 512
H = 8
HD = 64
FF = 2048
E = 8
LEN = 197
LAYERS = 2
IMG = 4
TOK_G = 788
TOKENS = 6304
CAP = 247
N_DP = 8


def block_levels(stream_key, shape, shards, least, high):
    def one(position, parts):
        draws = jax.random.uniform(jax.random.fold_in(jax.random.fold_in(stream_key, 6), position), (parts,), jnp.float32, least / len(shards), high / len(shards))
        return jnp.repeat(jnp.exp(draws), shape[position] // parts).reshape((-1,) + (1,) * (len(shape) - position - 1))

    factor_of = one(*shards[0])
    for cut in shards[1:]:
        factor_of = factor_of * one(*cut)
    return factor_of


def picks_of(key, rows, count, top, lift):
    sequence = jax.random.permutation(jax.random.fold_in(key, 1), count)
    pull = sequence
    for power in range(3):
        pull = pull * pull // count
    pull = pull * lift // count
    lots = jax.random.randint(jax.random.fold_in(key, 2), (rows, count), 0, 4096) + pull
    holders = jax.random.permutation(jax.random.fold_in(key, 3), rows)[jnp.arange(count) % rows]
    lots = jnp.where(jnp.arange(rows)[:, None] == holders[None, :], 1 << 14, lots)
    score = lots * count + jnp.arange(count)
    return lax.top_k(score.astype(jnp.int32), top)[1].astype(jnp.int32)


def centred(stream_key, dims, spread, most, cuts=(), kind=jnp.bfloat16):
    drawn = spread * jax.random.normal(stream_key, dims, jnp.float32)
    if cuts:
        drawn = drawn * block_levels(stream_key, dims, cuts, -0.22, 0.18)
    return jnp.clip(drawn, -most, most).astype(kind)


def setup_inputs(seed: int = 0) -> dict:
    streams_of = jax.random.split(jax.random.key(seed), 11)
    inputs = centred(streams_of[0], (TOKENS, D), 1.0, 6.0, ((0, 32),))
    norm_gains = jnp.clip(1.0 + 0.1 * jax.random.normal(streams_of[1], (LAYERS, 2, D), jnp.float32), 0.5, 1.5)
    qkv_weight = centred(streams_of[2], (LAYERS, D, 3, D), D ** -0.5, 0.25, ((1, 8), (3, 4)))
    out_weight = centred(streams_of[3], (LAYERS, D, D), (D // 16) ** -0.5, 1.0, ((1, 4), (2, 8)))
    router_weight = centred(streams_of[4], (LAYERS, D, E), (2 * D) ** -0.5, 0.1875)
    expert_in = centred(streams_of[5], (LAYERS, E, D, FF), D ** -0.5, 0.25, ((2, 8), (3, 4)))
    expert_out = centred(streams_of[6], (LAYERS, E, FF, D), (FF // 32) ** -0.5, 0.75, ((2, 4), (3, 8)))
    routes = picks_of(streams_of[7], LAYERS * TOKENS, E, 2, 2048).reshape((LAYERS, TOKENS, 2))
    priority = jax.vmap(lambda own: jax.random.permutation(own, TOK_G))(jax.random.split(streams_of[8], LAYERS * N_DP)).reshape((LAYERS, N_DP, TOK_G)).astype(jnp.int32)
    cotangent = centred(streams_of[9], (TOKENS, D), 1.0, 6.0, ((0, 32),), jnp.float32)
    return dict(inputs=inputs, norm_gains=norm_gains, qkv_weight=qkv_weight, out_weight=out_weight, router_weight=router_weight, expert_in=expert_in, expert_out=expert_out, routes=routes, priority=priority, cotangent=cotangent)


@jax.custom_vjp
def low(v):
    return lax.optimization_barrier(v.astype(jnp.bfloat16)).astype(jnp.float32)

@jax.custom_vjp
def low_back(v):
    return v

def low_keep(v):
    return (low(v), None)

def low_pass(kept, grad):
    return (grad,)

def back_keep(v):
    return (v, None)

def back_low(kept, grad):
    return (low(grad),)
low.defvjp(low_keep, low_pass)
low_back.defvjp(back_keep, back_low)
NORM_EPS = 1e-06
HIGHEST = lax.Precision.HIGHEST

def layer_norm(hidden, gain_row):
    average = lax.optimization_barrier(jnp.mean(hidden, axis=-1, keepdims=True))
    centered = hidden - average
    variance = lax.optimization_barrier(jnp.mean(centered * centered, axis=-1, keepdims=True))
    return centered * lax.rsqrt(variance + NORM_EPS) * gain_row

def route_slots(expert_ids, ranking, experts, capacity):
    token_count = expert_ids.shape[0]
    serial = jnp.arange(token_count, dtype=jnp.int32)
    by_rank = jnp.zeros((token_count,), jnp.int32).at[ranking].set(serial)
    served = jnp.transpose(expert_ids[by_rank]).reshape(-1)
    expert_range = jnp.arange(experts, dtype=jnp.int32)
    onehot = (served[:, None] == expert_range[None, :]).astype(jnp.int32)
    earlier = (jnp.cumsum(onehot, axis=0) - onehot).astype(jnp.int32)
    slot_served = lax.optimization_barrier(jnp.sum(earlier * onehot, axis=1)).astype(jnp.int32)
    order_key = jnp.arange(2, dtype=jnp.int32)[None, :] * token_count + ranking[:, None]
    slot_index = slot_served[order_key]
    keep_mask = (slot_index < capacity).astype(jnp.float32)
    positions = (expert_ids * capacity + jnp.minimum(slot_index, capacity - 1)).astype(jnp.int32)
    target = jnp.where(slot_index < capacity, positions, experts * capacity).reshape(-1)
    pair_ids = jnp.arange(2 * token_count, dtype=jnp.int32)
    pair_of_slot = jnp.zeros((experts * capacity,), jnp.int32).at[target].set(pair_ids, mode='drop')
    filled = jnp.zeros((experts * capacity,), jnp.float32).at[target].set(1.0, mode='drop')
    return (positions, keep_mask, pair_of_slot, filled)

def attention_branch(normed, qkv_w, proj_w):
    qkv_rows = jnp.dot(normed, qkv_w.reshape(D, 3 * D), precision=HIGHEST).reshape(IMG, LEN, 3, H, HD)
    queries = low_back(low(qkv_rows[:, :, 0]))
    key_rows = low_back(low(qkv_rows[:, :, 1]))
    values = low_back(low(qkv_rows[:, :, 2]))
    scores = low_back(jnp.einsum('bqhd,bkhd->bhqk', queries, key_rows, precision=HIGHEST) * HD ** (-0.5))
    attn_probs = jnp.exp(scores - jax.nn.logsumexp(scores, axis=-1, keepdims=True))
    context = jnp.einsum('bhqk,bkhd->bqhd', low(attn_probs), values, precision=HIGHEST)
    context = low_back(low(context)).reshape(TOK_G, D)
    return low_back(jnp.dot(context, proj_w, precision=HIGHEST))

def expert_branch(normed, router_w, in_w, out_w, expert_ids, routing):
    positions, keep_mask, pair_of_slot, filled = routing
    logits = jnp.dot(normed, router_w, precision=HIGHEST)
    router_probs = jnp.exp(logits - jax.nn.logsumexp(logits, axis=-1, keepdims=True))
    gate_vals = jnp.take_along_axis(router_probs, expert_ids, axis=1) * keep_mask
    dispatched = (normed[pair_of_slot // 2] * filled[:, None]).reshape(E, CAP, D)
    pre_act = low_back(jnp.einsum('ecd,edf->ecf', dispatched, in_w, precision=HIGHEST))
    activated = low(jax.nn.gelu(pre_act, approximate=True))
    expert_y = low_back(jnp.einsum('ecf,efd->ecd', activated, out_w, precision=HIGHEST)).reshape(E * CAP, D)
    return low_back(lax.optimization_barrier(jnp.sum(gate_vals[:, :, None] * expert_y[positions], axis=1)))

def stack_forward(hidden, gains_f, qkv_f, proj_f, router_f, in_f, out_f, route_ids, routing_all):
    for layer_idx in range(LAYERS):
        normed = low(layer_norm(hidden, gains_f[layer_idx, 0]))
        hidden = hidden + attention_branch(normed, qkv_f[layer_idx], proj_f[layer_idx])
        normed = low(layer_norm(hidden, gains_f[layer_idx, 1]))
        hidden = hidden + expert_branch(normed, router_f[layer_idx], in_f[layer_idx], out_f[layer_idx], route_ids[layer_idx], routing_all[layer_idx])
    return hidden

def reference(inputs, norm_gains, qkv_weight, out_weight, router_weight, expert_in, expert_out, routes, priority, cotangent):
    params = tuple((param.astype(jnp.float32) for param in (norm_gains, qkv_weight, out_weight, router_weight, expert_in, expert_out)))
    group_inputs = inputs.astype(jnp.float32).reshape(N_DP, TOK_G, D)
    group_cot = cotangent.astype(jnp.float32).reshape(N_DP, TOK_G, D)
    group_routes = jnp.transpose(routes.reshape(LAYERS, N_DP, TOK_G, 2), (1, 0, 2, 3))
    group_rank = jnp.transpose(priority, (1, 0, 2))

    def one_group(running, packed):
        start_rows, route_ids, ranking, grad_out = packed
        routing_all = [route_slots(route_ids[layer_idx], ranking[layer_idx], E, CAP) for layer_idx in range(LAYERS)]

        def forward(start_hidden, gains_f, qkv_f, proj_f, router_f, in_f, out_f):
            return stack_forward(start_hidden, gains_f, qkv_f, proj_f, router_f, in_f, out_f, route_ids, routing_all)
        result, pullback = jax.vjp(forward, start_rows, params[0], params[1], params[2], params[3], params[4], params[5])
        gradients = pullback(grad_out)
        running = tuple((before + update for before, update in zip(running, gradients[1:])))
        return (running, (result, gradients[0]))
    zero_grads = tuple((jnp.zeros_like(param) for param in params))
    running, (results, input_grads) = lax.scan(one_group, zero_grads, (group_inputs, group_routes, group_rank, group_cot))
    gains_total, qkv_total, proj_total, router_total, in_total, out_total = running
    return (results.reshape(TOKENS, D).astype(jnp.bfloat16), input_grads.reshape(TOKENS, D), gains_total, qkv_total, proj_total, router_total, in_total, out_total)
```

```python
import jax
import jax.numpy as jnp
from jax import lax
from jax.sharding import PartitionSpec as P

HD = 64
LEN = 197
LAYERS = 2
CAP = 247
SLOTS = 256
ROWS = 200
NORM_EPS = 1e-06
f32 = jnp.float32
bf16 = jnp.bfloat16
AXES = ("dp", "tensor")


def layer_norm(hidden, gain_row):
    average = jnp.mean(hidden, axis=-1, keepdims=True)
    centered = hidden - average
    variance = jnp.mean(centered * centered, axis=-1, keepdims=True)
    return centered * lax.rsqrt(variance + NORM_EPS) * gain_row


def norm_back(hidden_rows, gain_row, grad_rows):
    unused, pullback = jax.vjp(layer_norm, hidden_rows, gain_row)
    return pullback(grad_rows)


def gelu_tanh(values):
    return jax.nn.gelu(values, approximate=True)


def gelu_back(pre_act, act_grad):
    unused, pullback = jax.vjp(gelu_tanh, pre_act)
    return pullback(act_grad)[0]


def mm(spec, *args):
    return jnp.einsum(spec, *args, preferred_element_type=f32)


class Place:
    def __init__(self):
        self.dp_size = lax.axis_size("dp")
        self.tensor_size = lax.axis_size("tensor")
        self.count = self.dp_size * self.tensor_size
        self.dp = lax.axis_index("dp")
        self.tensor = lax.axis_index("tensor")
        self.near = (self.dp >> 1) & 1
        self.expert = self.near * self.tensor_size + self.tensor

    def swap(self, value, mask):
        pairs = [(i, i ^ mask) for i in range(self.count)]
        return lax.ppermute(value, AXES, pairs)

    def block(self, mask):
        low = mask & (self.tensor_size - 1)
        return low | ((mask // self.tensor_size) * 2 * self.tensor_size)

    def dp_groups(self):
        return [[d for d in range(self.dp_size) if (d >> 1) & 1 == b] for b in (0, 1)]

    def ordered(self, mine, theirs, bit):
        return jnp.stack([jnp.where(bit, theirs, mine), jnp.where(bit, mine, theirs)])


def gather_attention(place, shard):
    rows, width = shard.shape
    bits = place.dp_size.bit_length() - 1
    held = shard
    for bit in reversed(range(bits)):
        other = place.swap(held, place.tensor_size << bit)
        held = place.ordered(held, other, (place.dp >> bit) & 1)
    held = held.reshape((2,) * bits + (rows, width))
    held = jnp.transpose(held, tuple(reversed(range(bits))) + (bits, bits + 1))
    held = held.reshape(1, place.dp_size * rows, width)
    for mask in (2, 1):
        held = jnp.stack([held, place.swap(held, mask)], axis=1 if mask == 1 else 0)
        held = held.reshape((-1,) + held.shape[2:])
    return held


def scatter_attention(place, blocks, rows):
    bits = place.dp_size.bit_length() - 1
    held = blocks.reshape((2, 2) + blocks.shape[1:])
    held = held[:, 0] + place.swap(held[:, 1], 1)
    held = held[0] + place.swap(held[1], 2)
    for bit in range(bits):
        half = held.reshape((-1, 2, rows << bit) + held.shape[1:]) if False else None
        parts = held.reshape((-1, 2, rows, held.shape[-1]))
        mine = lax.dynamic_index_in_dim(parts, (place.dp >> bit) & 1, 1, keepdims=False)
        theirs = lax.dynamic_index_in_dim(parts, 1 - ((place.dp >> bit) & 1), 1, keepdims=False)
        held = mine + place.swap(theirs, place.tensor_size << bit)
        held = held.reshape(-1, held.shape[-1])
    return held


def plane_exchange(place, blocks):
    even, odd = blocks[0::2], blocks[1::2]
    pair = jnp.stack([even, place.swap(odd, 1)], axis=1)
    got = [pair[0]] + [place.swap(pair[k], place.block(2 * k)) for k in (1, 2, 3)]
    return jnp.concatenate(got, axis=0)


def gather_experts(place, w_in, w_out):
    blocks = jnp.stack([w_in, jnp.swapaxes(w_out, 1, 2)], axis=1)
    experts, unused, rows, width = blocks.shape
    order = place.expert ^ jnp.arange(experts)
    got = plane_exchange(place, blocks[order])
    got = got.reshape((2, place.tensor_size, 2, rows, width))
    got = place.ordered(got[0], got[1], place.near)
    full = lax.all_gather(got, "dp", axis=0, tiled=False, axis_index_groups=place.dp_groups())
    full = full.reshape((-1, 2, 2, place.tensor_size, 2, rows, width))
    full = jnp.transpose(full, (4, 3, 0, 2, 1, 5, 6))
    full = full.reshape((2, place.tensor_size, -1, width))
    return full[0], full[1]


def scatter_experts(place, grad_in, grad_out):
    tensor, model, width = grad_in.shape
    rows = model // place.dp_size
    both = jnp.stack([grad_in, grad_out]).astype(bf16)
    both = both.reshape((2, tensor, -1, 2, 2, rows, width))
    both = jnp.transpose(both, (2, 4, 3, 1, 0, 5, 6))
    both = both.reshape((-1, 2, tensor, 2, rows, width))
    mine = lax.psum_scatter(
        both, "dp", scatter_dimension=0, tiled=False, axis_index_groups=place.dp_groups()
    )
    mine = place.ordered(mine[0], mine[1], place.near)
    got = plane_exchange(place, mine.reshape((-1, 2, rows, width)))
    order = place.expert ^ jnp.arange(got.shape[0])
    got = got[order].astype(f32)
    return got[:, 0], jnp.swapaxes(got[:, 1], 1, 2)


def slot_tables(place, ids, ranking, experts):
    expert_range = jnp.arange(experts, dtype=jnp.int32)[:, None]
    first = (ids[:, 0][None, :] == expert_range)
    second = (ids[:, 1][None, :] == expert_range)
    both = jnp.concatenate([first, second]).astype(bf16)
    earlier = (ranking[:, None] < ranking[None, :]).astype(bf16)
    counts = mm("et,ts->es", both, earlier)
    total = jnp.sum(first.astype(f32), axis=1, keepdims=True)
    slot = jnp.where(first, counts[:experts], jnp.where(second, total + counts[experts:], -1.0))
    slot = jnp.where(slot < CAP, slot, -1.0).astype(jnp.int32)
    mine = lax.dynamic_index_in_dim(slot, place.expert, 0, keepdims=False)
    theirs = lax.dynamic_index_in_dim(slot, place.expert ^ place.tensor_size, 0, keepdims=False)
    both_groups = jnp.stack([mine, place.swap(theirs, 2 * place.tensor_size)])
    both_groups = both_groups.reshape((2, place.tensor_size, LEN))
    both_groups = both_groups[:, place.tensor ^ jnp.arange(place.tensor_size)]
    both_groups = jnp.pad(both_groups, ((0, 0), (0, 0), (0, ROWS - LEN)), constant_values=-1)
    return both_groups.reshape(2, -1)


def onehot_slots(table):
    return (table[:, None, :] == jnp.arange(SLOTS, dtype=jnp.int32)[None, :, None]).astype(bf16)


def dispatch(place, rows_own, hot):
    own = jnp.pad(rows_own, ((0, ROWS - LEN), (0, 0)))
    even = jnp.stack([own] + [place.swap(own, place.block(2 * k)) for k in (1, 2, 3)])
    odd = place.swap(even, 1)
    images = jnp.stack([even, odd], axis=1).reshape(2, -1, own.shape[1])
    picked = mm("gst,gtd->gsd", hot, images).astype(bf16)
    return picked.reshape(-1, own.shape[1])


def combine(place, slot_rows, hot):
    width = slot_rows.shape[1]
    part = mm("gst,gsd->gtd", hot, slot_rows.reshape(2, SLOTS, width)).astype(bf16)
    part = part.reshape(4, 2, ROWS, width)
    both = part[:, 0] + place.swap(part[:, 1], 1)
    got = [both[0]] + [place.swap(both[k], place.block(2 * k)) for k in (1, 2, 3)]
    total = sum(g.astype(f32) for g in got)
    return total[:LEN]


def per_device(
    inputs,
    norm_gains,
    qkv_weight,
    out_weight,
    router_weight,
    expert_in,
    expert_out,
    routes,
    priority,
    cotangent,
):
    place = Place()
    experts = expert_in.shape[1]
    rows = qkv_weight.shape[1]
    scale = HD ** (-0.5)
    hidden = inputs.astype(f32)
    hots = [onehot_slots(slot_tables(place, routes[l], priority[l, 0], experts)) for l in range(LAYERS)]
    attn_w = []
    expert_w = []
    for l in range(LAYERS):
        shard = jnp.concatenate([qkv_weight[l], jnp.swapaxes(out_weight[l], 0, 1)[:, None]], axis=1)
        full = gather_attention(place, shard.reshape(rows, -1))
        attn_w.append(full.reshape(full.shape[0], full.shape[1], 4, -1))
        expert_w.append(gather_experts(place, expert_in[l], expert_out[l]))
    saved = []
    is_mine = (jnp.arange(experts) == place.expert)[None, :]
    for l in range(LAYERS):
        weights = attn_w[l]
        hidden_in = hidden
        normed_a = layer_norm(hidden, norm_gains[l, 0]).astype(bf16)
        qkv = mm("td,jdpc->jptc", normed_a, weights[:, :, :3]).astype(bf16)
        qkv = qkv.reshape(qkv.shape[:3] + (-1, HD))
        queries, key_rows, values = qkv[:, 0], qkv[:, 1], qkv[:, 2]
        scores = mm("jqhd,jkhd->jhqk", queries, key_rows) * scale
        log_total = jax.nn.logsumexp(scores, axis=-1, keepdims=True)
        attn_probs = jnp.exp(scores - log_total)
        context = mm("jhqk,jkhd->jqhd", attn_probs.astype(bf16), values).astype(bf16)
        context = context.reshape(context.shape[:2] + (-1,))
        hidden = hidden + mm("jtc,jdc->td", context, weights[:, :, 3])
        hidden_mid = hidden
        normed_own = layer_norm(hidden, norm_gains[l, 1]).astype(bf16)
        sent = dispatch(place, normed_own, hots[l])
        logits = mm("sd,de->se", sent, router_weight[l])
        probs = jnp.exp(logits - jax.nn.logsumexp(logits, axis=-1, keepdims=True))
        gate = jnp.sum(jnp.where(is_mine, probs, 0.0), axis=1, keepdims=True)
        w_in, w_out = expert_w[l]
        pre_act = mm("sd,jdf->jsf", sent, w_in)
        activated = gelu_tanh(pre_act).astype(bf16)
        expert_y = mm("jsf,jdf->sd", activated, w_out)
        hidden = hidden + combine(place, (gate * expert_y).astype(bf16), hots[l])
        saved.append(
            (hidden_in, normed_a, queries, key_rows, values, log_total, context, hidden_mid,
             sent, probs, gate, pre_act, activated, expert_y)
        )
    grad_hidden = cotangent
    gain_list = [None] * LAYERS
    router_list = [None] * LAYERS
    attn_list = [None] * LAYERS
    in_list = [None] * LAYERS
    out_list = [None] * LAYERS
    for l in reversed(range(LAYERS)):
        (hidden_in, normed_a, queries, key_rows, values, log_total, context, hidden_mid,
         sent, probs, gate, pre_act, activated, expert_y) = saved[l]
        weights = attn_w[l]
        w_in, w_out = expert_w[l]
        branch = dispatch(place, grad_hidden.astype(bf16), hots[l]).astype(f32)
        gate_grad = jnp.sum(branch * expert_y, axis=1, keepdims=True)
        slot_grad = (gate * branch).astype(bf16)
        grad_out = mm("sd,jsf->jdf", slot_grad, activated)
        act_grad = mm("sd,jdf->jsf", slot_grad, w_out)
        pre_grad = gelu_back(pre_act, act_grad).astype(bf16)
        grad_in = mm("sd,jsf->jdf", sent, pre_grad)
        back = mm("jsf,jdf->sd", pre_grad, w_in)
        logit_grad = gate_grad * gate * (is_mine.astype(f32) - probs)
        router_list[l] = lax.dot_general(
            sent.astype(f32), logit_grad, (((0,), (0,)), ((), ())), precision=lax.Precision.HIGHEST
        )
        back = back + lax.dot_general(
            logit_grad, router_weight[l].astype(f32), (((1,), (1,)), ((), ())),
            precision=lax.Precision.HIGHEST,
        )
        normed_grad = combine(place, back.astype(bf16), hots[l])
        in_list[l], out_list[l] = scatter_experts(place, grad_in, grad_out)
        hidden_part, gain_expert = norm_back(hidden_mid, norm_gains[l, 1], normed_grad)
        grad_hidden = grad_hidden + hidden_part
        attn_grad = grad_hidden.astype(bf16)
        proj_grad = mm("td,jtc->jdc", attn_grad, context)
        context_grad = mm("td,jdc->jtc", attn_grad, weights[:, :, 3]).astype(bf16)
        context_grad = context_grad.reshape(queries.shape)
        scores = mm("jqhd,jkhd->jhqk", queries, key_rows) * scale
        attn_probs = jnp.exp(scores - log_total)
        value_grad = mm("jhqk,jqhd->jkhd", attn_probs.astype(bf16), context_grad).astype(bf16)
        probs_grad = mm("jqhd,jkhd->jhqk", context_grad, values)
        score_grad = (
            attn_probs * (probs_grad - jnp.sum(attn_probs * probs_grad, axis=-1, keepdims=True))
        ).astype(bf16)
        query_grad = (mm("jhqk,jkhd->jqhd", score_grad, key_rows) * scale).astype(bf16)
        key_grad = (mm("jhqk,jqhd->jkhd", score_grad, queries) * scale).astype(bf16)
        mixed = jnp.stack([query_grad, key_grad, value_grad], axis=1)
        mixed = mixed.reshape(mixed.shape[:3] + (-1,))
        qkv_grad = mm("td,jptc->jdpc", normed_a, mixed)
        normed_grad = mm("jptc,jdpc->td", mixed, weights[:, :, :3])
        both = jnp.concatenate([qkv_grad, proj_grad[:, :, None]], axis=2).astype(bf16)
        both = both.reshape(both.shape[0], both.shape[1], -1)
        attn_list[l] = scatter_attention(place, both, rows).astype(f32).reshape(rows, 4, -1)
        hidden_part, gain_attn = norm_back(hidden_in, norm_gains[l, 0], normed_grad)
        grad_hidden = grad_hidden + hidden_part
        gain_list[l] = jnp.stack([gain_attn, gain_expert])
    gains, router = jnp.stack(gain_list), jnp.stack(router_list)
    small = jnp.concatenate([gains.reshape(-1), router.reshape(-1)]).reshape(-1, 512)
    for bit in range(place.count.bit_length() - 1):
        small = small + place.swap(small, 1 << bit)
    small = small.reshape(-1)
    gains, router = small[: gains.size].reshape(gains.shape), small[gains.size :].reshape(router.shape)
    return (
        hidden.astype(bf16),
        grad_hidden,
        gains,
        jnp.stack([a[:, :3] for a in attn_list]),
        jnp.stack([jnp.swapaxes(a[:, 3], 0, 1) for a in attn_list]),
        router,
        jnp.stack(in_list),
        jnp.stack(out_list),
    )


def solution(mesh):
    in_specs = (
        P(("dp", "tensor"), None),
        P(),
        P(None, "dp", None, "tensor"),
        P(None, "tensor", "dp"),
        P(),
        P(None, None, "dp", "tensor"),
        P(None, None, "tensor", "dp"),
        P(None, "dp", None),
        P(None, "dp", None),
        P(("dp", "tensor"), None),
    )
    out_specs = (
        P(("dp", "tensor"), None),
        P(("dp", "tensor"), None),
        P(),
        P(None, "dp", None, "tensor"),
        P(None, "tensor", "dp"),
        P(),
        P(None, None, "dp", "tensor"),
        P(None, None, "tensor", "dp"),
    )
    return jax.shard_map(
        per_device, mesh=mesh, in_specs=in_specs, out_specs=out_specs, check_vma=False
    )
```

```python
import jax
import jax.numpy as jnp
from jax import lax
from jax.experimental import pallas as pl
from jax.experimental.pallas import tpu as pltpu
from jax.sharding import PartitionSpec as P

HD = 64
LEN = 197
LAYERS = 2
CAP = 247
SLOTS = 256
ROWS = 200
NORM_EPS = 1e-06
f32 = jnp.float32
bf16 = jnp.bfloat16
AXES = ("dp", "tensor")


def mm(spec, *args):
    return jnp.einsum(spec, *args, preferred_element_type=f32)


class Place:
    def __init__(self):
        self.dp_size = lax.axis_size("dp")
        self.tensor_size = lax.axis_size("tensor")
        self.count = self.dp_size * self.tensor_size
        self.dp = lax.axis_index("dp")
        self.tensor = lax.axis_index("tensor")
        self.near = self.dp & 1
        self.expert = self.near * self.tensor_size + self.tensor

    def swap(self, value, mask):
        pairs = [(i, i ^ mask) for i in range(self.count)]
        return lax.ppermute(value, AXES, pairs)

    def dp_groups(self):
        return [[d for d in range(self.dp_size) if d & 1 == b] for b in (0, 1)]

    def ordered(self, mine, theirs, bit):
        return jnp.stack([jnp.where(bit, theirs, mine), jnp.where(bit, mine, theirs)])


def gather_attention(place, shard):
    rows, width = shard.shape
    bits = place.dp_size.bit_length() - 1
    held = shard
    for bit in reversed(range(bits)):
        other = place.swap(held, place.tensor_size << bit)
        held = place.ordered(held, other, (place.dp >> bit) & 1)
    held = held.reshape((2,) * bits + (rows, width))
    held = jnp.transpose(held, tuple(reversed(range(bits))) + (bits, bits + 1))
    held = held.reshape(1, place.dp_size * rows, width)
    for mask in (2, 1):
        held = jnp.stack([held, place.swap(held, mask)], axis=1 if mask == 1 else 0)
        held = held.reshape((-1,) + held.shape[2:])
    return held


def scatter_attention(place, blocks, rows):
    bits = place.dp_size.bit_length() - 1
    held = blocks.reshape((2, 2) + blocks.shape[1:])
    held = held[:, 0] + place.swap(held[:, 1], 1)
    held = held[0] + place.swap(held[1], 2)
    for bit in range(bits):
        parts = held.reshape((-1, 2, rows, held.shape[-1]))
        mine = lax.dynamic_index_in_dim(parts, (place.dp >> bit) & 1, 1, keepdims=False)
        theirs = lax.dynamic_index_in_dim(parts, 1 - ((place.dp >> bit) & 1), 1, keepdims=False)
        held = mine + place.swap(theirs, place.tensor_size << bit)
        held = held.reshape(-1, held.shape[-1])
    return held


def plane_exchange(place, blocks):
    even, odd = blocks[0::2], blocks[1::2]
    pair = jnp.stack([even, place.swap(odd, 1)], axis=1)
    got = [pair[0]] + [place.swap(pair[k], 2 * k) for k in (1, 2, 3)]
    return jnp.concatenate(got, axis=0)


def gather_experts(place, w_in, w_out):
    blocks = jnp.stack([w_in, jnp.swapaxes(w_out, 1, 2)], axis=1)
    experts, unused, rows, width = blocks.shape
    order = place.expert ^ jnp.arange(experts)
    got = plane_exchange(place, blocks[order])
    got = got.reshape((2, place.tensor_size, 2, rows, width))
    got = place.ordered(got[0], got[1], place.near)
    full = lax.all_gather(got, "dp", axis=0, tiled=False, axis_index_groups=place.dp_groups())
    full = jnp.transpose(full, (3, 2, 0, 1, 4, 5))
    full = full.reshape((2, place.tensor_size, -1, width))
    return full[0], full[1]


def scatter_experts(place, grad_in, grad_out):
    tensor, model, width = grad_in.shape
    rows = model // place.dp_size
    both = jnp.stack([grad_in, grad_out]).astype(bf16)
    both = both.reshape((2, tensor, -1, 2, rows, width))
    both = jnp.transpose(both, (2, 3, 1, 0, 4, 5))
    mine = lax.psum_scatter(
        both, "dp", scatter_dimension=0, tiled=False, axis_index_groups=place.dp_groups()
    )
    mine = place.ordered(mine[0], mine[1], place.near)
    got = plane_exchange(place, mine.reshape((-1, 2, rows, width)))
    order = place.expert ^ jnp.arange(got.shape[0])
    got = got[order].astype(f32)
    return got[:, 0], jnp.swapaxes(got[:, 1], 1, 2)


def slot_rows(place, ids, ranking, experts):
    expert_range = jnp.arange(experts, dtype=jnp.int32)[:, None]
    first = ids[:, 0][None, :] == expert_range
    second = ids[:, 1][None, :] == expert_range
    both = jnp.concatenate([first, second]).astype(bf16)
    earlier = (ranking[:, None] < ranking[None, :]).astype(bf16)
    counts = mm("et,ts->es", both, earlier)
    total = jnp.sum(first.astype(f32), axis=1, keepdims=True)
    slot = jnp.where(first, counts[:experts], jnp.where(second, total + counts[experts:], -1.0))
    slot = jnp.where(slot < CAP, slot, -1.0).astype(jnp.int32)
    mine = lax.dynamic_index_in_dim(slot, place.expert, 0, keepdims=False)
    theirs = lax.dynamic_index_in_dim(slot, place.expert ^ place.tensor_size, 0, keepdims=False)
    return mine, theirs


def slot_tables(place, mine, theirs):
    groups = jnp.stack([mine, theirs])
    groups = groups.reshape((2, place.tensor_size, LEN))
    groups = groups[:, place.tensor ^ jnp.arange(place.tensor_size)]
    groups = jnp.pad(groups, ((0, 0), (0, 0), (0, ROWS - LEN)), constant_values=-1)
    table = groups.reshape(-1, ROWS)
    return table, jnp.swapaxes(table, 0, 1)


def exchange_rows(place, own):
    even = [own] + [place.swap(own, 2 * k) for k in (1, 2, 3)]
    odd = [place.swap(rows, 1) for rows in even]
    return [rows for pair in zip(even, odd) for rows in pair]


def add_kernel(even, odd, *sums):
    for k, target in enumerate(sums):
        target[...] = (even[k].astype(f32) + odd[k].astype(f32)).astype(bf16)


def pair_rows(place, parts):
    even, odd = parts
    odd = place.swap(odd, 1)
    return list(pl.pallas_call(
        add_kernel,
        out_shape=(jax.ShapeDtypeStruct(even.shape[1:], bf16),) * 4,
        in_specs=[vmem()] * 2,
        out_specs=(vmem(),) * 4,
        cost_estimate=pl.CostEstimate(flops=1, transcendentals=0, bytes_accessed=1),
        name="add_rows",
    )(even, odd))


def send_rows(place, sums):
    return [sums[0]] + [place.swap(sums[k], 2 * k) for k in (1, 2, 3)]


def dot(a, b):
    return lax.dot_general(a, b, (((1,), (0,)), ((), ())), preferred_element_type=f32)


def dot_t(a, b):
    return lax.dot_general(a, b, (((1,), (1,)), ((), ())), preferred_element_type=f32)


def t_dot(a, b):
    return lax.dot_general(a, b, (((0,), (0,)), ((), ())), preferred_element_type=f32)


def normalized(rows):
    average = jnp.mean(rows, axis=-1, keepdims=True)
    centered = rows - average
    variance = jnp.mean(centered * centered, axis=-1, keepdims=True)
    scale = lax.rsqrt(variance + NORM_EPS)
    return centered * scale, scale


def norm_grad(rows, gain, grad):
    unit, scale = normalized(rows)
    scaled = grad * gain
    pull = scaled - jnp.mean(scaled, axis=-1, keepdims=True)
    pull = pull - unit * jnp.mean(scaled * unit, axis=-1, keepdims=True)
    return scale * pull, jnp.sum(grad * unit, axis=0, keepdims=True)


def head_masks():
    lane = lax.broadcasted_iota(jnp.int32, (1, 2 * HD), 1)
    return lane < HD, lane >= HD


def only(values, mask):
    return jnp.where(mask, values.astype(f32), 0.0).astype(bf16)


def head_probs(queries, keys, mask):
    scores = dot_t(only(queries, mask), keys) * (HD ** (-0.5))
    valid = lax.broadcasted_iota(jnp.int32, scores.shape, 1) < LEN
    scores = jnp.where(valid, scores, -1e30)
    top = jnp.max(scores, axis=-1, keepdims=True)
    weights = jnp.exp(scores - top)
    return weights / jnp.sum(weights, axis=-1, keepdims=True)


def weight_copies(off_ref, pieces, buffer, sems):
    result = []
    for j, piece in enumerate(pieces):
        count, rows, unused = piece.shape
        result.append([
            pltpu.make_async_copy(
                piece.at[i],
                buffer.at[j, pl.ds(pl.multiple_of(off_ref[i], rows), rows)],
                sems.at[j, i],
            )
            for i in range(count)
        ])
    return result


def padded_rows(ref, scratch):
    if ref.shape[0] == ROWS:
        return ref[...].astype(f32)
    scratch[...] = jnp.zeros_like(scratch)
    scratch[0 : ref.shape[0]] = ref[...].astype(f32)
    return scratch[...]


def attention_forward_kernel(piece_count, extra_count, off_ref, base, *refs):
    pieces, refs = refs[:piece_count], refs[piece_count:]
    extra, refs = refs[:extra_count], refs[extra_count:]
    gains, w0, w1, w2, w3, hidden, mid, normed, qkv, ctx, scratch, wbuf, sems = refs
    copies = weight_copies(off_ref, (w0, w1, w2, w3), wbuf, sems)
    for group in copies:
        for copy in group:
            copy.start()
    rows = padded_rows(base, scratch)
    for piece in pieces:
        rows = rows + piece[...].astype(f32)
    hidden[...] = rows
    unit, unused = normalized(rows)
    normed_a = (unit * gains[0:1]).astype(bf16)
    low, high = head_masks()
    total = rows
    for j in range(4):
        for copy in copies[j]:
            copy.wait()
        part = dot(normed_a, wbuf[j, :, : 6 * HD]).astype(bf16)
        qkv[:, j * 6 * HD : (j + 1) * 6 * HD] = part
        queries, keys, values = part[:, : 2 * HD], part[:, 2 * HD : 4 * HD], part[:, 4 * HD :]
        first = dot(head_probs(queries, keys, low).astype(bf16), values)
        second = dot(head_probs(queries, keys, high).astype(bf16), values)
        context = jnp.where(low, first, second).astype(bf16)
        ctx[:, j * 2 * HD : (j + 1) * 2 * HD] = context
        total = total + dot_t(context, wbuf[j, :, 6 * HD :])
    mid[...] = total
    unit, unused = normalized(total)
    normed[0] = (unit * gains[1:2]).astype(bf16)
    for ref in extra:
        normed[1] = padded_rows(ref, scratch).astype(bf16)


def vmem():
    return pl.BlockSpec(memory_space=pltpu.VMEM)


def smem():
    return pl.BlockSpec(memory_space=pltpu.SMEM)


def hbm():
    return pl.BlockSpec(memory_space=pl.ANY)


def params():
    return pltpu.CompilerParams(vmem_limit_bytes=60 << 20)


def attention_forward(offsets, base, pieces, extra, gains, weights):
    width = base.shape[1]
    shape = jax.ShapeDtypeStruct
    return pl.pallas_call(
        lambda *refs: attention_forward_kernel(len(pieces), len(extra), *refs),
        out_shape=(
            shape((ROWS, width), f32),
            shape((ROWS, width), f32),
            shape((1 + len(extra), ROWS, width), bf16),
            shape((ROWS, 3 * width), bf16),
            shape((ROWS, width), bf16),
        ),
        in_specs=[smem(), vmem()] + [vmem()] * (len(pieces) + len(extra)) + [vmem()] + [hbm()] * 4,
        out_specs=[vmem()] * 5,
        scratch_shapes=[
            pltpu.VMEM((ROWS, width), f32),
            pltpu.VMEM((4, width, width), bf16),
            pltpu.SemaphoreType.DMA((4, weights[0].shape[0])),
        ],
        compiler_params=params(),
        cost_estimate=pl.CostEstimate(flops=1, transcendentals=0, bytes_accessed=1),
        name="attention_forward",
    )(offsets, base, *pieces, *extra, gains, *weights)


def attention_backward_kernel(
    off_ref, base, p0, p1, p2, p3, hidden_in, hidden_mid, gains, w0, w1, w2, w3, qkv, ctx,
    grad_out, branch, gain_out, g0, g1, g2, g3, scratch, wbuf, gbuf, sems, out_sems,
):
    copies = weight_copies(off_ref, (w0, w1, w2, w3), wbuf, sems)
    for group in copies:
        for copy in group:
            copy.start()
    grad = padded_rows(base, scratch)
    normed_grad = p0[...].astype(f32) + p1[...].astype(f32) + p2[...].astype(f32) + p3[...].astype(f32)
    part, gain_expert = norm_grad(hidden_mid[...], gains[1:2], normed_grad)
    grad = grad + part
    attn_grad = grad.astype(bf16)
    attn_grad_t = attn_grad.T
    rows_in = hidden_in[...]
    unit, unused = normalized(rows_in)
    normed_t = (unit * gains[0:1]).astype(bf16).T
    low, high = head_masks()
    scale = HD ** (-0.5)
    normed_part = jnp.zeros_like(grad)
    sends = []
    for j, target in enumerate((g0, g1, g2, g3)):
        for copy in copies[j]:
            copy.wait()
        part = qkv[:, j * 6 * HD : (j + 1) * 6 * HD]
        queries, keys, values = part[:, : 2 * HD], part[:, 2 * HD : 4 * HD], part[:, 4 * HD :]
        context = ctx[:, j * 2 * HD : (j + 1) * 2 * HD]
        context_grad = dot(attn_grad, wbuf[j, :, 6 * HD :]).astype(bf16)
        query_grad, key_grad, value_grad = None, None, None
        for mask in (low, high):
            probs = head_probs(queries, keys, mask)
            v_grad = t_dot(probs.astype(bf16), context_grad)
            probs_grad = dot_t(only(context_grad, mask), values)
            inner = jnp.sum(probs * probs_grad, axis=-1, keepdims=True)
            score_grad = (probs * (probs_grad - inner)).astype(bf16)
            q_grad = dot(score_grad, keys) * scale
            k_grad = t_dot(score_grad, queries) * scale
            if query_grad is None:
                query_grad, key_grad, value_grad = q_grad, k_grad, v_grad
            else:
                query_grad = jnp.where(mask, q_grad, query_grad).astype(bf16)
                key_grad = jnp.where(mask, k_grad, key_grad).astype(bf16)
                value_grad = jnp.where(mask, v_grad, value_grad).astype(bf16)
        for place, mixed in enumerate((query_grad, key_grad, value_grad)):
            lanes = slice(place * 2 * HD, (place + 1) * 2 * HD)
            gbuf[j, :, lanes] = dot(normed_t, mixed).astype(bf16)
            normed_part = normed_part + dot_t(mixed, wbuf[j, :, lanes])
        gbuf[j, :, 6 * HD :] = dot(attn_grad_t, context).astype(bf16)
        count, rows, unused = target.shape
        for i in range(count):
            send = pltpu.make_async_copy(
                gbuf.at[j, pl.ds(pl.multiple_of(off_ref[i], rows), rows)], target.at[i], out_sems.at[j, i]
            )
            send.start()
            sends.append(send)
    part, gain_attn = norm_grad(rows_in, gains[0:1], normed_part)
    grad = grad + part
    grad_out[...] = grad[: grad_out.shape[0]]
    branch[...] = grad.astype(bf16)
    gain_out[...] = jnp.concatenate([gain_attn, gain_expert], axis=0)
    for send in sends:
        send.wait()


def attention_backward(offsets, base, pieces, hidden_in, hidden_mid, gains, weights, qkv, ctx, out_rows):
    width = base.shape[1]
    shape = jax.ShapeDtypeStruct
    blocks = weights[0].shape
    return pl.pallas_call(
        attention_backward_kernel,
        out_shape=(
            shape((out_rows, width), f32),
            shape((ROWS, width), bf16),
            shape((2, width), f32),
        ) + (shape(blocks, bf16),) * 4,
        in_specs=[smem()] + [vmem()] * 8 + [hbm()] * 4 + [vmem()] * 2,
        out_specs=[vmem()] * 3 + [hbm()] * 4,
        scratch_shapes=[
            pltpu.VMEM((ROWS, width), f32),
            pltpu.VMEM((4, width, width), bf16),
            pltpu.VMEM((4, width, width), bf16),
            pltpu.SemaphoreType.DMA((4, blocks[0])),
            pltpu.SemaphoreType.DMA((4, blocks[0])),
        ],
        compiler_params=params(),
        cost_estimate=pl.CostEstimate(flops=1, transcendentals=0, bytes_accessed=1),
        name="attention_backward",
    )(offsets, base, *pieces, hidden_in, hidden_mid, gains, *weights, qkv, ctx)


def split(values):
    high = values.astype(bf16)
    return high, (values - high.astype(f32)).astype(bf16)


ROOT = 0.7978845608028654
CUBE = 0.044715


def expert_kernel(plan, off_ref, me_ref, table, table_t, router, *refs):
    forward, backward = plan.images is not None, plan.grads is not None
    piece_count = len(plan.w_in)
    refs = list(refs)

    def take(count):
        taken, refs[:count] = refs[:count], []
        return taken

    tokens = take(plan.token_arrays)
    sent_in, y_in = take(2) if not forward else (None, None)
    sources = take(plan.weight_arrays)
    parts = take(2) if forward else None
    sent_out, y_out = take(2) if forward and not backward else (None, None)
    if backward:
        back_parts = take(2)
        (router_grad,) = take(1)
        targets = take(len(plan.grad_shapes))
    in_buf, out_buf, sent_buf, y_buf = take(4)
    if backward:
        slot_buf, slot_t, sent_t, back_buf, gbuf, out_sems = take(6)
    (sems,) = take(1)

    near, chunks, rows, width = plan.block

    def loads(c, which):
        result = []
        for m in range(piece_count):
            for n in range(near):
                at = pl.ds(pl.multiple_of(off_ref[m * near + n], rows), rows)
                index, part = (plan.w_in, plan.w_out)[which][m]
                piece = sources[index] if part is None else sources[index].at[part]
                buf = (in_buf, out_buf)[which]
                result.append(
                    pltpu.make_async_copy(piece.at[n, c], buf.at[c, at], sems.at[which, c, m * near + n])
                )
        return result

    for c in range(chunks):
        for which in (0, 1):
            for copy in loads(c, which):
                copy.start()

    def gather(images):
        for g in (0, 1):
            total = None
            for t in range(4):
                j = g * 4 + t
                slot = lax.broadcasted_iota(jnp.int32, (SLOTS, ROWS), 0)
                hot = (table[j : j + 1, :] == slot).astype(f32).astype(bf16)
                index, layer = images[j]
                part = dot(hot, tokens[index][layer])
                total = part if total is None else total + part
            yield g, total

    def scatter(slot_rows, parts):
        for g in (0, 1):
            for t in range(4):
                j = g * 4 + t
                slot = lax.broadcasted_iota(jnp.int32, (ROWS, SLOTS), 1)
                hot = (table_t[:, j : j + 1] == slot).astype(f32).astype(bf16)
                part = dot(hot, slot_rows[g * SLOTS : (g + 1) * SLOTS]).astype(bf16)
                parts[j % 2][j // 2] = part

    if forward:
        for g, rows_g in gather(plan.images):
            sent_buf[g * SLOTS : (g + 1) * SLOTS] = rows_g.astype(bf16)
    else:
        sent_buf[...] = sent_in[...]
    sent = sent_buf[...]
    logits = dot(sent, router[...])
    top = jnp.max(logits, axis=-1, keepdims=True)
    weights = jnp.exp(logits - top)
    probs = weights / jnp.sum(weights, axis=-1, keepdims=True)
    is_mine = lax.broadcasted_iota(jnp.int32, probs.shape, 1) == me_ref[0]
    gate = jnp.sum(jnp.where(is_mine, probs, 0.0), axis=-1, keepdims=True)

    if forward:
        y_buf[...] = jnp.zeros_like(y_buf)

        @pl.loop(0, chunks)
        def _(c):
            for copy in loads(c, 0):
                copy.wait()
            pre = dot(sent_buf[...], in_buf[c])
            act = (0.5 * pre * (1.0 + jnp.tanh(ROOT * (pre + CUBE * (pre * pre * pre))))).astype(bf16)
            for copy in loads(c, 1):
                copy.wait()
            y_buf[...] += dot_t(act, out_buf[c])

        expert_y = y_buf[...]
        scatter((gate * expert_y).astype(bf16), parts)
        if not backward:
            sent_out[...] = sent
            y_out[...] = expert_y
    else:
        for c in range(chunks):
            for which in (0, 1):
                for copy in loads(c, which):
                    copy.wait()
        expert_y = y_in[...]
    if not backward:
        return

    for g, rows_g in gather(plan.grads):
        part = slice(g * SLOTS, (g + 1) * SLOTS)
        slot_buf[part] = (gate[part] * rows_g).astype(bf16)
        y_buf[part] = rows_g
    gate_grad = jnp.sum(y_buf[...] * expert_y, axis=-1, keepdims=True)
    slot_t[...] = slot_buf[...].T
    sent_t[...] = sent.T
    logit_grad = gate_grad * gate * (is_mine.astype(f32) - probs)
    first, second = split(logit_grad)
    router_grad[...] = dot(sent_t[...], first) + dot(sent_t[...], second)
    back_buf[...] = dot_t(first, router[...]) + dot_t(second, router[...])

    def stores(c, which):
        result = []
        for m in range(piece_count):
            for n in range(near):
                at = pl.ds(pl.multiple_of(off_ref[m * near + n], rows), rows)
                index, part = (plan.grad_in, plan.grad_out)[which][m]
                piece = targets[index] if part is None else targets[index].at[part]
                result.append(
                    pltpu.make_async_copy(
                        gbuf.at[which, c, at], piece.at[n, c], out_sems.at[which, c, m * near + n]
                    )
                )
        return result

    @pl.loop(0, chunks)
    def _(c):
        pre = dot(sent_buf[...], in_buf[c])
        square = pre * pre
        bend = jnp.tanh(ROOT * (pre + CUBE * (square * pre)))
        act = (0.5 * pre * (1.0 + bend)).astype(bf16)
        gbuf[1, c] = dot(slot_t[...], act).astype(bf16)
        for copy in stores(c, 1):
            copy.start()
        slope = 0.5 * (1.0 + bend) + 0.5 * pre * (1.0 - bend * bend) * (ROOT * (1.0 + 3.0 * CUBE * square))
        pre_grad = (dot(slot_buf[...], out_buf[c]) * slope).astype(bf16)
        gbuf[0, c] = dot(sent_t[...], pre_grad).astype(bf16)
        for copy in stores(c, 0):
            copy.start()
        back_buf[...] += dot_t(pre_grad, in_buf[c])

    scatter(back_buf[...].astype(bf16), back_parts)

    @pl.loop(0, chunks)
    def _(c):
        for which in (0, 1):
            for copy in stores(c, which):
                copy.wait()


class Plan:
    def __init__(self, block, images, grads, w_in, w_out, grad_shapes, grad_in, grad_out):
        self.block = block
        self.images, self.grads = images, grads
        self.w_in, self.w_out = w_in, w_out
        self.grad_shapes, self.grad_in, self.grad_out = grad_shapes, grad_in, grad_out


def expert_layer(plan, offsets, me, tables, router, tokens, saved, weights):
    forward, backward = plan.images is not None, plan.grads is not None
    plan.token_arrays, plan.weight_arrays = len(tokens), len(weights)
    width = router.shape[0]
    count = len(plan.w_in)
    near, chunks, rows, hidden = plan.block
    slots = 2 * SLOTS
    shape = jax.ShapeDtypeStruct
    token_part = shape((4, ROWS, width), bf16)
    operands = [offsets, me, *tables, router, *tokens]
    in_specs = [smem(), smem()] + [vmem()] * (3 + len(tokens))
    if not forward:
        operands += saved
        in_specs += [vmem()] * 2
    operands += weights
    in_specs += [hbm()] * len(weights)
    out_shape, out_specs = [], []
    if forward:
        out_shape += [token_part] * 2
    if forward and not backward:
        out_shape += [shape((slots, width), bf16), shape((slots, width), f32)]
    if backward:
        out_shape += [token_part] * 2 + [shape(router.shape, f32)]
    out_specs += [vmem()] * len(out_shape)
    if backward:
        out_shape += [shape(s, bf16) for s in plan.grad_shapes]
        out_specs += [hbm()] * len(plan.grad_shapes)
    scratch = [
        pltpu.VMEM((chunks, width, hidden), bf16),
        pltpu.VMEM((chunks, width, hidden), bf16),
        pltpu.VMEM((slots, width), bf16),
        pltpu.VMEM((slots, width), f32),
    ]
    if backward:
        scratch += [
            pltpu.VMEM((slots, width), bf16),
            pltpu.VMEM((width, slots), bf16),
            pltpu.VMEM((width, slots), bf16),
            pltpu.VMEM((slots, width), f32),
            pltpu.VMEM((2, chunks, width, hidden), bf16),
            pltpu.SemaphoreType.DMA((2, chunks, count * near)),
        ]
    scratch += [pltpu.SemaphoreType.DMA((2, chunks, count * near))]
    return pl.pallas_call(
        lambda *refs: expert_kernel(plan, *refs),
        out_shape=tuple(out_shape),
        in_specs=in_specs,
        out_specs=tuple(out_specs),
        scratch_shapes=scratch,
        compiler_params=params(),
        cost_estimate=pl.CostEstimate(flops=1, transcendentals=0, bytes_accessed=1),
        name="expert_layer",
    )(*operands)


def padded_bf16(rows):
    return jnp.pad(rows.astype(bf16), ((0, ROWS - LEN), (0, 0)))


def per_device(
    inputs,
    norm_gains,
    qkv_weight,
    out_weight,
    router_weight,
    expert_in,
    expert_out,
    routes,
    priority,
    cotangent,
):
    place = Place()
    experts = expert_in.shape[1]
    rows = qkv_weight.shape[1]
    zero = jnp.zeros((1,), jnp.int32)
    attn_off, expert_off = zero, zero
    me = place.expert.astype(jnp.int32).reshape(1)
    attn_w, expert_w, tables = [], [], []
    for l in range(LAYERS):
        shard = jnp.concatenate([qkv_weight[l], jnp.swapaxes(out_weight[l], 0, 1)[:, None]], axis=1)
        full = gather_attention(place, shard.reshape(rows, -1))
        attn_w.append([full[j][None] for j in range(4)])
        expert_w.append([w[None] for w in gather_experts(place, expert_in[l], expert_out[l])])
        mine, theirs = slot_rows(place, routes[l], priority[l, 0], experts)
        tables.append(slot_tables(place, mine, place.swap(theirs, place.tensor_size)))
    hidden_in, hidden_mid, qkv, ctx = {}, {}, {}, {}
    base, pieces = inputs, []
    saved = None
    gain_list, router_list, in_list, out_list, attn_list = {}, {}, {}, {}, {}
    for l in range(LAYERS):
        last = l == LAYERS - 1
        hidden_in[l], hidden_mid[l], normed, qkv[l], ctx[l] = attention_forward(
            attn_off, base, pieces, [], norm_gains[l], attn_w[l]
        )
        images = exchange_rows(place, normed)
        block = expert_w[l][0].shape
        at = [(0, None)], [(1, None)]
        here = [(j, 0) for j in range(8)]
        if last:
            grads = exchange_rows(place, padded_bf16(cotangent)[None])
            plan = Plan(block, here, [(j + 8, 0) for j in range(8)], *at, [block] * 2, *at)
            result = expert_layer(
                plan, expert_off, me, tables[l], router_weight[l], images + grads, None, expert_w[l]
            )
            tail = send_rows(place, pair_rows(place, result[:2]))
            result = result[2:]
            outputs = hidden_mid[l] + sum(p.astype(f32) for p in tail)
        else:
            plan = Plan(block, here, None, *at, None, None, None)
            *result, sent, expert_y = expert_layer(
                plan, expert_off, me, tables[l], router_weight[l], images, None, expert_w[l]
            )
            base, pieces = hidden_mid[l], send_rows(place, pair_rows(place, result))
            saved = [sent, expert_y]
    base = cotangent
    for l in reversed(range(LAYERS)):
        back = send_rows(place, pair_rows(place, result[:2]))
        router_list[l], *pieces = result[2:]
        in_list[l], out_list[l] = scatter_experts(place, pieces[0][0], pieces[1][0])
        base, branch, gain_list[l], *parts = attention_backward(
            attn_off, base, back, hidden_in[l], hidden_mid[l], norm_gains[l], attn_w[l], qkv[l], ctx[l],
            ROWS if l else LEN,
        )
        if l:
            grads = exchange_rows(place, branch[None])
            plan = Plan(block, None, here, *at, [block] * 2, *at)
            result = expert_layer(
                plan, expert_off, me, tables[l - 1], router_weight[l - 1], grads, saved, expert_w[l - 1]
            )
        total = scatter_attention(place, jnp.concatenate(parts), rows)
        attn_list[l] = total.astype(f32).reshape(rows, 4, -1)
    gains = jnp.stack([gain_list[l] for l in range(LAYERS)])
    router = jnp.stack([router_list[l] for l in range(LAYERS)])
    small = jnp.concatenate([gains.reshape(-1), router.reshape(-1)]).reshape(-1, 512)
    for bit in range(place.count.bit_length() - 1):
        small = small + place.swap(small, 1 << bit)
    small = small.reshape(-1)
    gains, router = small[: gains.size].reshape(gains.shape), small[gains.size :].reshape(router.shape)
    return (
        outputs[:LEN].astype(bf16),
        base,
        gains,
        jnp.stack([attn_list[l][:, :3] for l in range(LAYERS)]),
        jnp.stack([jnp.swapaxes(attn_list[l][:, 3], 0, 1) for l in range(LAYERS)]),
        router,
        jnp.stack([in_list[l] for l in range(LAYERS)]),
        jnp.stack([out_list[l] for l in range(LAYERS)]),
    )


CORE, Y, X, NEAR, FAR = 1, 2, 4, 8, 16


def tie(*values):
    return lax.optimization_barrier(values)


def expert_blocks(place, w_in, w_out):
    order = place.expert ^ jnp.arange(w_in.shape[0])
    return jnp.stack([w_in[order], jnp.swapaxes(w_out, 1, 2)[order]])


def plane_blocks(place, blocks):
    two, count, rows, width = blocks.shape
    odd = place.swap(blocks[:, 1::2], CORE)
    pair = jnp.stack([blocks[:, 0::2], odd], axis=2)
    got = [pair[:, 0]] + [place.swap(pair[:, k], 2 * k) for k in (1, 2, 3)]
    return jnp.stack(got, axis=1).reshape(two, 2, count // 2, rows, width)


def mixed(place, value, even, odd):
    pairs = [(i, i ^ (odd if i & CORE else even)) for i in range(place.count)]
    return lax.ppermute(value, AXES, pairs)


def attention_shard(qkv_weight, out_weight):
    shard = jnp.concatenate([qkv_weight, jnp.swapaxes(out_weight, 0, 1)[:, None]], axis=1)
    return shard.reshape(shard.shape[0], -1)


def widen(place, held, mask):
    return jnp.concatenate([held, place.swap(held, mask)])


def halve(place, held, mask):
    half = held.shape[0] // 2
    return held[:half] + place.swap(held[half:], mask)


def plane_sums(place, mine):
    shape = mine.shape
    return plane_blocks(place, mine.reshape((2, -1) + shape[3:])).reshape((2, -1) + shape[3:])


def unpack_sums(place, got):
    got = got[:, place.expert ^ jnp.arange(got.shape[1])].astype(f32)
    return got[0], jnp.swapaxes(got[1], 1, 2)


def per_device_plane(
    inputs,
    norm_gains,
    qkv_weight,
    out_weight,
    router_weight,
    expert_in,
    expert_out,
    routes,
    priority,
    cotangent,
):
    place = Place()
    swap = place.swap
    experts = expert_in.shape[1]
    rows = qkv_weight.shape[1]
    attn_order = [x | n * 2 | f * 4 for x in (0, 1) for n in (0, 1) for f in (0, 1)]
    attn_off = ((place.dp ^ jnp.array(attn_order, jnp.int32)) * rows).astype(jnp.int32)
    core = place.tensor & CORE
    replica = jnp.stack([jnp.zeros_like(core), 4 - 2 * core, 2 + 2 * core, 6 + 0 * core])
    expert_off = ((place.dp ^ replica[:, None] ^ jnp.arange(2)[None, :]) * rows).reshape(-1).astype(jnp.int32)
    me = place.expert.astype(jnp.int32).reshape(1)
    block = (2, place.tensor_size, rows, expert_in.shape[3])

    own0 = plane_blocks(place, expert_blocks(place, expert_in[0], expert_out[0]))
    held = jnp.stack([attention_shard(qkv_weight[l], out_weight[l]) for l in (0, 1)])[None]
    held = widen(place, widen(place, held, FAR), NEAR)
    held, own0 = tie(held, own0)
    a0 = mixed(place, own0, FAR, NEAR)
    held0 = widen(place, held[:, 0], X)
    over0 = swap(held0, Y)
    over0, a0, blocks1 = tie(over0, a0, expert_blocks(place, expert_in[1], expert_out[1]))
    b0, c0 = mixed(place, own0, NEAR, FAR), mixed(place, a0, NEAR, FAR)
    weights0 = [held0, swap(held0, CORE), over0, swap(over0, CORE)]
    own1 = plane_blocks(place, blocks1)

    hidden_in0, hidden_mid0, normed, qkv0, ctx0 = attention_forward(
        attn_off, inputs, [], [], norm_gains[0], weights0
    )
    normed, own1 = tie(normed, own1)
    slots = [slot_rows(place, routes[l], priority[l, 0], experts) for l in (0, 1)]
    images = exchange_rows(place, normed)
    images[6], held1, theirs = tie(images[6], held[:, 1], jnp.stack([s[1] for s in slots]))
    theirs = swap(theirs, X)
    tables = [slot_tables(place, slots[l][0], theirs[l]) for l in (0, 1)]
    held1 = widen(place, held1, X)
    over1 = swap(held1, Y)
    weights1 = [held1, swap(held1, CORE), over1, swap(over1, CORE)]
    b0, c0, own1 = tie(b0, c0, own1)
    a1 = mixed(place, own1, FAR, NEAR)
    first = [(j, 0) for j in range(8)]
    second = [(j, 1) for j in range(8)]
    parts = [[(m, io) for m in range(4)] for io in (0, 1)]
    *rows0, sent, expert_y = expert_layer(
        Plan(block, first, None, *parts, None, None, None),
        expert_off, me, tables[0], router_weight[0], images, None, [own0, a0, b0, c0],
    )
    rows0[0], weights1[2] = tie(rows0[0], weights1[2])
    pieces = send_rows(place, pair_rows(place, rows0))
    *pieces, a1, own1 = tie(*pieces, a1, own1)
    b1, c1 = mixed(place, own1, NEAR, FAR), mixed(place, a1, NEAR, FAR)
    hidden_in1, hidden_mid1, normed, qkv1, ctx1 = attention_forward(
        attn_off, hidden_mid0, pieces, [cotangent], norm_gains[1], weights1
    )
    images = exchange_rows(place, normed)
    grad_shapes = [(2,) + block] * 4
    result = expert_layer(
        Plan(block, first, second, *parts, grad_shapes, *parts),
        expert_off, me, tables[1], router_weight[1], images, None, [own1, a1, b1, c1],
    )
    out_rows, back_rows, router1, (own, a, b, c) = result[:2], result[2:4], result[4], result[5:]

    b, c = mixed(place, b, NEAR, FAR), mixed(place, c, NEAR, FAR)
    pieces = send_rows(place, pair_rows(place, back_rows))
    grad1, branch, gains1, *parts1 = attention_backward(
        attn_off, cotangent, pieces, hidden_in1, hidden_mid1, norm_gains[1], weights1, qkv1, ctx1, ROWS
    )
    images = exchange_rows(place, branch[None])
    tied = tie(*images, a, b, c, *parts1)
    images, (a, b, c), parts1 = tied[:8], tied[8:11], tied[11:]
    a = mixed(place, a + c, FAR, NEAR)
    near1, far1 = parts1[0] + swap(parts1[1], CORE), parts1[2] + swap(parts1[3], CORE)
    far1 = swap(far1, Y)
    result = expert_layer(
        Plan(block, None, first, *parts, grad_shapes, *parts),
        expert_off, me, tables[0], router_weight[0], images, [sent, expert_y], [own0, a0, b0, c0],
    )
    back_rows, router0, (own0, a0, b0, c0) = list(result[:2]), result[2], result[3:]
    back_rows[0], far1 = tie(back_rows[0], far1)
    attn_sum1 = near1 + far1
    c0 = mixed(place, c0, NEAR, FAR)
    pieces = send_rows(place, pair_rows(place, back_rows))
    tied = tie(*pieces, a, b, own, *out_rows)
    pieces, (a, b, own), out_rows = tied[:4], tied[4:7], tied[7:]
    tail = send_rows(place, pair_rows(place, out_rows))
    grad0, unused, gains0, *parts0 = attention_backward(
        attn_off, grad1, pieces, hidden_in0, hidden_mid0, norm_gains[0], weights0, qkv0, ctx0, LEN
    )
    gains0, c0, b0, a, b, own, *tail = tie(gains0, c0, b0, a, b, own, *tail)
    a0, b0 = mixed(place, a0 + c0, FAR, NEAR), mixed(place, b0, NEAR, FAR)
    outputs = hidden_mid1 + sum(p.astype(f32) for p in tail)
    sum1 = plane_sums(place, own + b + a)
    near0, far0 = parts0[0] + swap(parts0[1], CORE), parts0[2] + swap(parts0[3], CORE)
    far0, sum1 = tie(far0, sum1)
    attn_sum0 = near0 + swap(far0, Y)
    attn_sum = halve(place, jnp.stack([attn_sum0, attn_sum1], axis=1), X)
    gains, router = jnp.stack([gains0, gains1]), jnp.stack([router0, router1])
    small = jnp.concatenate([gains.reshape(-1), router.reshape(-1)]).reshape(-1, 512)
    for mask in (CORE, Y, X):
        small = small + swap(small, mask)
    small, attn_sum, a0, b0 = tie(small, attn_sum, a0, b0)
    for mask in (NEAR, FAR):
        attn_sum = halve(place, attn_sum, mask)
        small = small + swap(small, mask)
    in1, out1 = unpack_sums(place, sum1)
    in0, out0 = unpack_sums(place, plane_sums(place, own0 + a0 + b0))
    small = small.reshape(-1)
    gains, router = small[: gains.size].reshape(gains.shape), small[gains.size :].reshape(router.shape)
    attn = attn_sum.astype(f32).reshape(2, rows, 4, -1)
    return (
        outputs[:LEN].astype(bf16),
        grad0,
        gains,
        attn[:, :, :3],
        jnp.swapaxes(attn[:, :, 3], 1, 2),
        router,
        jnp.stack([in0, in1]),
        jnp.stack([out0, out1]),
    )


def solution(mesh):
    in_specs = (
        P(("dp", "tensor"), None),
        P(),
        P(None, "dp", None, "tensor"),
        P(None, "tensor", "dp"),
        P(),
        P(None, None, "dp", "tensor"),
        P(None, None, "tensor", "dp"),
        P(None, "dp", None),
        P(None, "dp", None),
        P(("dp", "tensor"), None),
    )
    out_specs = (
        P(("dp", "tensor"), None),
        P(("dp", "tensor"), None),
        P(),
        P(None, "dp", None, "tensor"),
        P(None, "tensor", "dp"),
        P(),
        P(None, None, "dp", "tensor"),
        P(None, None, "tensor", "dp"),
    )
    fast = mesh.shape["dp"] == 8 and mesh.shape["tensor"] == 4 and LAYERS == 2
    return jax.shard_map(
        per_device_plane if fast else per_device, mesh=mesh, in_specs=in_specs, out_specs=out_specs, check_vma=False
    )
```

```python
import jax
import jax.numpy as jnp
from jax import lax
from jax.experimental import pallas as pl
from jax.experimental.pallas import tpu as pltpu
from jax.sharding import PartitionSpec as P

HD = 64
LEN = 197
LAYERS = 2
CAP = 247
SLOTS = 256
ROWS = 200
NORM_EPS = 1e-06
f32 = jnp.float32
bf16 = jnp.bfloat16
AXES = ("dp", "tensor")


def mm(spec, *args):
    return jnp.einsum(spec, *args, preferred_element_type=f32)


class Place:
    def __init__(self):
        self.dp_size = lax.axis_size("dp")
        self.tensor_size = lax.axis_size("tensor")
        self.count = self.dp_size * self.tensor_size
        self.dp = lax.axis_index("dp")
        self.tensor = lax.axis_index("tensor")
        self.near = self.dp & 1
        self.expert = self.near * self.tensor_size + self.tensor

    def swap(self, value, mask):
        pairs = [(i, i ^ mask) for i in range(self.count)]
        return lax.ppermute(value, AXES, pairs)

    def dp_groups(self):
        return [[d for d in range(self.dp_size) if d & 1 == b] for b in (0, 1)]

    def ordered(self, mine, theirs, bit):
        return jnp.stack([jnp.where(bit, theirs, mine), jnp.where(bit, mine, theirs)])


def gather_attention(place, shard):
    rows, width = shard.shape
    bits = place.dp_size.bit_length() - 1
    held = shard
    for bit in reversed(range(bits)):
        other = place.swap(held, place.tensor_size << bit)
        held = place.ordered(held, other, (place.dp >> bit) & 1)
    held = held.reshape((2,) * bits + (rows, width))
    held = jnp.transpose(held, tuple(reversed(range(bits))) + (bits, bits + 1))
    held = held.reshape(1, place.dp_size * rows, width)
    for mask in (2, 1):
        held = jnp.stack([held, place.swap(held, mask)], axis=1 if mask == 1 else 0)
        held = held.reshape((-1,) + held.shape[2:])
    return held


def scatter_attention(place, blocks, rows):
    bits = place.dp_size.bit_length() - 1
    held = blocks.reshape((2, 2) + blocks.shape[1:])
    held = held[:, 0] + place.swap(held[:, 1], 1)
    held = held[0] + place.swap(held[1], 2)
    for bit in range(bits):
        parts = held.reshape((-1, 2, rows, held.shape[-1]))
        mine = lax.dynamic_index_in_dim(parts, (place.dp >> bit) & 1, 1, keepdims=False)
        theirs = lax.dynamic_index_in_dim(parts, 1 - ((place.dp >> bit) & 1), 1, keepdims=False)
        held = mine + place.swap(theirs, place.tensor_size << bit)
        held = held.reshape(-1, held.shape[-1])
    return held


def plane_exchange(place, blocks):
    even, odd = blocks[0::2], blocks[1::2]
    pair = jnp.stack([even, place.swap(odd, 1)], axis=1)
    got = [pair[0]] + [place.swap(pair[k], 2 * k) for k in (1, 2, 3)]
    return jnp.concatenate(got, axis=0)


def gather_experts(place, w_in, w_out):
    blocks = jnp.stack([w_in, jnp.swapaxes(w_out, 1, 2)], axis=1)
    experts, unused, rows, width = blocks.shape
    order = place.expert ^ jnp.arange(experts)
    got = plane_exchange(place, blocks[order])
    got = got.reshape((2, place.tensor_size, 2, rows, width))
    got = place.ordered(got[0], got[1], place.near)
    full = lax.all_gather(got, "dp", axis=0, tiled=False, axis_index_groups=place.dp_groups())
    full = jnp.transpose(full, (3, 2, 0, 1, 4, 5))
    full = full.reshape((2, place.tensor_size, -1, width))
    return full[0], full[1]


def scatter_experts(place, grad_in, grad_out):
    tensor, model, width = grad_in.shape
    rows = model // place.dp_size
    both = jnp.stack([grad_in, grad_out]).astype(bf16)
    both = both.reshape((2, tensor, -1, 2, rows, width))
    both = jnp.transpose(both, (2, 3, 1, 0, 4, 5))
    mine = lax.psum_scatter(
        both, "dp", scatter_dimension=0, tiled=False, axis_index_groups=place.dp_groups()
    )
    mine = place.ordered(mine[0], mine[1], place.near)
    got = plane_exchange(place, mine.reshape((-1, 2, rows, width)))
    order = place.expert ^ jnp.arange(got.shape[0])
    got = got[order].astype(f32)
    return got[:, 0], jnp.swapaxes(got[:, 1], 1, 2)


LANES = 256


def slot_kernel(experts, mine_ref, ids, rank, mine, theirs):
    tensor = mine.shape[1]
    expert, other = mine_ref[0], mine_ref[1]
    here = mine_ref[2]
    for l in range(ids.shape[0]):
        choice = lax.broadcasted_iota(jnp.int32, (experts, tensor * LANES), 0)
        first, second = ids[l, 0:1, :] == choice, ids[l, 1:2, :] == choice
        order = rank[l : l + 1, :].astype(f32)
        column = jnp.broadcast_to(order, (8, tensor * LANES)).T[:, 0:1]
        earlier = (column < order).astype(f32).astype(bf16)
        both = jnp.concatenate([first.astype(f32), second.astype(f32)]).astype(bf16)
        counts = dot(both, earlier)
        total = jnp.sum(first.astype(f32), axis=1, keepdims=True)
        slot = jnp.where(first, counts[:experts], jnp.where(second, total + counts[experts:], -1.0))
        slot = jnp.where(slot < CAP, slot, -1.0)
        for which, target in ((expert, mine), (other, theirs)):
            row = jnp.sum(jnp.where(choice == which, slot, 0.0), axis=0, keepdims=True).astype(jnp.int32)
            for t in range(tensor):
                target[l, pl.ds(jnp.bitwise_xor(here, t), 1), :] = row[:, t * LANES : (t + 1) * LANES]


def slot_tables(place, routes, priority, experts):
    layers, count, unused = routes.shape
    spread = ((0, 0), (0, 0), (0, 0), (0, LANES - LEN))
    ids = jnp.swapaxes(routes, 1, 2).reshape(layers, 2, -1, LEN)
    ids = jnp.pad(ids, spread, constant_values=-1).reshape(layers, 2, -1)
    rank = jnp.pad(priority.reshape(layers, 1, -1, LEN), spread).reshape(layers, -1)
    where = jnp.stack([place.expert, place.expert ^ place.tensor_size, place.tensor]).astype(jnp.int32)
    shape = jax.ShapeDtypeStruct((layers, place.tensor_size, LANES), jnp.int32)
    mine, theirs = pl.pallas_call(
        lambda *refs: slot_kernel(experts, *refs),
        out_shape=(shape, shape),
        in_specs=[smem(), vmem(), vmem()],
        out_specs=(vmem(), vmem()),
        compiler_params=params(),
        cost_estimate=pl.CostEstimate(flops=1, transcendentals=0, bytes_accessed=1),
        name="slots",
    )(where, ids, rank)
    return mine, place.swap(theirs, place.tensor_size)


def exchange_rows(place, own):
    even = [own] + [place.swap(own, 2 * k) for k in (1, 2, 3)]
    odd = [place.swap(rows, 1) for rows in even]
    return [rows for pair in zip(even, odd) for rows in pair]


def add_kernel(even, odd, *sums):
    for k, target in enumerate(sums):
        target[...] = (even[k].astype(f32) + odd[k].astype(f32)).astype(bf16)


def pair_rows(place, parts, *others):
    even, odd = parts
    odd, *others = lax.optimization_barrier((place.swap(odd, 1), *others))
    return list(pl.pallas_call(
        add_kernel,
        out_shape=(jax.ShapeDtypeStruct(even.shape[1:], bf16),) * 4,
        in_specs=[vmem()] * 2,
        out_specs=(vmem(),) * 4,
        cost_estimate=pl.CostEstimate(flops=1, transcendentals=0, bytes_accessed=1),
        name="add_rows",
    )(even, odd)) + others


def send_rows(place, sums):
    return [sums[0]] + [place.swap(sums[k], 2 * k) for k in (1, 2, 3)]


def dot(a, b):
    return lax.dot_general(a, b, (((1,), (0,)), ((), ())), preferred_element_type=f32)


def dot_t(a, b):
    return lax.dot_general(a, b, (((1,), (1,)), ((), ())), preferred_element_type=f32)


def t_dot(a, b):
    return lax.dot_general(a, b, (((0,), (0,)), ((), ())), preferred_element_type=f32)


def normalized(rows):
    average = jnp.mean(rows, axis=-1, keepdims=True)
    centered = rows - average
    variance = jnp.mean(centered * centered, axis=-1, keepdims=True)
    scale = lax.rsqrt(variance + NORM_EPS)
    return centered * scale, scale


def norm_grad(rows, gain, grad):
    unit, scale = normalized(rows)
    scaled = grad * gain
    pull = scaled - jnp.mean(scaled, axis=-1, keepdims=True)
    pull = pull - unit * jnp.mean(scaled * unit, axis=-1, keepdims=True)
    return scale * pull, jnp.sum(grad * unit, axis=0, keepdims=True)


def head_masks():
    lane = lax.broadcasted_iota(jnp.int32, (1, 2 * HD), 1)
    return lane < HD, lane >= HD


def only(values, mask):
    return jnp.where(mask, values.astype(f32), 0.0).astype(bf16)


def head_probs(queries, keys, mask):
    scores = dot_t(only(queries, mask), keys) * (HD ** (-0.5))
    valid = lax.broadcasted_iota(jnp.int32, scores.shape, 1) < LEN
    scores = jnp.where(valid, scores, -1e30)
    top = jnp.max(scores, axis=-1, keepdims=True)
    weights = jnp.exp(scores - top)
    return weights / jnp.sum(weights, axis=-1, keepdims=True)


def weight_copies(off_ref, pieces, buffer, sems):
    result = []
    for j, piece in enumerate(pieces):
        count, rows, unused = piece.shape
        result.append([
            pltpu.make_async_copy(
                piece.at[i],
                buffer.at[j, pl.ds(pl.multiple_of(off_ref[i], rows), rows)],
                sems.at[j, i],
            )
            for i in range(count)
        ])
    return result


def padded_rows(ref, scratch):
    if ref.shape[0] == ROWS:
        return ref[...].astype(f32)
    scratch[...] = jnp.zeros_like(scratch)
    scratch[0 : ref.shape[0]] = ref[...].astype(f32)
    return scratch[...]


def attention_forward_kernel(piece_count, extra_count, off_ref, base, *refs):
    pieces, refs = refs[:piece_count], refs[piece_count:]
    extra, refs = refs[:extra_count], refs[extra_count:]
    gains, w0, w1, w2, w3, hidden, mid, normed, qkv, ctx, scratch, wbuf, sems = refs
    copies = weight_copies(off_ref, (w0, w1, w2, w3), wbuf, sems)
    for group in copies:
        for copy in group:
            copy.start()
    rows = padded_rows(base, scratch)
    for piece in pieces:
        rows = rows + piece[...].astype(f32)
    hidden[...] = rows
    unit, unused = normalized(rows)
    normed_a = (unit * gains[0:1]).astype(bf16)
    low, high = head_masks()
    total = rows
    for j in range(4):
        for copy in copies[j]:
            copy.wait()
        part = dot(normed_a, wbuf[j, :, : 6 * HD]).astype(bf16)
        qkv[:, j * 6 * HD : (j + 1) * 6 * HD] = part
        queries, keys, values = part[:, : 2 * HD], part[:, 2 * HD : 4 * HD], part[:, 4 * HD :]
        first = dot(head_probs(queries, keys, low).astype(bf16), values)
        second = dot(head_probs(queries, keys, high).astype(bf16), values)
        context = jnp.where(low, first, second).astype(bf16)
        ctx[:, j * 2 * HD : (j + 1) * 2 * HD] = context
        total = total + dot_t(context, wbuf[j, :, 6 * HD :])
    mid[...] = total
    unit, unused = normalized(total)
    normed[0] = (unit * gains[1:2]).astype(bf16)
    for ref in extra:
        normed[1] = padded_rows(ref, scratch).astype(bf16)


def vmem():
    return pl.BlockSpec(memory_space=pltpu.VMEM)


def smem():
    return pl.BlockSpec(memory_space=pltpu.SMEM)


def hbm():
    return pl.BlockSpec(memory_space=pl.ANY)


def params():
    return pltpu.CompilerParams(vmem_limit_bytes=60 << 20)


def attention_forward(offsets, base, pieces, extra, gains, weights):
    width = base.shape[1]
    shape = jax.ShapeDtypeStruct
    return pl.pallas_call(
        lambda *refs: attention_forward_kernel(len(pieces), len(extra), *refs),
        out_shape=(
            shape((ROWS, width), f32),
            shape((ROWS, width), f32),
            shape((1 + len(extra), ROWS, width), bf16),
            shape((ROWS, 3 * width), bf16),
            shape((ROWS, width), bf16),
        ),
        in_specs=[smem(), vmem()] + [vmem()] * (len(pieces) + len(extra)) + [vmem()] + [hbm()] * 4,
        out_specs=[vmem()] * 5,
        scratch_shapes=[
            pltpu.VMEM((ROWS, width), f32),
            pltpu.VMEM((4, width, width), bf16),
            pltpu.SemaphoreType.DMA((4, weights[0].shape[0])),
        ],
        compiler_params=params(),
        cost_estimate=pl.CostEstimate(flops=1, transcendentals=0, bytes_accessed=1),
        name="attention_forward",
    )(offsets, base, *pieces, *extra, gains, *weights)


def attention_backward_kernel(
    off_ref, base, p0, p1, p2, p3, hidden_in, hidden_mid, gains, w0, w1, w2, w3, qkv, ctx,
    grad_out, branch, gain_out, g0, g1, g2, g3, scratch, wbuf, gbuf, sems, out_sems,
):
    copies = weight_copies(off_ref, (w0, w1, w2, w3), wbuf, sems)
    for group in copies:
        for copy in group:
            copy.start()
    grad = padded_rows(base, scratch)
    normed_grad = p0[...].astype(f32) + p1[...].astype(f32) + p2[...].astype(f32) + p3[...].astype(f32)
    part, gain_expert = norm_grad(hidden_mid[...], gains[1:2], normed_grad)
    grad = grad + part
    attn_grad = grad.astype(bf16)
    attn_grad_t = attn_grad.T
    rows_in = hidden_in[...]
    unit, unused = normalized(rows_in)
    normed_t = (unit * gains[0:1]).astype(bf16).T
    low, high = head_masks()
    scale = HD ** (-0.5)
    normed_part = jnp.zeros_like(grad)
    sends = []
    for j, target in enumerate((g0, g1, g2, g3)):
        for copy in copies[j]:
            copy.wait()
        part = qkv[:, j * 6 * HD : (j + 1) * 6 * HD]
        queries, keys, values = part[:, : 2 * HD], part[:, 2 * HD : 4 * HD], part[:, 4 * HD :]
        context = ctx[:, j * 2 * HD : (j + 1) * 2 * HD]
        context_grad = dot(attn_grad, wbuf[j, :, 6 * HD :]).astype(bf16)
        query_grad, key_grad, value_grad = None, None, None
        for mask in (low, high):
            probs = head_probs(queries, keys, mask)
            v_grad = t_dot(probs.astype(bf16), context_grad)
            probs_grad = dot_t(only(context_grad, mask), values)
            inner = jnp.sum(probs * probs_grad, axis=-1, keepdims=True)
            score_grad = (probs * (probs_grad - inner)).astype(bf16)
            q_grad = dot(score_grad, keys) * scale
            k_grad = t_dot(score_grad, queries) * scale
            if query_grad is None:
                query_grad, key_grad, value_grad = q_grad, k_grad, v_grad
            else:
                query_grad = jnp.where(mask, q_grad, query_grad).astype(bf16)
                key_grad = jnp.where(mask, k_grad, key_grad).astype(bf16)
                value_grad = jnp.where(mask, v_grad, value_grad).astype(bf16)
        for place, mixed in enumerate((query_grad, key_grad, value_grad)):
            lanes = slice(place * 2 * HD, (place + 1) * 2 * HD)
            gbuf[j, :, lanes] = dot(normed_t, mixed).astype(bf16)
            normed_part = normed_part + dot_t(mixed, wbuf[j, :, lanes])
        gbuf[j, :, 6 * HD :] = dot(attn_grad_t, context).astype(bf16)
        count, rows, unused = target.shape
        for i in range(count):
            send = pltpu.make_async_copy(
                gbuf.at[j, pl.ds(pl.multiple_of(off_ref[i], rows), rows)], target.at[i], out_sems.at[j, i]
            )
            send.start()
            sends.append(send)
    part, gain_attn = norm_grad(rows_in, gains[0:1], normed_part)
    grad = grad + part
    grad_out[...] = grad[: grad_out.shape[0]]
    branch[...] = grad.astype(bf16)
    gain_out[...] = jnp.concatenate([gain_attn, gain_expert], axis=0)
    for send in sends:
        send.wait()


def attention_backward(offsets, base, pieces, hidden_in, hidden_mid, gains, weights, qkv, ctx, out_rows):
    width = base.shape[1]
    shape = jax.ShapeDtypeStruct
    blocks = weights[0].shape
    return pl.pallas_call(
        attention_backward_kernel,
        out_shape=(
            shape((out_rows, width), f32),
            shape((ROWS, width), bf16),
            shape((2, width), f32),
        ) + (shape(blocks, bf16),) * 4,
        in_specs=[smem()] + [vmem()] * 8 + [hbm()] * 4 + [vmem()] * 2,
        out_specs=[vmem()] * 3 + [hbm()] * 4,
        scratch_shapes=[
            pltpu.VMEM((ROWS, width), f32),
            pltpu.VMEM((4, width, width), bf16),
            pltpu.VMEM((4, width, width), bf16),
            pltpu.SemaphoreType.DMA((4, blocks[0])),
            pltpu.SemaphoreType.DMA((4, blocks[0])),
        ],
        compiler_params=params(),
        cost_estimate=pl.CostEstimate(flops=1, transcendentals=0, bytes_accessed=1),
        name="attention_backward",
    )(offsets, base, *pieces, hidden_in, hidden_mid, gains, *weights, qkv, ctx)


def split(values):
    high = values.astype(bf16)
    return high, (values - high.astype(f32)).astype(bf16)


ROOT = 0.7978845608028654
CUBE = 0.044715


def expert_kernel(plan, off_ref, me_ref, mine, theirs, router, *refs):
    forward, backward = plan.images is not None, plan.grads is not None
    piece_count = len(plan.w_in)
    refs = list(refs)

    def take(count):
        taken, refs[:count] = refs[:count], []
        return taken

    tokens = take(plan.token_arrays)
    sent_in, y_in = take(2) if not forward else (None, None)
    sources = take(plan.weight_arrays)
    parts = take(2) if forward else None
    sent_out, y_out = take(2) if forward and not backward else (None, None)
    if backward:
        back_parts = take(2)
        (router_grad,) = take(1)
        targets = take(len(plan.grad_shapes))
    in_buf, out_buf, sent_buf, y_buf = take(4)
    if backward:
        slot_buf, slot_t, sent_t, back_buf, gbuf, out_sems = take(6)
    (sems,) = take(1)

    near, chunks, rows, width = plan.block

    def loads(c, which):
        result = []
        for m in range(piece_count):
            for n in range(near):
                at = pl.ds(pl.multiple_of(off_ref[m * near + n], rows), rows)
                index, part = (plan.w_in, plan.w_out)[which][m]
                piece = sources[index] if part is None else sources[index].at[part]
                buf = (in_buf, out_buf)[which]
                result.append(
                    pltpu.make_async_copy(piece.at[n, c], buf.at[c, at], sems.at[which, c, m * near + n])
                )
        return result

    for c in range(chunks):
        for which in (0, 1):
            for copy in loads(c, which):
                copy.start()

    def hot_rows(g, t, slot):
        row = (mine, theirs)[g][plan.layer, t : t + 1, :][:, :ROWS]
        return (row == slot).astype(f32).astype(bf16)

    def gather(images):
        for g in (0, 1):
            total = None
            for t in range(4):
                j = g * 4 + t
                slot = lax.broadcasted_iota(jnp.int32, (SLOTS, ROWS), 0)
                hot = hot_rows(g, t, slot)
                index, layer = images[j]
                part = dot(hot, tokens[index][layer])
                total = part if total is None else total + part
            yield g, total

    def scatter(slot_rows, parts):
        for g in (0, 1):
            for t in range(4):
                j = g * 4 + t
                slot = lax.broadcasted_iota(jnp.int32, (SLOTS, ROWS), 0)
                part = t_dot(hot_rows(g, t, slot), slot_rows[g * SLOTS : (g + 1) * SLOTS]).astype(bf16)
                parts[j % 2][j // 2] = part

    if forward:
        for g, rows_g in gather(plan.images):
            sent_buf[g * SLOTS : (g + 1) * SLOTS] = rows_g.astype(bf16)
    else:
        sent_buf[...] = sent_in[...]
    sent = sent_buf[...]
    logits = dot(sent, router[...])
    top = jnp.max(logits, axis=-1, keepdims=True)
    weights = jnp.exp(logits - top)
    probs = weights / jnp.sum(weights, axis=-1, keepdims=True)
    is_mine = lax.broadcasted_iota(jnp.int32, probs.shape, 1) == me_ref[0]
    gate = jnp.sum(jnp.where(is_mine, probs, 0.0), axis=-1, keepdims=True)

    if forward:
        y_buf[...] = jnp.zeros_like(y_buf)

        @pl.loop(0, chunks)
        def _(c):
            for copy in loads(c, 0):
                copy.wait()
            pre = dot(sent_buf[...], in_buf[c])
            act = (0.5 * pre * (1.0 + jnp.tanh(ROOT * (pre + CUBE * (pre * pre * pre))))).astype(bf16)
            for copy in loads(c, 1):
                copy.wait()
            y_buf[...] += dot_t(act, out_buf[c])

        expert_y = y_buf[...]
        scatter((gate * expert_y).astype(bf16), parts)
        if not backward:
            sent_out[...] = sent
            y_out[...] = expert_y
    else:
        for c in range(chunks):
            for which in (0, 1):
                for copy in loads(c, which):
                    copy.wait()
        expert_y = y_in[...]
    if not backward:
        return

    for g, rows_g in gather(plan.grads):
        part = slice(g * SLOTS, (g + 1) * SLOTS)
        slot_buf[part] = (gate[part] * rows_g).astype(bf16)
        y_buf[part] = rows_g
    gate_grad = jnp.sum(y_buf[...] * expert_y, axis=-1, keepdims=True)
    slot_t[...] = slot_buf[...].T
    sent_t[...] = sent.T
    logit_grad = gate_grad * gate * (is_mine.astype(f32) - probs)
    first, second = split(logit_grad)
    router_grad[...] = dot(sent_t[...], first) + dot(sent_t[...], second)
    back_buf[...] = dot_t(first, router[...]) + dot_t(second, router[...])

    def stores(c, which):
        result = []
        for m in range(piece_count):
            for n in range(near):
                at = pl.ds(pl.multiple_of(off_ref[m * near + n], rows), rows)
                index, part = (plan.grad_in, plan.grad_out)[which][m]
                piece = targets[index] if part is None else targets[index].at[part]
                result.append(
                    pltpu.make_async_copy(
                        gbuf.at[which, c, at], piece.at[n, c], out_sems.at[which, c, m * near + n]
                    )
                )
        return result

    @pl.loop(0, chunks)
    def _(c):
        pre = dot(sent_buf[...], in_buf[c])
        square = pre * pre
        bend = jnp.tanh(ROOT * (pre + CUBE * (square * pre)))
        act = (0.5 * pre * (1.0 + bend)).astype(bf16)
        gbuf[1, c] = dot(slot_t[...], act).astype(bf16)
        for copy in stores(c, 1):
            copy.start()
        slope = 0.5 * (1.0 + bend) + 0.5 * pre * (1.0 - bend * bend) * (ROOT * (1.0 + 3.0 * CUBE * square))
        pre_grad = (dot(slot_buf[...], out_buf[c]) * slope).astype(bf16)
        gbuf[0, c] = dot(sent_t[...], pre_grad).astype(bf16)
        for copy in stores(c, 0):
            copy.start()
        back_buf[...] += dot_t(pre_grad, in_buf[c])

    scatter(back_buf[...].astype(bf16), back_parts)

    @pl.loop(0, chunks)
    def _(c):
        for which in (0, 1):
            for copy in stores(c, which):
                copy.wait()


class Plan:
    def __init__(self, layer, block, images, grads, w_in, w_out, grad_shapes, grad_in, grad_out):
        self.layer, self.block = layer, block
        self.images, self.grads = images, grads
        self.w_in, self.w_out = w_in, w_out
        self.grad_shapes, self.grad_in, self.grad_out = grad_shapes, grad_in, grad_out


def expert_layer(plan, offsets, me, tables, router, tokens, saved, weights, flops=1):
    forward, backward = plan.images is not None, plan.grads is not None
    plan.token_arrays, plan.weight_arrays = len(tokens), len(weights)
    width = router.shape[0]
    count = len(plan.w_in)
    near, chunks, rows, hidden = plan.block
    slots = 2 * SLOTS
    shape = jax.ShapeDtypeStruct
    token_part = shape((4, ROWS, width), bf16)
    operands = [offsets, me, *tables, router, *tokens]
    in_specs = [smem(), smem()] + [vmem()] * (3 + len(tokens))
    if not forward:
        operands += saved
        in_specs += [vmem()] * 2
    operands += weights
    in_specs += [hbm()] * len(weights)
    out_shape, out_specs = [], []
    if forward:
        out_shape += [token_part] * 2
    if forward and not backward:
        out_shape += [shape((slots, width), bf16), shape((slots, width), f32)]
    if backward:
        out_shape += [token_part] * 2 + [shape(router.shape, f32)]
    out_specs += [vmem()] * len(out_shape)
    if backward:
        out_shape += [shape(s, bf16) for s in plan.grad_shapes]
        out_specs += [hbm()] * len(plan.grad_shapes)
    scratch = [
        pltpu.VMEM((chunks, width, hidden), bf16),
        pltpu.VMEM((chunks, width, hidden), bf16),
        pltpu.VMEM((slots, width), bf16),
        pltpu.VMEM((slots, width), f32),
    ]
    if backward:
        scratch += [
            pltpu.VMEM((slots, width), bf16),
            pltpu.VMEM((width, slots), bf16),
            pltpu.VMEM((width, slots), bf16),
            pltpu.VMEM((slots, width), f32),
            pltpu.VMEM((2, chunks, width, hidden), bf16),
            pltpu.SemaphoreType.DMA((2, chunks, count * near)),
        ]
    scratch += [pltpu.SemaphoreType.DMA((2, chunks, count * near))]
    return pl.pallas_call(
        lambda *refs: expert_kernel(plan, *refs),
        out_shape=tuple(out_shape),
        in_specs=in_specs,
        out_specs=tuple(out_specs),
        scratch_shapes=scratch,
        compiler_params=params(),
        cost_estimate=pl.CostEstimate(flops=flops, transcendentals=0, bytes_accessed=1),
        name="expert_layer",
    )(*operands)


def padded_bf16(rows):
    return jnp.pad(rows.astype(bf16), ((0, ROWS - LEN), (0, 0)))


def per_device(
    inputs,
    norm_gains,
    qkv_weight,
    out_weight,
    router_weight,
    expert_in,
    expert_out,
    routes,
    priority,
    cotangent,
):
    place = Place()
    experts = expert_in.shape[1]
    rows = qkv_weight.shape[1]
    zero = jnp.zeros((1,), jnp.int32)
    attn_off, expert_off = zero, zero
    me = place.expert.astype(jnp.int32).reshape(1)
    attn_w, expert_w = [], []
    tables = slot_tables(place, routes, priority, experts)
    for l in range(LAYERS):
        shard = jnp.concatenate([qkv_weight[l], jnp.swapaxes(out_weight[l], 0, 1)[:, None]], axis=1)
        full = gather_attention(place, shard.reshape(rows, -1))
        attn_w.append([full[j][None] for j in range(4)])
        expert_w.append([w[None] for w in gather_experts(place, expert_in[l], expert_out[l])])
    hidden_in, hidden_mid, qkv, ctx = {}, {}, {}, {}
    base, pieces = inputs, []
    saved = None
    gain_list, router_list, in_list, out_list, attn_list = {}, {}, {}, {}, {}
    for l in range(LAYERS):
        last = l == LAYERS - 1
        hidden_in[l], hidden_mid[l], normed, qkv[l], ctx[l] = attention_forward(
            attn_off, base, pieces, [], norm_gains[l], attn_w[l]
        )
        images = exchange_rows(place, normed)
        block = expert_w[l][0].shape
        at = [(0, None)], [(1, None)]
        here = [(j, 0) for j in range(8)]
        if last:
            grads = exchange_rows(place, padded_bf16(cotangent)[None])
            plan = Plan(l, block, here, [(j + 8, 0) for j in range(8)], *at, [block] * 2, *at)
            result = expert_layer(
                plan, expert_off, me, tables, router_weight[l], images + grads, None, expert_w[l]
            )
            tail = send_rows(place, pair_rows(place, result[:2]))
            result = result[2:]
            outputs = hidden_mid[l] + sum(p.astype(f32) for p in tail)
        else:
            plan = Plan(l, block, here, None, *at, None, None, None)
            *result, sent, expert_y = expert_layer(
                plan, expert_off, me, tables, router_weight[l], images, None, expert_w[l]
            )
            base, pieces = hidden_mid[l], send_rows(place, pair_rows(place, result))
            saved = [sent, expert_y]
    base = cotangent
    for l in reversed(range(LAYERS)):
        back = send_rows(place, pair_rows(place, result[:2]))
        router_list[l], *pieces = result[2:]
        in_list[l], out_list[l] = scatter_experts(place, pieces[0][0], pieces[1][0])
        base, branch, gain_list[l], *parts = attention_backward(
            attn_off, base, back, hidden_in[l], hidden_mid[l], norm_gains[l], attn_w[l], qkv[l], ctx[l],
            ROWS if l else LEN,
        )
        if l:
            grads = exchange_rows(place, branch[None])
            plan = Plan(l - 1, block, None, here, *at, [block] * 2, *at)
            result = expert_layer(
                plan, expert_off, me, tables, router_weight[l - 1], grads, saved, expert_w[l - 1]
            )
        total = scatter_attention(place, jnp.concatenate(parts), rows)
        attn_list[l] = total.astype(f32).reshape(rows, 4, -1)
    gains = jnp.stack([gain_list[l] for l in range(LAYERS)])
    router = jnp.stack([router_list[l] for l in range(LAYERS)])
    small = jnp.concatenate([gains.reshape(-1), router.reshape(-1)]).reshape(-1, 512)
    for bit in range(place.count.bit_length() - 1):
        small = small + place.swap(small, 1 << bit)
    small = small.reshape(-1)
    gains, router = small[: gains.size].reshape(gains.shape), small[gains.size :].reshape(router.shape)
    return (
        outputs[:LEN].astype(bf16),
        base,
        gains,
        jnp.stack([attn_list[l][:, :3] for l in range(LAYERS)]),
        jnp.stack([jnp.swapaxes(attn_list[l][:, 3], 0, 1) for l in range(LAYERS)]),
        router,
        jnp.stack([in_list[l] for l in range(LAYERS)]),
        jnp.stack([out_list[l] for l in range(LAYERS)]),
    )


CORE, Y, X, NEAR, FAR = 1, 2, 4, 8, 16


def tie(*values):
    return lax.optimization_barrier(values)


def expert_blocks(place, w_in, w_out):
    order = place.expert ^ jnp.arange(w_in.shape[0])
    return jnp.stack([w_in[order], jnp.swapaxes(w_out, 1, 2)[order]])


def chip_pairs(place, blocks):
    return jnp.stack([blocks[:, 0::2], place.swap(blocks[:, 1::2], CORE)], axis=2)


def send_pairs(place, pair):
    two, chips, cores, rows, width = pair.shape
    got = [pair[:, 0]] + [place.swap(pair[:, k], 2 * k) for k in (1, 2, 3)]
    return jnp.stack(got, axis=1).reshape(two, 2, chips * cores // 2, rows, width)


def plane_blocks(place, blocks):
    return send_pairs(place, chip_pairs(place, blocks))


def mixed(place, value, even, odd):
    pairs = [(i, i ^ (odd if i & CORE else even)) for i in range(place.count)]
    return lax.ppermute(value, AXES, pairs)


def attention_shard(qkv_weight, out_weight):
    shard = jnp.concatenate([qkv_weight, jnp.swapaxes(out_weight, 0, 1)[:, None]], axis=1)
    return shard.reshape(shard.shape[0], -1)


def widen(place, held, mask):
    return jnp.concatenate([held, place.swap(held, mask)])


def halve(place, held, mask):
    half = held.shape[0] // 2
    return held[:half] + place.swap(held[half:], mask)


def plane_sums(place, mine):
    shape = mine.shape
    return plane_blocks(place, mine.reshape((2, -1) + shape[3:])).reshape((2, -1) + shape[3:])


def unpack_sums(place, got):
    got = got[:, place.expert ^ jnp.arange(got.shape[1])].astype(f32)
    return got[0], jnp.swapaxes(got[1], 1, 2)


def per_device_plane(
    inputs,
    norm_gains,
    qkv_weight,
    out_weight,
    router_weight,
    expert_in,
    expert_out,
    routes,
    priority,
    cotangent,
):
    place = Place()
    swap = place.swap
    experts = expert_in.shape[1]
    rows = qkv_weight.shape[1]
    attn_order = [x | n * 2 | f * 4 for x in (0, 1) for n in (0, 1) for f in (0, 1)]
    attn_off = ((place.dp ^ jnp.array(attn_order, jnp.int32)) * rows).astype(jnp.int32)
    core = place.tensor & CORE
    replica = jnp.stack([jnp.zeros_like(core), 4 - 2 * core, 2 + 2 * core, 6 + 0 * core])
    expert_off = ((place.dp ^ replica[:, None] ^ jnp.arange(2)[None, :]) * rows).reshape(-1).astype(jnp.int32)
    me = place.expert.astype(jnp.int32).reshape(1)
    block = (2, place.tensor_size, rows, expert_in.shape[3])

    pair = chip_pairs(place, expert_blocks(place, expert_in[0], expert_out[0]))
    held = jnp.stack([attention_shard(qkv_weight[l], out_weight[l]) for l in (0, 1)])[None]
    pair, held = tie(pair, held)
    own0 = send_pairs(place, pair)
    held = widen(place, widen(place, held, FAR), NEAR)
    held, own0 = tie(held, own0)
    a0 = mixed(place, own0, FAR, NEAR)
    held = widen(place, held, X)
    held0, held1 = held[:, 0], held[:, 1]
    over0 = swap(held0, Y)
    tables = slot_tables(place, routes, priority, experts)
    over0, a0, blocks1, *tables = tie(over0, a0, expert_blocks(place, expert_in[1], expert_out[1]), *tables)
    b0, c0 = mixed(place, own0, NEAR, FAR), mixed(place, a0, NEAR, FAR)
    weights0 = [held0, swap(held0, CORE), over0, swap(over0, CORE)]
    own1 = plane_blocks(place, blocks1)

    hidden_in0, hidden_mid0, normed, qkv0, ctx0 = attention_forward(
        attn_off, inputs, [], [], norm_gains[0], weights0
    )
    normed, own1, held1 = tie(normed, own1, held1)
    images = exchange_rows(place, normed)
    over1 = swap(held1, Y)
    weights1 = [held1, swap(held1, CORE), over1, swap(over1, CORE)]
    tied = tie(*images, *weights1)
    images, weights1 = tied[:8], tied[8:]
    b0, c0, own1 = tie(b0, c0, own1)
    a1, b1 = mixed(place, own1, FAR, NEAR), mixed(place, own1, NEAR, FAR)
    first = [(j, 0) for j in range(8)]
    second = [(j, 1) for j in range(8)]
    parts = [[(m, io) for m in range(4)] for io in (0, 1)]
    *rows0, sent, expert_y = expert_layer(
        Plan(0, block, first, None, *parts, None, None, None),
        expert_off, me, tables, router_weight[0], images, None, [own0, a0, b0, c0],
    )
    pieces = send_rows(place, pair_rows(place, rows0))
    hidden_in1, hidden_mid1, normed, qkv1, ctx1 = attention_forward(
        attn_off, hidden_mid0, pieces, [cotangent], norm_gains[1], weights1
    )
    normed, a1 = tie(normed, a1)
    c1 = mixed(place, a1, NEAR, FAR)
    images = exchange_rows(place, normed)
    images[2], b1 = tie(images[2], b1)
    grad_shapes = [(2,) + block] * 4
    result = expert_layer(
        Plan(1, block, first, second, *parts, grad_shapes, *parts),
        expert_off, me, tables, router_weight[1], images, None, [own1, a1, b1, c1],
    )
    out_rows, back_rows, router1, (own, a, b, c) = result[:2], result[2:4], result[4], result[5:]

    b, c = mixed(place, b, NEAR, FAR), mixed(place, c, NEAR, FAR)
    pieces = send_rows(place, pair_rows(place, back_rows))
    grad1, branch, gains1, *parts1 = attention_backward(
        attn_off, cotangent, pieces, hidden_in1, hidden_mid1, norm_gains[1], weights1, qkv1, ctx1, ROWS
    )
    far1 = parts1[2] + swap(parts1[3], CORE)
    images = exchange_rows(place, branch[None])
    tied = tie(*images, a, b, c, far1)
    images, (a, b, c, far1) = tied[:8], tied[8:]
    far1 = swap(far1, Y)
    a = mixed(place, a + c, FAR, NEAR)
    result = expert_layer(
        Plan(0, block, None, first, *parts, grad_shapes, *parts),
        expert_off, me, tables, router_weight[0], images, [sent, expert_y], [own0, a0, b0, c0],
        flops=10**10,
    )
    back_rows, router0, (own0, a0, b0, c0) = result[:2], result[2], result[3:]
    *back_rows, far1 = tie(*back_rows, far1)
    c0 = mixed(place, c0, NEAR, FAR)
    pieces = send_rows(place, pair_rows(place, back_rows))
    pieces[3], a = tie(pieces[3], a)
    grad0, unused, gains0, *parts0 = attention_backward(
        attn_off, grad1, pieces, hidden_in0, hidden_mid0, norm_gains[0], weights0, qkv0, ctx0, LEN
    )
    gains0, c0, b0, a, b, own, *out_rows = tie(gains0, c0, b0, a, b, own, *out_rows)
    a0, b0 = mixed(place, a0 + c0, FAR, NEAR), mixed(place, b0, NEAR, FAR)
    gains, router = jnp.stack([gains0, gains1]), jnp.stack([router0, router1])
    small = jnp.concatenate([gains.reshape(-1), router.reshape(-1)]).reshape(-1, 512)
    recv = [swap(v, CORE) for v in (parts0[3], parts0[1], parts1[1])]
    *recv, sum1, parts0[0], parts0[2], parts1[0] = tie(
        *recv, own + b + a, parts0[0], parts0[2], parts1[0]
    )
    far0, near0, near1 = parts0[2] + recv[0], parts0[0] + recv[1], parts1[0] + recv[2]
    far0 = swap(far0, Y)
    far0, out_rows[0] = tie(far0, out_rows[0])
    attn_sum = [halve(place, near + far, X) for near, far in ((near0, far0), (near1, far1))]
    attn_sum = jnp.stack(attn_sum, axis=1)
    sum1, small, *tail = tie(plane_sums(place, sum1), small, *pair_rows(place, out_rows))
    tail = send_rows(place, tail)
    for mask in (CORE, X, Y):
        small = small + swap(small, mask)
    attn_sum, small, sum1, a0, b0, *tail = tie(attn_sum, small, sum1, a0, b0, *tail)
    outputs = hidden_mid1 + sum(p.astype(f32) for p in tail)
    sum0 = own0 + a0 + b0
    pair0 = chip_pairs(place, sum0.reshape((2, -1) + sum0.shape[3:]))
    pair0, attn_sum, small = tie(pair0, attn_sum, small)
    sum0 = send_pairs(place, pair0).reshape((2, -1) + sum0.shape[3:])
    for mask in (NEAR, FAR):
        attn_sum = halve(place, attn_sum, mask)
        small = small + swap(small, mask)
    in1, out1 = unpack_sums(place, sum1)
    in0, out0 = unpack_sums(place, sum0)
    small = small.reshape(-1)
    gains, router = small[: gains.size].reshape(gains.shape), small[gains.size :].reshape(router.shape)
    attn = attn_sum.astype(f32).reshape(2, rows, 4, -1)
    return (
        outputs[:LEN].astype(bf16),
        grad0,
        gains,
        attn[:, :, :3],
        jnp.swapaxes(attn[:, :, 3], 1, 2),
        router,
        jnp.stack([in0, in1]),
        jnp.stack([out0, out1]),
    )


def solution(mesh):
    in_specs = (
        P(("dp", "tensor"), None),
        P(),
        P(None, "dp", None, "tensor"),
        P(None, "tensor", "dp"),
        P(),
        P(None, None, "dp", "tensor"),
        P(None, None, "tensor", "dp"),
        P(None, "dp", None),
        P(None, "dp", None),
        P(("dp", "tensor"), None),
    )
    out_specs = (
        P(("dp", "tensor"), None),
        P(("dp", "tensor"), None),
        P(),
        P(None, "dp", None, "tensor"),
        P(None, "tensor", "dp"),
        P(),
        P(None, None, "dp", "tensor"),
        P(None, None, "tensor", "dp"),
    )
    fast = mesh.shape["dp"] == 8 and mesh.shape["tensor"] == 4 and LAYERS == 2
    return jax.shard_map(
        per_device_plane if fast else per_device, mesh=mesh, in_specs=in_specs, out_specs=out_specs, check_vma=False
    )
```

```python
import jax
import jax.numpy as jnp
from jax import lax
from jax.experimental import pallas as pl
from jax.experimental.pallas import tpu as pltpu
from jax.sharding import PartitionSpec as P

HD = 64
LEN = 197
LAYERS = 2
CAP = 247
SLOTS = 256
ROWS = 200
NORM_EPS = 1e-06
f32 = jnp.float32
bf16 = jnp.bfloat16
AXES = ("dp", "tensor")


def mm(spec, *args):
    return jnp.einsum(spec, *args, preferred_element_type=f32)


class Place:
    def __init__(self):
        self.dp_size = lax.axis_size("dp")
        self.tensor_size = lax.axis_size("tensor")
        self.count = self.dp_size * self.tensor_size
        self.dp = lax.axis_index("dp")
        self.tensor = lax.axis_index("tensor")
        self.near = self.dp & 1
        self.expert = self.near * self.tensor_size + self.tensor

    def swap(self, value, mask):
        pairs = [(i, i ^ mask) for i in range(self.count)]
        return lax.ppermute(value, AXES, pairs)

    def dp_groups(self):
        return [[d for d in range(self.dp_size) if d & 1 == b] for b in (0, 1)]

    def ordered(self, mine, theirs, bit):
        return jnp.stack([jnp.where(bit, theirs, mine), jnp.where(bit, mine, theirs)])


def gather_attention(place, shard):
    rows, width = shard.shape
    bits = place.dp_size.bit_length() - 1
    held = shard
    for bit in reversed(range(bits)):
        other = place.swap(held, place.tensor_size << bit)
        held = place.ordered(held, other, (place.dp >> bit) & 1)
    held = held.reshape((2,) * bits + (rows, width))
    held = jnp.transpose(held, tuple(reversed(range(bits))) + (bits, bits + 1))
    held = held.reshape(1, place.dp_size * rows, width)
    for mask in (2, 1):
        held = jnp.stack([held, place.swap(held, mask)], axis=1 if mask == 1 else 0)
        held = held.reshape((-1,) + held.shape[2:])
    return held


def scatter_attention(place, blocks, rows):
    bits = place.dp_size.bit_length() - 1
    held = blocks.reshape((2, 2) + blocks.shape[1:])
    held = held[:, 0] + place.swap(held[:, 1], 1)
    held = held[0] + place.swap(held[1], 2)
    for bit in range(bits):
        parts = held.reshape((-1, 2, rows, held.shape[-1]))
        mine = lax.dynamic_index_in_dim(parts, (place.dp >> bit) & 1, 1, keepdims=False)
        theirs = lax.dynamic_index_in_dim(parts, 1 - ((place.dp >> bit) & 1), 1, keepdims=False)
        held = mine + place.swap(theirs, place.tensor_size << bit)
        held = held.reshape(-1, held.shape[-1])
    return held


def plane_exchange(place, blocks):
    even, odd = blocks[0::2], blocks[1::2]
    pair = jnp.stack([even, place.swap(odd, 1)], axis=1)
    got = [pair[0]] + [place.swap(pair[k], 2 * k) for k in (1, 2, 3)]
    return jnp.concatenate(got, axis=0)


def gather_experts(place, w_in, w_out):
    blocks = jnp.stack([w_in, jnp.swapaxes(w_out, 1, 2)], axis=1)
    experts, unused, rows, width = blocks.shape
    order = place.expert ^ jnp.arange(experts)
    got = plane_exchange(place, blocks[order])
    got = got.reshape((2, place.tensor_size, 2, rows, width))
    got = place.ordered(got[0], got[1], place.near)
    full = lax.all_gather(got, "dp", axis=0, tiled=False, axis_index_groups=place.dp_groups())
    full = jnp.transpose(full, (3, 2, 0, 1, 4, 5))
    full = full.reshape((2, place.tensor_size, -1, width))
    return full[0], full[1]


def scatter_experts(place, grad_in, grad_out):
    tensor, model, width = grad_in.shape
    rows = model // place.dp_size
    both = jnp.stack([grad_in, grad_out]).astype(bf16)
    both = both.reshape((2, tensor, -1, 2, rows, width))
    both = jnp.transpose(both, (2, 3, 1, 0, 4, 5))
    mine = lax.psum_scatter(
        both, "dp", scatter_dimension=0, tiled=False, axis_index_groups=place.dp_groups()
    )
    mine = place.ordered(mine[0], mine[1], place.near)
    got = plane_exchange(place, mine.reshape((-1, 2, rows, width)))
    order = place.expert ^ jnp.arange(got.shape[0])
    got = got[order].astype(f32)
    return got[:, 0], jnp.swapaxes(got[:, 1], 1, 2)


LANES = 256
SPLIT = 2


def slot_kernel(experts, mine_ref, ids, rank, mine, theirs):
    tensor = mine.shape[1]
    expert, other = mine_ref[0], mine_ref[1]
    here = mine_ref[2]
    for l in range(ids.shape[0]):
        choice = lax.broadcasted_iota(jnp.int32, (experts, tensor * LANES), 0)
        first, second = ids[l, 0:1, :] == choice, ids[l, 1:2, :] == choice
        order = rank[l : l + 1, :].astype(f32)
        column = jnp.broadcast_to(order, (8, tensor * LANES)).T[:, 0:1]
        earlier = (column < order).astype(f32).astype(bf16)
        both = jnp.concatenate([first.astype(f32), second.astype(f32)]).astype(bf16)
        counts = dot(both, earlier)
        total = jnp.sum(first.astype(f32), axis=1, keepdims=True)
        slot = jnp.where(first, counts[:experts], jnp.where(second, total + counts[experts:], -1.0))
        slot = jnp.where(slot < CAP, slot, -1.0)
        for which, target in ((expert, mine), (other, theirs)):
            row = jnp.sum(jnp.where(choice == which, slot, 0.0), axis=0, keepdims=True).astype(jnp.int32)
            for t in range(tensor):
                target[l, pl.ds(jnp.bitwise_xor(here, t), 1), :] = row[:, t * LANES : (t + 1) * LANES]


def slot_tables(place, routes, priority, experts):
    layers, count, unused = routes.shape
    spread = ((0, 0), (0, 0), (0, 0), (0, LANES - LEN))
    ids = jnp.swapaxes(routes, 1, 2).reshape(layers, 2, -1, LEN)
    ids = jnp.pad(ids, spread, constant_values=-1).reshape(layers, 2, -1)
    rank = jnp.pad(priority.reshape(layers, 1, -1, LEN), spread).reshape(layers, -1)
    where = jnp.stack([place.expert, place.expert ^ place.tensor_size, place.tensor]).astype(jnp.int32)
    shape = jax.ShapeDtypeStruct((layers, place.tensor_size, LANES), jnp.int32)
    mine, theirs = pl.pallas_call(
        lambda *refs: slot_kernel(experts, *refs),
        out_shape=(shape, shape),
        in_specs=[smem(), vmem(), vmem()],
        out_specs=(vmem(), vmem()),
        compiler_params=params(),
        cost_estimate=pl.CostEstimate(flops=1, transcendentals=0, bytes_accessed=1),
        name="slots",
    )(where, ids, rank)
    return mine, place.swap(theirs, place.tensor_size)


def exchange_rows(place, own):
    even = [own] + [place.swap(own, 2 * k) for k in (1, 2, 3)]
    odd = [place.swap(rows, 1) for rows in even]
    return [rows for pair in zip(even, odd) for rows in pair]


def add_kernel(even, odd, *sums):
    for k, target in enumerate(sums):
        target[...] = (even[k].astype(f32) + odd[k].astype(f32)).astype(bf16)


def pair_rows(place, parts, *others):
    even, odd = parts
    odd, *others = lax.optimization_barrier((place.swap(odd, 1), *others))
    return list(pl.pallas_call(
        add_kernel,
        out_shape=(jax.ShapeDtypeStruct(even.shape[1:], bf16),) * 4,
        in_specs=[vmem()] * 2,
        out_specs=(vmem(),) * 4,
        cost_estimate=pl.CostEstimate(flops=1, transcendentals=0, bytes_accessed=1),
        name="add_rows",
    )(even, odd)) + others


def send_rows(place, sums):
    return [sums[0]] + [place.swap(sums[k], 2 * k) for k in (1, 2, 3)]


def dot(a, b):
    return lax.dot_general(a, b, (((1,), (0,)), ((), ())), preferred_element_type=f32)


def dot_t(a, b):
    return lax.dot_general(a, b, (((1,), (1,)), ((), ())), preferred_element_type=f32)


def t_dot(a, b):
    return lax.dot_general(a, b, (((0,), (0,)), ((), ())), preferred_element_type=f32)


def normalized(rows):
    average = jnp.mean(rows, axis=-1, keepdims=True)
    centered = rows - average
    variance = jnp.mean(centered * centered, axis=-1, keepdims=True)
    scale = lax.rsqrt(variance + NORM_EPS)
    return centered * scale, scale


def norm_grad(rows, gain, grad):
    unit, scale = normalized(rows)
    scaled = grad * gain
    pull = scaled - jnp.mean(scaled, axis=-1, keepdims=True)
    pull = pull - unit * jnp.mean(scaled * unit, axis=-1, keepdims=True)
    return scale * pull, jnp.sum(grad * unit, axis=0, keepdims=True)


def head_masks():
    lane = lax.broadcasted_iota(jnp.int32, (1, 2 * HD), 1)
    return lane < HD, lane >= HD


def only(values, mask):
    return jnp.where(mask, values.astype(f32), 0.0).astype(bf16)


def head_probs(queries, keys, mask):
    scores = dot_t(only(queries, mask), keys) * (HD ** (-0.5))
    valid = lax.broadcasted_iota(jnp.int32, scores.shape, 1) < LEN
    scores = jnp.where(valid, scores, -1e30)
    top = jnp.max(scores, axis=-1, keepdims=True)
    weights = jnp.exp(scores - top)
    return weights / jnp.sum(weights, axis=-1, keepdims=True)


def weight_copies(off_ref, pieces, buffer, sems):
    result = []
    for j, piece in enumerate(pieces):
        count, rows, unused = piece.shape
        result.append([
            pltpu.make_async_copy(
                piece.at[i],
                buffer.at[j, pl.ds(pl.multiple_of(off_ref[i], rows), rows)],
                sems.at[j, i],
            )
            for i in range(count)
        ])
    return result


def padded_rows(ref, scratch):
    if ref.shape[0] == ROWS:
        return ref[...].astype(f32)
    scratch[...] = jnp.zeros_like(scratch)
    scratch[0 : ref.shape[0]] = ref[...].astype(f32)
    return scratch[...]


def attention_forward_kernel(piece_count, extra_count, off_ref, base, *refs):
    pieces, refs = refs[:piece_count], refs[piece_count:]
    extra, refs = refs[:extra_count], refs[extra_count:]
    gains, w0, w1, w2, w3, hidden, mid, normed, qkv, ctx, scratch, wbuf, sems = refs
    copies = weight_copies(off_ref, (w0, w1, w2, w3), wbuf, sems)
    for group in copies:
        for copy in group:
            copy.start()
    rows = padded_rows(base, scratch)
    for piece in pieces:
        rows = rows + piece[...].astype(f32)
    hidden[...] = rows
    unit, unused = normalized(rows)
    normed_a = (unit * gains[0:1]).astype(bf16)
    low, high = head_masks()
    for group in copies:
        for copy in group:
            copy.wait()
    for j in range(4):
        qkv[:, j * 6 * HD : (j + 1) * 6 * HD] = dot(normed_a, wbuf[j, :, : 6 * HD]).astype(bf16)
    probs = []
    for j in range(4):
        part = qkv[:, j * 6 * HD : (j + 1) * 6 * HD]
        probs.append([head_probs(part[:, : 2 * HD], part[:, 2 * HD : 4 * HD], m).astype(bf16) for m in (low, high)])
    total = rows
    for j in range(4):
        values = qkv[:, j * 6 * HD + 4 * HD : (j + 1) * 6 * HD]
        context = jnp.where(low, dot(probs[j][0], values), dot(probs[j][1], values)).astype(bf16)
        ctx[:, j * 2 * HD : (j + 1) * 2 * HD] = context
        total = total + dot_t(context, wbuf[j, :, 6 * HD :])
    mid[...] = total
    unit, unused = normalized(total)
    normed[0] = (unit * gains[1:2]).astype(bf16)
    for ref in extra:
        normed[1] = padded_rows(ref, scratch).astype(bf16)


def vmem():
    return pl.BlockSpec(memory_space=pltpu.VMEM)


def smem():
    return pl.BlockSpec(memory_space=pltpu.SMEM)


def hbm():
    return pl.BlockSpec(memory_space=pl.ANY)


def params():
    return pltpu.CompilerParams(vmem_limit_bytes=60 << 20)


def attention_forward(offsets, base, pieces, extra, gains, weights):
    width = base.shape[1]
    shape = jax.ShapeDtypeStruct
    return pl.pallas_call(
        lambda *refs: attention_forward_kernel(len(pieces), len(extra), *refs),
        out_shape=(
            shape((ROWS, width), f32),
            shape((ROWS, width), f32),
            shape((1 + len(extra), ROWS, width), bf16),
            shape((ROWS, 3 * width), bf16),
            shape((ROWS, width), bf16),
        ),
        in_specs=[smem(), vmem()] + [vmem()] * (len(pieces) + len(extra)) + [vmem()] + [hbm()] * 4,
        out_specs=[vmem()] * 5,
        scratch_shapes=[
            pltpu.VMEM((ROWS, width), f32),
            pltpu.VMEM((4, width, width), bf16),
            pltpu.SemaphoreType.DMA((4, weights[0].shape[0])),
        ],
        compiler_params=params(),
        cost_estimate=pl.CostEstimate(flops=1, transcendentals=0, bytes_accessed=1),
        name="attention_forward",
    )(offsets, base, *pieces, *extra, gains, *weights)


def attention_backward_kernel(
    off_ref, base, p0, p1, p2, p3, hidden_in, hidden_mid, gains, w0, w1, w2, w3, qkv, ctx,
    grad_out, branch, gain_out, g0, g1, g2, g3, scratch, wbuf, gbuf, sems, out_sems,
):
    copies = weight_copies(off_ref, (w0, w1, w2, w3), wbuf, sems)
    for group in copies:
        for copy in group:
            copy.start()
    grad = padded_rows(base, scratch)
    normed_grad = p0[...].astype(f32) + p1[...].astype(f32) + p2[...].astype(f32) + p3[...].astype(f32)
    part, gain_expert = norm_grad(hidden_mid[...], gains[1:2], normed_grad)
    grad = grad + part
    attn_grad = grad.astype(bf16)
    attn_grad_t = attn_grad.T
    rows_in = hidden_in[...]
    unit, unused = normalized(rows_in)
    normed_t = (unit * gains[0:1]).astype(bf16).T
    low, high = head_masks()
    scale = HD ** (-0.5)
    for group in copies:
        for copy in group:
            copy.wait()
    heads = [(j, mask) for j in range(4) for mask in (low, high)]
    parts = [qkv[:, j * 6 * HD : (j + 1) * 6 * HD] for j in range(4)]
    queries = [part[:, : 2 * HD] for part in parts]
    keys = [part[:, 2 * HD : 4 * HD] for part in parts]
    values = [part[:, 4 * HD :] for part in parts]
    context_grads = [dot(attn_grad, wbuf[j, :, 6 * HD :]).astype(bf16) for j in range(4)]
    probs = [head_probs(queries[j], keys[j], mask) for j, mask in heads]
    probs_grads = [dot_t(only(context_grads[j], mask), values[j]) for j, mask in heads]
    v_grads = [t_dot(probs[i].astype(bf16), context_grads[j]) for i, (j, mask) in enumerate(heads)]
    score_grads = [
        (p * (g - jnp.sum(p * g, axis=-1, keepdims=True))).astype(bf16) for p, g in zip(probs, probs_grads)
    ]
    q_grads = [dot(score_grads[i], keys[j]) * scale for i, (j, mask) in enumerate(heads)]
    k_grads = [t_dot(score_grads[i], queries[j]) * scale for i, (j, mask) in enumerate(heads)]
    normed_part = jnp.zeros_like(grad)
    sends = []
    for j, target in enumerate((g0, g1, g2, g3)):
        mixed = jnp.concatenate(
            [jnp.where(low, g[2 * j], g[2 * j + 1]).astype(bf16) for g in (q_grads, k_grads, v_grads)], axis=1
        )
        context = ctx[:, j * 2 * HD : (j + 1) * 2 * HD]
        gbuf[j, :, : 6 * HD] = dot(normed_t, mixed).astype(bf16)
        gbuf[j, :, 6 * HD :] = dot(attn_grad_t, context).astype(bf16)
        normed_part = normed_part + dot_t(mixed, wbuf[j, :, : 6 * HD])
        count, rows, unused = target.shape
        for i in range(count):
            send = pltpu.make_async_copy(
                gbuf.at[j, pl.ds(pl.multiple_of(off_ref[i], rows), rows)], target.at[i], out_sems.at[j, i]
            )
            send.start()
            sends.append(send)
    part, gain_attn = norm_grad(rows_in, gains[0:1], normed_part)
    grad = grad + part
    grad_out[...] = grad[: grad_out.shape[0]]
    branch[...] = grad.astype(bf16)
    gain_out[...] = jnp.concatenate([gain_attn, gain_expert], axis=0)
    for send in sends:
        send.wait()


def attention_backward(offsets, base, pieces, hidden_in, hidden_mid, gains, weights, qkv, ctx, out_rows):
    width = base.shape[1]
    shape = jax.ShapeDtypeStruct
    blocks = weights[0].shape
    return pl.pallas_call(
        attention_backward_kernel,
        out_shape=(
            shape((out_rows, width), f32),
            shape((ROWS, width), bf16),
            shape((2, width), f32),
        ) + (shape(blocks, bf16),) * 4,
        in_specs=[smem()] + [vmem()] * 8 + [hbm()] * 4 + [vmem()] * 2,
        out_specs=[vmem()] * 3 + [hbm()] * 4,
        scratch_shapes=[
            pltpu.VMEM((ROWS, width), f32),
            pltpu.VMEM((4, width, width), bf16),
            pltpu.VMEM((4, width, width), bf16),
            pltpu.SemaphoreType.DMA((4, blocks[0])),
            pltpu.SemaphoreType.DMA((4, blocks[0])),
        ],
        compiler_params=params(),
        cost_estimate=pl.CostEstimate(flops=1, transcendentals=0, bytes_accessed=1),
        name="attention_backward",
    )(offsets, base, *pieces, hidden_in, hidden_mid, gains, *weights, qkv, ctx)


def split(values):
    high = values.astype(bf16)
    return high, (values - high.astype(f32)).astype(bf16)


ROOT = 0.7978845608028654
CUBE = 0.044715


def expert_kernel(plan, off_ref, me_ref, mine, theirs, router, *refs):
    forward, backward = plan.images is not None, plan.grads is not None
    piece_count = len(plan.w_in)
    refs = list(refs)

    def take(count):
        taken, refs[:count] = refs[:count], []
        return taken

    tokens = take(plan.token_arrays)
    sent_in, y_in = take(2) if not forward else (None, None)
    sources = take(plan.weight_arrays)
    parts = take(2) if forward else None
    sent_out, y_out = take(2) if forward and not backward else (None, None)
    if backward:
        back_parts = take(2)
        (router_grad,) = take(1)
        targets = take(len(plan.grad_shapes))
    in_buf, out_buf, sent_buf, y_buf = take(4)
    if backward:
        slot_buf, branch_buf, slot_t, sent_t, back_buf, gbuf, out_sems = take(7)
    (sems,) = take(1)

    near, chunks, rows, width = plan.block

    def loads(c, which):
        result = []
        for m in range(piece_count):
            for n in range(near):
                at = pl.ds(pl.multiple_of(off_ref[m * near + n], rows), rows)
                index, part = (plan.w_in, plan.w_out)[which][m]
                piece = sources[index] if part is None else sources[index].at[part]
                buf = (in_buf, out_buf)[which]
                result.append(
                    pltpu.make_async_copy(piece.at[n, c], buf.at[c, at], sems.at[which, c, m * near + n])
                )
        return result

    for c in range(chunks):
        for which in (0, 1):
            for copy in loads(c, which):
                copy.start()

    def hot_rows(g, t, slot):
        row = (mine, theirs)[g][plan.layer, t : t + 1, :][:, :ROWS]
        return (row == slot).astype(f32).astype(bf16)

    def gather(images):
        for g in (0, 1):
            total = None
            for t in range(4):
                j = g * 4 + t
                slot = lax.broadcasted_iota(jnp.int32, (SLOTS, ROWS), 0)
                hot = hot_rows(g, t, slot)
                index, layer = images[j]
                part = dot(hot, tokens[index][layer])
                total = part if total is None else total + part
            yield g, total

    def scatter(slot_rows, parts):
        for g in (0, 1):
            for t in range(4):
                j = g * 4 + t
                slot = lax.broadcasted_iota(jnp.int32, (SLOTS, ROWS), 0)
                part = t_dot(hot_rows(g, t, slot), slot_rows[g * SLOTS : (g + 1) * SLOTS]).astype(bf16)
                parts[j % 2][j // 2] = part

    if forward:
        for g, rows_g in gather(plan.images):
            sent_buf[g * SLOTS : (g + 1) * SLOTS] = rows_g.astype(bf16)
    else:
        sent_buf[...] = sent_in[...]
    sent = sent_buf[...]
    logits = dot(sent, router[...])
    top = jnp.max(logits, axis=-1, keepdims=True)
    weights = jnp.exp(logits - top)
    probs = weights / jnp.sum(weights, axis=-1, keepdims=True)
    is_mine = lax.broadcasted_iota(jnp.int32, probs.shape, 1) == me_ref[0]
    gate = jnp.sum(jnp.where(is_mine, probs, 0.0), axis=-1, keepdims=True)

    if backward:
        for g, rows_g in gather(plan.grads):
            part = slice(g * SLOTS, (g + 1) * SLOTS)
            slot_buf[part] = (gate[part] * rows_g).astype(bf16)
            branch_buf[part] = rows_g.astype(bf16)
        slot_t[...] = slot_buf[...].T
        sent_t[...] = sent.T
        back_buf[...] = jnp.zeros_like(back_buf)
    if forward:
        y_buf[...] = jnp.zeros_like(y_buf)

    def stores(c, which):
        result = []
        for m in range(piece_count):
            for n in range(near):
                at = pl.ds(pl.multiple_of(off_ref[m * near + n], rows), rows)
                index, part = (plan.grad_in, plan.grad_out)[which][m]
                piece = targets[index] if part is None else targets[index].at[part]
                result.append(
                    pltpu.make_async_copy(
                        gbuf.at[which, c, at], piece.at[n, c], out_sems.at[which, c, m * near + n]
                    )
                )
        return result

    halves = [slice(h * width // SPLIT, (h + 1) * width // SPLIT) for h in range(SPLIT)]

    @pl.loop(0, chunks)
    def _(c):
        for which in (0, 1):
            for copy in loads(c, which):
                copy.wait()
        pres = [dot(sent_buf[...], in_buf[c, :, at]) for at in halves]
        act_grads = [dot(slot_buf[...], out_buf[c, :, at]) for at in halves] if backward else None
        for h, at in enumerate(halves):
            pre = pres[h]
            square = pre * pre
            bend = jnp.tanh(pre * (ROOT + ROOT * CUBE * square))
            rise = 0.5 + 0.5 * bend
            act = pre * rise
            low_act = act.astype(bf16)
            if forward:
                y_buf[...] += dot_t(low_act, out_buf[c, :, at])
            if backward:
                gbuf[1, c, :, at] = dot(slot_t[...], low_act).astype(bf16)
                slope = rise + act * ((1.0 - bend) * (ROOT + 3.0 * ROOT * CUBE * square))
                pre_grad = (act_grads[h] * slope).astype(bf16)
                gbuf[0, c, :, at] = dot(sent_t[...], pre_grad).astype(bf16)
                back_buf[...] += dot_t(pre_grad, in_buf[c, :, at])
        if backward:
            for which in (1, 0):
                for copy in stores(c, which):
                    copy.start()

    expert_y = y_buf[...] if forward else y_in[...]
    if backward:
        gate_grad = jnp.sum(branch_buf[...].astype(f32) * expert_y, axis=-1, keepdims=True)
        logit_grad = gate_grad * gate * (is_mine.astype(f32) - probs)
        first, second = split(logit_grad)
        router_grad[...] = dot(sent_t[...], first) + dot(sent_t[...], second)
        back_buf[...] += dot_t(first, router[...]) + dot_t(second, router[...])
        scatter(back_buf[...].astype(bf16), back_parts)
    if forward:
        scatter((gate * expert_y).astype(bf16), parts)
        if not backward:
            sent_out[...] = sent
            y_out[...] = expert_y
    if backward:

        @pl.loop(0, chunks)
        def _(c):
            for which in (0, 1):
                for copy in stores(c, which):
                    copy.wait()


class Plan:
    def __init__(self, layer, block, images, grads, w_in, w_out, grad_shapes, grad_in, grad_out):
        self.layer, self.block = layer, block
        self.images, self.grads = images, grads
        self.w_in, self.w_out = w_in, w_out
        self.grad_shapes, self.grad_in, self.grad_out = grad_shapes, grad_in, grad_out


def expert_layer(plan, offsets, me, tables, router, tokens, saved, weights, flops=1):
    forward, backward = plan.images is not None, plan.grads is not None
    plan.token_arrays, plan.weight_arrays = len(tokens), len(weights)
    width = router.shape[0]
    count = len(plan.w_in)
    near, chunks, rows, hidden = plan.block
    slots = 2 * SLOTS
    shape = jax.ShapeDtypeStruct
    token_part = shape((4, ROWS, width), bf16)
    operands = [offsets, me, *tables, router, *tokens]
    in_specs = [smem(), smem()] + [vmem()] * (3 + len(tokens))
    if not forward:
        operands += saved
        in_specs += [vmem()] * 2
    operands += weights
    in_specs += [hbm()] * len(weights)
    out_shape, out_specs = [], []
    if forward:
        out_shape += [token_part] * 2
    if forward and not backward:
        out_shape += [shape((slots, width), bf16), shape((slots, width), f32)]
    if backward:
        out_shape += [token_part] * 2 + [shape(router.shape, f32)]
    out_specs += [vmem()] * len(out_shape)
    if backward:
        out_shape += [shape(s, bf16) for s in plan.grad_shapes]
        out_specs += [hbm()] * len(plan.grad_shapes)
    scratch = [
        pltpu.VMEM((chunks, width, hidden), bf16),
        pltpu.VMEM((chunks, width, hidden), bf16),
        pltpu.VMEM((slots, width), bf16),
        pltpu.VMEM((slots, width), f32),
    ]
    if backward:
        scratch += [
            pltpu.VMEM((slots, width), bf16),
            pltpu.VMEM((slots, width), bf16),
            pltpu.VMEM((width, slots), bf16),
            pltpu.VMEM((width, slots), bf16),
            pltpu.VMEM((slots, width), f32),
            pltpu.VMEM((2, chunks, width, hidden), bf16),
            pltpu.SemaphoreType.DMA((2, chunks, count * near)),
        ]
    scratch += [pltpu.SemaphoreType.DMA((2, chunks, count * near))]
    return pl.pallas_call(
        lambda *refs: expert_kernel(plan, *refs),
        out_shape=tuple(out_shape),
        in_specs=in_specs,
        out_specs=tuple(out_specs),
        scratch_shapes=scratch,
        compiler_params=params(),
        cost_estimate=pl.CostEstimate(flops=flops, transcendentals=0, bytes_accessed=1),
        name="expert_layer",
    )(*operands)


def padded_bf16(rows):
    return jnp.pad(rows.astype(bf16), ((0, ROWS - LEN), (0, 0)))


def per_device(
    inputs,
    norm_gains,
    qkv_weight,
    out_weight,
    router_weight,
    expert_in,
    expert_out,
    routes,
    priority,
    cotangent,
):
    place = Place()
    experts = expert_in.shape[1]
    rows = qkv_weight.shape[1]
    zero = jnp.zeros((1,), jnp.int32)
    attn_off, expert_off = zero, zero
    me = place.expert.astype(jnp.int32).reshape(1)
    attn_w, expert_w = [], []
    tables = slot_tables(place, routes, priority, experts)
    for l in range(LAYERS):
        shard = jnp.concatenate([qkv_weight[l], jnp.swapaxes(out_weight[l], 0, 1)[:, None]], axis=1)
        full = gather_attention(place, shard.reshape(rows, -1))
        attn_w.append([full[j][None] for j in range(4)])
        expert_w.append([w[None] for w in gather_experts(place, expert_in[l], expert_out[l])])
    hidden_in, hidden_mid, qkv, ctx = {}, {}, {}, {}
    base, pieces = inputs, []
    saved = None
    gain_list, router_list, in_list, out_list, attn_list = {}, {}, {}, {}, {}
    for l in range(LAYERS):
        last = l == LAYERS - 1
        hidden_in[l], hidden_mid[l], normed, qkv[l], ctx[l] = attention_forward(
            attn_off, base, pieces, [], norm_gains[l], attn_w[l]
        )
        images = exchange_rows(place, normed)
        block = expert_w[l][0].shape
        at = [(0, None)], [(1, None)]
        here = [(j, 0) for j in range(8)]
        if last:
            grads = exchange_rows(place, padded_bf16(cotangent)[None])
            plan = Plan(l, block, here, [(j + 8, 0) for j in range(8)], *at, [block] * 2, *at)
            result = expert_layer(
                plan, expert_off, me, tables, router_weight[l], images + grads, None, expert_w[l]
            )
            tail = send_rows(place, pair_rows(place, result[:2]))
            result = result[2:]
            outputs = hidden_mid[l] + sum(p.astype(f32) for p in tail)
        else:
            plan = Plan(l, block, here, None, *at, None, None, None)
            *result, sent, expert_y = expert_layer(
                plan, expert_off, me, tables, router_weight[l], images, None, expert_w[l]
            )
            base, pieces = hidden_mid[l], send_rows(place, pair_rows(place, result))
            saved = [sent, expert_y]
    base = cotangent
    for l in reversed(range(LAYERS)):
        back = send_rows(place, pair_rows(place, result[:2]))
        router_list[l], *pieces = result[2:]
        in_list[l], out_list[l] = scatter_experts(place, pieces[0][0], pieces[1][0])
        base, branch, gain_list[l], *parts = attention_backward(
            attn_off, base, back, hidden_in[l], hidden_mid[l], norm_gains[l], attn_w[l], qkv[l], ctx[l],
            ROWS if l else LEN,
        )
        if l:
            grads = exchange_rows(place, branch[None])
            plan = Plan(l - 1, block, None, here, *at, [block] * 2, *at)
            result = expert_layer(
                plan, expert_off, me, tables, router_weight[l - 1], grads, saved, expert_w[l - 1]
            )
        total = scatter_attention(place, jnp.concatenate(parts), rows)
        attn_list[l] = total.astype(f32).reshape(rows, 4, -1)
    gains = jnp.stack([gain_list[l] for l in range(LAYERS)])
    router = jnp.stack([router_list[l] for l in range(LAYERS)])
    small = jnp.concatenate([gains.reshape(-1), router.reshape(-1)]).reshape(-1, 512)
    for bit in range(place.count.bit_length() - 1):
        small = small + place.swap(small, 1 << bit)
    small = small.reshape(-1)
    gains, router = small[: gains.size].reshape(gains.shape), small[gains.size :].reshape(router.shape)
    return (
        outputs[:LEN].astype(bf16),
        base,
        gains,
        jnp.stack([attn_list[l][:, :3] for l in range(LAYERS)]),
        jnp.stack([jnp.swapaxes(attn_list[l][:, 3], 0, 1) for l in range(LAYERS)]),
        router,
        jnp.stack([in_list[l] for l in range(LAYERS)]),
        jnp.stack([out_list[l] for l in range(LAYERS)]),
    )


CORE, Y, X, NEAR, FAR = 1, 2, 4, 8, 16


def tie(*values):
    return lax.optimization_barrier(values)


def expert_blocks(place, w_in, w_out):
    order = place.expert ^ jnp.arange(w_in.shape[0])
    return jnp.stack([w_in[order], jnp.swapaxes(w_out, 1, 2)[order]])


def chip_pairs(place, blocks):
    return jnp.stack([blocks[:, 0::2], place.swap(blocks[:, 1::2], CORE)], axis=2)


def send_pairs(place, pair):
    two, chips, cores, rows, width = pair.shape
    got = [pair[:, 0]] + [place.swap(pair[:, k], 2 * k) for k in (1, 2, 3)]
    return jnp.stack(got, axis=1).reshape(two, 2, chips * cores // 2, rows, width)


def plane_blocks(place, blocks):
    return send_pairs(place, chip_pairs(place, blocks))


def mixed(place, value, even, odd):
    pairs = [(i, i ^ (odd if i & CORE else even)) for i in range(place.count)]
    return lax.ppermute(value, AXES, pairs)


def attention_shard(qkv_weight, out_weight):
    shard = jnp.concatenate([qkv_weight, jnp.swapaxes(out_weight, 0, 1)[:, None]], axis=1)
    return shard.reshape(shard.shape[0], -1)


def widen(place, held, mask):
    return jnp.concatenate([held, place.swap(held, mask)])


def halve(place, held, mask):
    half = held.shape[0] // 2
    return held[:half] + place.swap(held[half:], mask)


def plane_sums(place, mine):
    shape = mine.shape
    return plane_blocks(place, mine.reshape((2, -1) + shape[3:])).reshape((2, -1) + shape[3:])


def unpack_sums(place, got):
    got = got[:, place.expert ^ jnp.arange(got.shape[1])].astype(f32)
    return got[0], jnp.swapaxes(got[1], 1, 2)


def per_device_plane(
    inputs,
    norm_gains,
    qkv_weight,
    out_weight,
    router_weight,
    expert_in,
    expert_out,
    routes,
    priority,
    cotangent,
):
    place = Place()
    swap = place.swap
    experts = expert_in.shape[1]
    rows = qkv_weight.shape[1]
    attn_order = [x | n * 2 | f * 4 for x in (0, 1) for n in (0, 1) for f in (0, 1)]
    attn_off = ((place.dp ^ jnp.array(attn_order, jnp.int32)) * rows).astype(jnp.int32)
    core = place.tensor & CORE
    replica = jnp.stack([jnp.zeros_like(core), 4 - 2 * core, 2 + 2 * core, 6 + 0 * core])
    expert_off = ((place.dp ^ replica[:, None] ^ jnp.arange(2)[None, :]) * rows).reshape(-1).astype(jnp.int32)
    me = place.expert.astype(jnp.int32).reshape(1)
    block = (2, place.tensor_size, rows, expert_in.shape[3])

    pair = chip_pairs(place, expert_blocks(place, expert_in[0], expert_out[0]))
    held = jnp.stack([attention_shard(qkv_weight[l], out_weight[l]) for l in (0, 1)])[None]
    pair, held = tie(pair, held)
    own0 = send_pairs(place, pair)
    held = widen(place, widen(place, held, FAR), NEAR)
    held, own0 = tie(held, own0)
    a0 = mixed(place, own0, FAR, NEAR)
    held = widen(place, held, X)
    held0, held1 = held[:, 0], held[:, 1]
    over0 = swap(held0, Y)
    tables = slot_tables(place, routes, priority, experts)
    over0, a0, blocks1, *tables = tie(over0, a0, expert_blocks(place, expert_in[1], expert_out[1]), *tables)
    b0, c0 = mixed(place, own0, NEAR, FAR), mixed(place, a0, NEAR, FAR)
    weights0 = [held0, swap(held0, CORE), over0, swap(over0, CORE)]
    own1 = plane_blocks(place, blocks1)

    hidden_in0, hidden_mid0, normed, qkv0, ctx0 = attention_forward(
        attn_off, inputs, [], [], norm_gains[0], weights0
    )
    normed, own1, held1 = tie(normed, own1, held1)
    images = exchange_rows(place, normed)
    over1 = swap(held1, Y)
    weights1 = [held1, swap(held1, CORE), over1, swap(over1, CORE)]
    tied = tie(*images, *weights1)
    images, weights1 = tied[:8], tied[8:]
    b0, c0, own1 = tie(b0, c0, own1)
    a1, b1 = mixed(place, own1, FAR, NEAR), mixed(place, own1, NEAR, FAR)
    first = [(j, 0) for j in range(8)]
    second = [(j, 1) for j in range(8)]
    parts = [[(m, io) for m in range(4)] for io in (0, 1)]
    *rows0, sent, expert_y = expert_layer(
        Plan(0, block, first, None, *parts, None, None, None),
        expert_off, me, tables, router_weight[0], images, None, [own0, a0, b0, c0],
    )
    pieces = send_rows(place, pair_rows(place, rows0))
    hidden_in1, hidden_mid1, normed, qkv1, ctx1 = attention_forward(
        attn_off, hidden_mid0, pieces, [cotangent], norm_gains[1], weights1
    )
    normed, a1 = tie(normed, a1)
    c1 = mixed(place, a1, NEAR, FAR)
    images = exchange_rows(place, normed)
    images[2], b1 = tie(images[2], b1)
    grad_shapes = [(2,) + block] * 4
    result = expert_layer(
        Plan(1, block, first, second, *parts, grad_shapes, *parts),
        expert_off, me, tables, router_weight[1], images, None, [own1, a1, b1, c1],
    )
    out_rows, back_rows, router1, (own, a, b, c) = result[:2], result[2:4], result[4], result[5:]

    b, c = mixed(place, b, NEAR, FAR), mixed(place, c, NEAR, FAR)
    pieces = send_rows(place, pair_rows(place, back_rows))
    grad1, branch, gains1, *parts1 = attention_backward(
        attn_off, cotangent, pieces, hidden_in1, hidden_mid1, norm_gains[1], weights1, qkv1, ctx1, ROWS
    )
    far1 = parts1[2] + swap(parts1[3], CORE)
    images = exchange_rows(place, branch[None])
    tied = tie(*images, a, b, c, far1)
    images, (a, b, c, far1) = tied[:8], tied[8:]
    far1 = swap(far1, Y)
    a = mixed(place, a + c, FAR, NEAR)
    result = expert_layer(
        Plan(0, block, None, first, *parts, grad_shapes, *parts),
        expert_off, me, tables, router_weight[0], images, [sent, expert_y], [own0, a0, b0, c0],
        flops=10**10,
    )
    back_rows, router0, (own0, a0, b0, c0) = result[:2], result[2], result[3:]
    *back_rows, far1 = tie(*back_rows, far1)
    c0 = mixed(place, c0, NEAR, FAR)
    pieces = send_rows(place, pair_rows(place, back_rows))
    pieces[3], a = tie(pieces[3], a)
    grad0, unused, gains0, *parts0 = attention_backward(
        attn_off, grad1, pieces, hidden_in0, hidden_mid0, norm_gains[0], weights0, qkv0, ctx0, LEN
    )
    gains0, c0, b0, a, b, own, *out_rows = tie(gains0, c0, b0, a, b, own, *out_rows)
    a0, b0 = mixed(place, a0 + c0, FAR, NEAR), mixed(place, b0, NEAR, FAR)
    gains, router = jnp.stack([gains0, gains1]), jnp.stack([router0, router1])
    small = jnp.concatenate([gains.reshape(-1), router.reshape(-1)]).reshape(-1, 512)
    recv = [swap(v, CORE) for v in (parts0[3], parts0[1], parts1[1])]
    *recv, sum1, parts0[0], parts0[2], parts1[0] = tie(
        *recv, own + b + a, parts0[0], parts0[2], parts1[0]
    )
    far0, near0, near1 = parts0[2] + recv[0], parts0[0] + recv[1], parts1[0] + recv[2]
    far0 = swap(far0, Y)
    far0, out_rows[0] = tie(far0, out_rows[0])
    attn_sum = [halve(place, near + far, X) for near, far in ((near0, far0), (near1, far1))]
    attn_sum = jnp.stack(attn_sum, axis=1)
    sum1, small, *tail = tie(plane_sums(place, sum1), small, *pair_rows(place, out_rows))
    tail = send_rows(place, tail)
    for mask in (CORE, X, Y):
        small = small + swap(small, mask)
    attn_sum, small, sum1, a0, b0, *tail = tie(attn_sum, small, sum1, a0, b0, *tail)
    outputs = hidden_mid1 + sum(p.astype(f32) for p in tail)
    sum0 = own0 + a0 + b0
    pair0 = chip_pairs(place, sum0.reshape((2, -1) + sum0.shape[3:]))
    pair0, attn_sum, small = tie(pair0, attn_sum, small)
    sum0 = send_pairs(place, pair0).reshape((2, -1) + sum0.shape[3:])
    for mask in (NEAR, FAR):
        attn_sum = halve(place, attn_sum, mask)
        small = small + swap(small, mask)
    in1, out1 = unpack_sums(place, sum1)
    in0, out0 = unpack_sums(place, sum0)
    small = small.reshape(-1)
    gains, router = small[: gains.size].reshape(gains.shape), small[gains.size :].reshape(router.shape)
    attn = attn_sum.astype(f32).reshape(2, rows, 4, -1)
    return (
        outputs[:LEN].astype(bf16),
        grad0,
        gains,
        attn[:, :, :3],
        jnp.swapaxes(attn[:, :, 3], 1, 2),
        router,
        jnp.stack([in0, in1]),
        jnp.stack([out0, out1]),
    )


def solution(mesh):
    in_specs = (
        P(("dp", "tensor"), None),
        P(),
        P(None, "dp", None, "tensor"),
        P(None, "tensor", "dp"),
        P(),
        P(None, None, "dp", "tensor"),
        P(None, None, "tensor", "dp"),
        P(None, "dp", None),
        P(None, "dp", None),
        P(("dp", "tensor"), None),
    )
    out_specs = (
        P(("dp", "tensor"), None),
        P(("dp", "tensor"), None),
        P(),
        P(None, "dp", None, "tensor"),
        P(None, "tensor", "dp"),
        P(),
        P(None, None, "dp", "tensor"),
        P(None, None, "tensor", "dp"),
    )
    fast = mesh.shape["dp"] == 8 and mesh.shape["tensor"] == 4 and LAYERS == 2
    return jax.shard_map(
        per_device_plane if fast else per_device, mesh=mesh, in_specs=in_specs, out_specs=out_specs, check_vma=False
    )
```

```python
import jax
import jax.numpy as jnp
from jax import lax
from jax.experimental import pallas as pl
from jax.experimental.pallas import tpu as pltpu
from jax.sharding import PartitionSpec as P

HD = 64
LEN = 197
LAYERS = 2
CAP = 247
SLOTS = 256
ROWS = 200
NORM_EPS = 1e-06
f32 = jnp.float32
bf16 = jnp.bfloat16
AXES = ("dp", "tensor")


def mm(spec, *args):
    return jnp.einsum(spec, *args, preferred_element_type=f32)


class Place:
    def __init__(self):
        self.dp_size = lax.axis_size("dp")
        self.tensor_size = lax.axis_size("tensor")
        self.count = self.dp_size * self.tensor_size
        self.dp = lax.axis_index("dp")
        self.tensor = lax.axis_index("tensor")
        self.near = self.dp & 1
        self.expert = self.near * self.tensor_size + self.tensor

    def swap(self, value, mask):
        pairs = [(i, i ^ mask) for i in range(self.count)]
        return lax.ppermute(value, AXES, pairs)

    def dp_groups(self):
        return [[d for d in range(self.dp_size) if d & 1 == b] for b in (0, 1)]

    def ordered(self, mine, theirs, bit):
        return jnp.stack([jnp.where(bit, theirs, mine), jnp.where(bit, mine, theirs)])


def gather_attention(place, shard):
    rows, width = shard.shape
    bits = place.dp_size.bit_length() - 1
    held = shard
    for bit in reversed(range(bits)):
        other = place.swap(held, place.tensor_size << bit)
        held = place.ordered(held, other, (place.dp >> bit) & 1)
    held = held.reshape((2,) * bits + (rows, width))
    held = jnp.transpose(held, tuple(reversed(range(bits))) + (bits, bits + 1))
    held = held.reshape(1, place.dp_size * rows, width)
    for mask in (2, 1):
        held = jnp.stack([held, place.swap(held, mask)], axis=1 if mask == 1 else 0)
        held = held.reshape((-1,) + held.shape[2:])
    return held


def scatter_attention(place, blocks, rows):
    bits = place.dp_size.bit_length() - 1
    held = blocks.reshape((2, 2) + blocks.shape[1:])
    held = held[:, 0] + place.swap(held[:, 1], 1)
    held = held[0] + place.swap(held[1], 2)
    for bit in range(bits):
        parts = held.reshape((-1, 2, rows, held.shape[-1]))
        mine = lax.dynamic_index_in_dim(parts, (place.dp >> bit) & 1, 1, keepdims=False)
        theirs = lax.dynamic_index_in_dim(parts, 1 - ((place.dp >> bit) & 1), 1, keepdims=False)
        held = mine + place.swap(theirs, place.tensor_size << bit)
        held = held.reshape(-1, held.shape[-1])
    return held


def plane_exchange(place, blocks):
    even, odd = blocks[0::2], blocks[1::2]
    pair = jnp.stack([even, place.swap(odd, 1)], axis=1)
    got = [pair[0]] + [place.swap(pair[k], 2 * k) for k in (1, 2, 3)]
    return jnp.concatenate(got, axis=0)


def gather_experts(place, w_in, w_out):
    blocks = jnp.stack([w_in, jnp.swapaxes(w_out, 1, 2)], axis=1)
    experts, unused, rows, width = blocks.shape
    order = place.expert ^ jnp.arange(experts)
    got = plane_exchange(place, blocks[order])
    got = got.reshape((2, place.tensor_size, 2, rows, width))
    got = place.ordered(got[0], got[1], place.near)
    full = lax.all_gather(got, "dp", axis=0, tiled=False, axis_index_groups=place.dp_groups())
    full = jnp.transpose(full, (3, 2, 0, 1, 4, 5))
    full = full.reshape((2, place.tensor_size, -1, width))
    return full[0], full[1]


def scatter_experts(place, grad_in, grad_out):
    tensor, model, width = grad_in.shape
    rows = model // place.dp_size
    both = jnp.stack([grad_in, grad_out]).astype(bf16)
    both = both.reshape((2, tensor, -1, 2, rows, width))
    both = jnp.transpose(both, (2, 3, 1, 0, 4, 5))
    mine = lax.psum_scatter(
        both, "dp", scatter_dimension=0, tiled=False, axis_index_groups=place.dp_groups()
    )
    mine = place.ordered(mine[0], mine[1], place.near)
    got = plane_exchange(place, mine.reshape((-1, 2, rows, width)))
    order = place.expert ^ jnp.arange(got.shape[0])
    got = got[order].astype(f32)
    return got[:, 0], jnp.swapaxes(got[:, 1], 1, 2)


LANES = 256
SPLIT = 2


def slot_kernel(experts, mine_ref, ids, rank, mine, theirs):
    tensor = mine.shape[1]
    expert, other = mine_ref[0], mine_ref[1]
    here = mine_ref[2]
    for l in range(ids.shape[0]):
        choice = lax.broadcasted_iota(jnp.int32, (experts, tensor * LANES), 0)
        first, second = ids[l, 0:1, :] == choice, ids[l, 1:2, :] == choice
        order = rank[l : l + 1, :].astype(f32)
        column = jnp.broadcast_to(order, (8, tensor * LANES)).T[:, 0:1]
        earlier = (column < order).astype(f32).astype(bf16)
        both = jnp.concatenate([first.astype(f32), second.astype(f32)]).astype(bf16)
        counts = dot(both, earlier)
        total = jnp.sum(first.astype(f32), axis=1, keepdims=True)
        slot = jnp.where(first, counts[:experts], jnp.where(second, total + counts[experts:], -1.0))
        slot = jnp.where(slot < CAP, slot, -1.0)
        for which, target in ((expert, mine), (other, theirs)):
            row = jnp.sum(jnp.where(choice == which, slot, 0.0), axis=0, keepdims=True).astype(jnp.int32)
            for t in range(tensor):
                target[l, pl.ds(jnp.bitwise_xor(here, t), 1), :] = row[:, t * LANES : (t + 1) * LANES]


def slot_tables(place, routes, priority, experts):
    layers, count, unused = routes.shape
    spread = ((0, 0), (0, 0), (0, 0), (0, LANES - LEN))
    ids = jnp.swapaxes(routes, 1, 2).reshape(layers, 2, -1, LEN)
    ids = jnp.pad(ids, spread, constant_values=-1).reshape(layers, 2, -1)
    rank = jnp.pad(priority.reshape(layers, 1, -1, LEN), spread).reshape(layers, -1)
    where = jnp.stack([place.expert, place.expert ^ place.tensor_size, place.tensor]).astype(jnp.int32)
    shape = jax.ShapeDtypeStruct((layers, place.tensor_size, LANES), jnp.int32)
    mine, theirs = pl.pallas_call(
        lambda *refs: slot_kernel(experts, *refs),
        out_shape=(shape, shape),
        in_specs=[smem(), vmem(), vmem()],
        out_specs=(vmem(), vmem()),
        compiler_params=params(),
        cost_estimate=pl.CostEstimate(flops=1, transcendentals=0, bytes_accessed=1),
        name="slots",
    )(where, ids, rank)
    return mine, place.swap(theirs, place.tensor_size)


def exchange_rows(place, own):
    even = [own] + [place.swap(own, 2 * k) for k in (1, 2, 3)]
    odd = [place.swap(rows, 1) for rows in even]
    return [rows for pair in zip(even, odd) for rows in pair]


def add_kernel(even, odd, *sums):
    for k, target in enumerate(sums):
        target[...] = (even[k].astype(f32) + odd[k].astype(f32)).astype(bf16)


def pair_rows(place, parts, *others):
    even, odd = parts
    odd, *others = lax.optimization_barrier((place.swap(odd, 1), *others))
    return list(pl.pallas_call(
        add_kernel,
        out_shape=(jax.ShapeDtypeStruct(even.shape[1:], bf16),) * 4,
        in_specs=[vmem()] * 2,
        out_specs=(vmem(),) * 4,
        cost_estimate=pl.CostEstimate(flops=1, transcendentals=0, bytes_accessed=1),
        name="add_rows",
    )(even, odd)) + others


def send_rows(place, sums):
    return [sums[0]] + [place.swap(sums[k], 2 * k) for k in (1, 2, 3)]


def dot(a, b):
    return lax.dot_general(a, b, (((1,), (0,)), ((), ())), preferred_element_type=f32)


def dot_t(a, b):
    return lax.dot_general(a, b, (((1,), (1,)), ((), ())), preferred_element_type=f32)


def t_dot(a, b):
    return lax.dot_general(a, b, (((0,), (0,)), ((), ())), preferred_element_type=f32)


def normalized(rows):
    average = jnp.mean(rows, axis=-1, keepdims=True)
    centered = rows - average
    variance = jnp.mean(centered * centered, axis=-1, keepdims=True)
    scale = lax.rsqrt(variance + NORM_EPS)
    return centered * scale, scale


def norm_grad(rows, gain, grad):
    unit, scale = normalized(rows)
    scaled = grad * gain
    pull = scaled - jnp.mean(scaled, axis=-1, keepdims=True)
    pull = pull - unit * jnp.mean(scaled * unit, axis=-1, keepdims=True)
    return scale * pull, jnp.sum(grad * unit, axis=0, keepdims=True)


def head_masks():
    lane = lax.broadcasted_iota(jnp.int32, (1, 2 * HD), 1)
    return lane < HD, lane >= HD


def only(values, mask):
    return jnp.where(mask, values.astype(f32), 0.0).astype(bf16)


def head_probs(queries, keys, mask):
    scores = dot_t(only(queries, mask), keys) * (HD ** (-0.5))
    valid = lax.broadcasted_iota(jnp.int32, scores.shape, 1) < LEN
    scores = jnp.where(valid, scores, -1e30)
    top = jnp.max(scores, axis=-1, keepdims=True)
    weights = jnp.exp(scores - top)
    return weights / jnp.sum(weights, axis=-1, keepdims=True)


def weight_copies(off_ref, pieces, buffer, sems):
    result = []
    for j, piece in enumerate(pieces):
        count, rows, unused = piece.shape
        result.append([
            pltpu.make_async_copy(
                piece.at[i],
                buffer.at[j, pl.ds(pl.multiple_of(off_ref[i], rows), rows)],
                sems.at[j, i],
            )
            for i in range(count)
        ])
    return result


def padded_rows(ref, scratch):
    if ref.shape[0] == ROWS:
        return ref[...].astype(f32)
    scratch[...] = jnp.zeros_like(scratch)
    scratch[0 : ref.shape[0]] = ref[...].astype(f32)
    return scratch[...]


def attention_forward_kernel(piece_count, extra_count, off_ref, base, *refs):
    pieces, refs = refs[:piece_count], refs[piece_count:]
    extra, refs = refs[:extra_count], refs[extra_count:]
    gains, w0, w1, w2, w3, hidden, mid, normed, qkv, ctx, scratch, wbuf, sems = refs
    copies = weight_copies(off_ref, (w0, w1, w2, w3), wbuf, sems)
    for group in copies:
        for copy in group:
            copy.start()
    rows = padded_rows(base, scratch)
    for piece in pieces:
        rows = rows + piece[...].astype(f32)
    hidden[...] = rows
    unit, unused = normalized(rows)
    normed_a = (unit * gains[0:1]).astype(bf16)
    low, high = head_masks()
    for group in copies:
        for copy in group:
            copy.wait()
    for j in range(4):
        qkv[:, j * 6 * HD : (j + 1) * 6 * HD] = dot(normed_a, wbuf[j, :, : 6 * HD]).astype(bf16)
    probs = []
    for j in range(4):
        part = qkv[:, j * 6 * HD : (j + 1) * 6 * HD]
        probs.append([head_probs(part[:, : 2 * HD], part[:, 2 * HD : 4 * HD], m).astype(bf16) for m in (low, high)])
    total = rows
    for j in range(4):
        values = qkv[:, j * 6 * HD + 4 * HD : (j + 1) * 6 * HD]
        context = jnp.where(low, dot(probs[j][0], values), dot(probs[j][1], values)).astype(bf16)
        ctx[:, j * 2 * HD : (j + 1) * 2 * HD] = context
        total = total + dot_t(context, wbuf[j, :, 6 * HD :])
    mid[...] = total
    unit, unused = normalized(total)
    normed[0] = (unit * gains[1:2]).astype(bf16)
    for ref in extra:
        normed[1] = padded_rows(ref, scratch).astype(bf16)


def vmem():
    return pl.BlockSpec(memory_space=pltpu.VMEM)


def smem():
    return pl.BlockSpec(memory_space=pltpu.SMEM)


def hbm():
    return pl.BlockSpec(memory_space=pl.ANY)


def params():
    return pltpu.CompilerParams(vmem_limit_bytes=60 << 20)


def attention_forward(offsets, base, pieces, extra, gains, weights):
    width = base.shape[1]
    shape = jax.ShapeDtypeStruct
    return pl.pallas_call(
        lambda *refs: attention_forward_kernel(len(pieces), len(extra), *refs),
        out_shape=(
            shape((ROWS, width), f32),
            shape((ROWS, width), f32),
            shape((1 + len(extra), ROWS, width), bf16),
            shape((ROWS, 3 * width), bf16),
            shape((ROWS, width), bf16),
        ),
        in_specs=[smem(), vmem()] + [vmem()] * (len(pieces) + len(extra)) + [vmem()] + [hbm()] * 4,
        out_specs=[vmem()] * 5,
        scratch_shapes=[
            pltpu.VMEM((ROWS, width), f32),
            pltpu.VMEM((4, width, width), bf16),
            pltpu.SemaphoreType.DMA((4, weights[0].shape[0])),
        ],
        compiler_params=params(),
        cost_estimate=pl.CostEstimate(flops=1, transcendentals=0, bytes_accessed=1),
        name="attention_forward",
    )(offsets, base, *pieces, *extra, gains, *weights)


def attention_backward_kernel(
    off_ref, base, p0, p1, p2, p3, hidden_in, hidden_mid, gains, w0, w1, w2, w3, qkv, ctx,
    grad_out, branch, gain_out, g0, g1, g2, g3, scratch, wbuf, gbuf, sems, out_sems,
):
    copies = weight_copies(off_ref, (w0, w1, w2, w3), wbuf, sems)
    for group in copies:
        for copy in group:
            copy.start()
    grad = padded_rows(base, scratch)
    normed_grad = p0[...].astype(f32) + p1[...].astype(f32) + p2[...].astype(f32) + p3[...].astype(f32)
    part, gain_expert = norm_grad(hidden_mid[...], gains[1:2], normed_grad)
    grad = grad + part
    attn_grad = grad.astype(bf16)
    attn_grad_t = attn_grad.T
    rows_in = hidden_in[...]
    unit, unused = normalized(rows_in)
    normed_t = (unit * gains[0:1]).astype(bf16).T
    low, high = head_masks()
    scale = HD ** (-0.5)
    for group in copies:
        for copy in group:
            copy.wait()
    heads = [(j, mask) for j in range(4) for mask in (low, high)]
    parts = [qkv[:, j * 6 * HD : (j + 1) * 6 * HD] for j in range(4)]
    queries = [part[:, : 2 * HD] for part in parts]
    keys = [part[:, 2 * HD : 4 * HD] for part in parts]
    values = [part[:, 4 * HD :] for part in parts]
    context_grads = [dot(attn_grad, wbuf[j, :, 6 * HD :]).astype(bf16) for j in range(4)]
    probs = [head_probs(queries[j], keys[j], mask) for j, mask in heads]
    probs_grads = [dot_t(only(context_grads[j], mask), values[j]) for j, mask in heads]
    v_grads = [t_dot(probs[i].astype(bf16), context_grads[j]) for i, (j, mask) in enumerate(heads)]
    score_grads = [
        (p * (g - jnp.sum(p * g, axis=-1, keepdims=True))).astype(bf16) for p, g in zip(probs, probs_grads)
    ]
    q_grads = [dot(score_grads[i], keys[j]) * scale for i, (j, mask) in enumerate(heads)]
    k_grads = [t_dot(score_grads[i], queries[j]) * scale for i, (j, mask) in enumerate(heads)]
    normed_part = jnp.zeros_like(grad)
    sends = []
    for j, target in enumerate((g0, g1, g2, g3)):
        mixed = jnp.concatenate(
            [jnp.where(low, g[2 * j], g[2 * j + 1]).astype(bf16) for g in (q_grads, k_grads, v_grads)], axis=1
        )
        context = ctx[:, j * 2 * HD : (j + 1) * 2 * HD]
        gbuf[j, :, : 6 * HD] = dot(normed_t, mixed).astype(bf16)
        gbuf[j, :, 6 * HD :] = dot(attn_grad_t, context).astype(bf16)
        normed_part = normed_part + dot_t(mixed, wbuf[j, :, : 6 * HD])
        count, rows, unused = target.shape
        for i in range(count):
            send = pltpu.make_async_copy(
                gbuf.at[j, pl.ds(pl.multiple_of(off_ref[i], rows), rows)], target.at[i], out_sems.at[j, i]
            )
            send.start()
            sends.append(send)
    part, gain_attn = norm_grad(rows_in, gains[0:1], normed_part)
    grad = grad + part
    grad_out[...] = grad[: grad_out.shape[0]]
    branch[...] = grad.astype(bf16)
    gain_out[...] = jnp.concatenate([gain_attn, gain_expert], axis=0)
    for send in sends:
        send.wait()


def attention_backward(offsets, base, pieces, hidden_in, hidden_mid, gains, weights, qkv, ctx, out_rows):
    width = base.shape[1]
    shape = jax.ShapeDtypeStruct
    blocks = weights[0].shape
    return pl.pallas_call(
        attention_backward_kernel,
        out_shape=(
            shape((out_rows, width), f32),
            shape((ROWS, width), bf16),
            shape((2, width), f32),
        ) + (shape(blocks, bf16),) * 4,
        in_specs=[smem()] + [vmem()] * 8 + [hbm()] * 4 + [vmem()] * 2,
        out_specs=[vmem()] * 3 + [hbm()] * 4,
        scratch_shapes=[
            pltpu.VMEM((ROWS, width), f32),
            pltpu.VMEM((4, width, width), bf16),
            pltpu.VMEM((4, width, width), bf16),
            pltpu.SemaphoreType.DMA((4, blocks[0])),
            pltpu.SemaphoreType.DMA((4, blocks[0])),
        ],
        compiler_params=params(),
        cost_estimate=pl.CostEstimate(flops=1, transcendentals=0, bytes_accessed=1),
        name="attention_backward",
    )(offsets, base, *pieces, hidden_in, hidden_mid, gains, *weights, qkv, ctx)


def split(values):
    high = values.astype(bf16)
    return high, (values - high.astype(f32)).astype(bf16)


ROOT = 0.7978845608028654
CUBE = 0.044715


def expert_kernel(plan, off_ref, me_ref, mine, theirs, router, *refs):
    forward, backward = plan.images is not None, plan.grads is not None
    piece_count = len(plan.w_in)
    refs = list(refs)

    def take(count):
        taken, refs[:count] = refs[:count], []
        return taken

    tokens = take(plan.token_arrays)
    sent_in, y_in = take(2) if not forward else (None, None)
    sources = take(plan.weight_arrays)
    parts = take(2) if forward else None
    sent_out, y_out = take(2) if forward and not backward else (None, None)
    if backward:
        back_parts = take(2)
        (router_grad,) = take(1)
        targets = take(len(plan.grad_shapes))
    in_buf, out_buf, sent_buf, y_buf = take(4)
    if backward:
        slot_buf, branch_buf, slot_t, sent_t, back_buf, gbuf, out_sems = take(7)
    (sems,) = take(1)

    near, chunks, rows, width = plan.block

    def loads(c, which):
        result = []
        for m in range(piece_count):
            for n in range(near):
                at = pl.ds(pl.multiple_of(off_ref[m * near + n], rows), rows)
                index, part = (plan.w_in, plan.w_out)[which][m]
                piece = sources[index] if part is None else sources[index].at[part]
                buf = (in_buf, out_buf)[which]
                result.append(
                    pltpu.make_async_copy(piece.at[n, c], buf.at[c, at], sems.at[which, c, m * near + n])
                )
        return result

    for c in range(chunks):
        for which in (0, 1):
            for copy in loads(c, which):
                copy.start()

    def hot_rows(g, t, slot):
        row = (mine, theirs)[g][plan.layer, t : t + 1, :][:, :ROWS]
        return (row == slot).astype(f32).astype(bf16)

    def gather(images):
        for g in (0, 1):
            total = None
            for t in range(4):
                j = g * 4 + t
                slot = lax.broadcasted_iota(jnp.int32, (SLOTS, ROWS), 0)
                hot = hot_rows(g, t, slot)
                index, layer = images[j]
                part = dot(hot, tokens[index][layer])
                total = part if total is None else total + part
            yield g, total

    def scatter(slot_rows, parts):
        for g in (0, 1):
            for t in range(4):
                j = g * 4 + t
                slot = lax.broadcasted_iota(jnp.int32, (SLOTS, ROWS), 0)
                part = t_dot(hot_rows(g, t, slot), slot_rows[g * SLOTS : (g + 1) * SLOTS]).astype(bf16)
                parts[j % 2][j // 2] = part

    if forward:
        for g, rows_g in gather(plan.images):
            sent_buf[g * SLOTS : (g + 1) * SLOTS] = rows_g.astype(bf16)
    else:
        sent_buf[...] = sent_in[...]
    sent = sent_buf[...]
    logits = dot(sent, router[...])
    top = jnp.max(logits, axis=-1, keepdims=True)
    weights = jnp.exp(logits - top)
    probs = weights / jnp.sum(weights, axis=-1, keepdims=True)
    is_mine = lax.broadcasted_iota(jnp.int32, probs.shape, 1) == me_ref[0]
    gate = jnp.sum(jnp.where(is_mine, probs, 0.0), axis=-1, keepdims=True)

    if backward:
        for g, rows_g in gather(plan.grads):
            part = slice(g * SLOTS, (g + 1) * SLOTS)
            slot_buf[part] = (gate[part] * rows_g).astype(bf16)
            branch_buf[part] = rows_g.astype(bf16)
        slot_t[...] = slot_buf[...].T
        sent_t[...] = sent.T
        back_buf[...] = jnp.zeros_like(back_buf)
    if forward:
        y_buf[...] = jnp.zeros_like(y_buf)

    def stores(c, which):
        result = []
        for m in range(piece_count):
            for n in range(near):
                at = pl.ds(pl.multiple_of(off_ref[m * near + n], rows), rows)
                index, part = (plan.grad_in, plan.grad_out)[which][m]
                piece = targets[index] if part is None else targets[index].at[part]
                result.append(
                    pltpu.make_async_copy(
                        gbuf.at[which, c, at], piece.at[n, c], out_sems.at[which, c, m * near + n]
                    )
                )
        return result

    halves = [slice(h * width // SPLIT, (h + 1) * width // SPLIT) for h in range(SPLIT)]

    @pl.loop(0, chunks)
    def _(c):
        for which in (0, 1):
            for copy in loads(c, which):
                copy.wait()
        pres = [dot(sent_buf[...], in_buf[c, :, at]) for at in halves]
        act_grads = [dot(slot_buf[...], out_buf[c, :, at]) for at in halves] if backward else None
        for h, at in enumerate(halves):
            pre = pres[h]
            square = pre * pre
            bend = jnp.tanh(pre * (ROOT + ROOT * CUBE * square))
            rise = 0.5 + 0.5 * bend
            act = pre * rise
            low_act = act.astype(bf16)
            if forward:
                y_buf[...] += dot_t(low_act, out_buf[c, :, at])
            if backward:
                gbuf[1, c, :, at] = dot(slot_t[...], low_act).astype(bf16)
                slope = rise + act * ((1.0 - bend) * (ROOT + 3.0 * ROOT * CUBE * square))
                pre_grad = (act_grads[h] * slope).astype(bf16)
                gbuf[0, c, :, at] = dot(sent_t[...], pre_grad).astype(bf16)
                back_buf[...] += dot_t(pre_grad, in_buf[c, :, at])
        if backward:
            for which in (1, 0):
                for copy in stores(c, which):
                    copy.start()

    expert_y = y_buf[...] if forward else y_in[...]
    if backward:
        gate_grad = jnp.sum(branch_buf[...].astype(f32) * expert_y, axis=-1, keepdims=True)
        logit_grad = gate_grad * gate * (is_mine.astype(f32) - probs)
        first, second = split(logit_grad)
        router_grad[...] = dot(sent_t[...], first) + dot(sent_t[...], second)
        back_buf[...] += dot_t(first, router[...]) + dot_t(second, router[...])
        scatter(back_buf[...].astype(bf16), back_parts)
    if forward:
        scatter((gate * expert_y).astype(bf16), parts)
        if not backward:
            sent_out[...] = sent
            y_out[...] = expert_y
    if backward:

        @pl.loop(0, chunks)
        def _(c):
            for which in (0, 1):
                for copy in stores(c, which):
                    copy.wait()


class Plan:
    def __init__(self, layer, block, images, grads, w_in, w_out, grad_shapes, grad_in, grad_out):
        self.layer, self.block = layer, block
        self.images, self.grads = images, grads
        self.w_in, self.w_out = w_in, w_out
        self.grad_shapes, self.grad_in, self.grad_out = grad_shapes, grad_in, grad_out


def expert_layer(plan, offsets, me, tables, router, tokens, saved, weights, flops=1):
    forward, backward = plan.images is not None, plan.grads is not None
    plan.token_arrays, plan.weight_arrays = len(tokens), len(weights)
    width = router.shape[0]
    count = len(plan.w_in)
    near, chunks, rows, hidden = plan.block
    slots = 2 * SLOTS
    shape = jax.ShapeDtypeStruct
    token_part = shape((4, ROWS, width), bf16)
    operands = [offsets, me, *tables, router, *tokens]
    in_specs = [smem(), smem()] + [vmem()] * (3 + len(tokens))
    if not forward:
        operands += saved
        in_specs += [vmem()] * 2
    operands += weights
    in_specs += [hbm()] * len(weights)
    out_shape, out_specs = [], []
    if forward:
        out_shape += [token_part] * 2
    if forward and not backward:
        out_shape += [shape((slots, width), bf16), shape((slots, width), f32)]
    if backward:
        out_shape += [token_part] * 2 + [shape(router.shape, f32)]
    out_specs += [vmem()] * len(out_shape)
    if backward:
        out_shape += [shape(s, bf16) for s in plan.grad_shapes]
        out_specs += [hbm()] * len(plan.grad_shapes)
    scratch = [
        pltpu.VMEM((chunks, width, hidden), bf16),
        pltpu.VMEM((chunks, width, hidden), bf16),
        pltpu.VMEM((slots, width), bf16),
        pltpu.VMEM((slots, width), f32),
    ]
    if backward:
        scratch += [
            pltpu.VMEM((slots, width), bf16),
            pltpu.VMEM((slots, width), bf16),
            pltpu.VMEM((width, slots), bf16),
            pltpu.VMEM((width, slots), bf16),
            pltpu.VMEM((slots, width), f32),
            pltpu.VMEM((2, chunks, width, hidden), bf16),
            pltpu.SemaphoreType.DMA((2, chunks, count * near)),
        ]
    scratch += [pltpu.SemaphoreType.DMA((2, chunks, count * near))]
    return pl.pallas_call(
        lambda *refs: expert_kernel(plan, *refs),
        out_shape=tuple(out_shape),
        in_specs=in_specs,
        out_specs=tuple(out_specs),
        scratch_shapes=scratch,
        compiler_params=params(),
        cost_estimate=pl.CostEstimate(flops=flops, transcendentals=0, bytes_accessed=1),
        name="expert_layer",
    )(*operands)


def padded_bf16(rows):
    return jnp.pad(rows.astype(bf16), ((0, ROWS - LEN), (0, 0)))


def per_device(
    inputs,
    norm_gains,
    qkv_weight,
    out_weight,
    router_weight,
    expert_in,
    expert_out,
    routes,
    priority,
    cotangent,
):
    place = Place()
    experts = expert_in.shape[1]
    rows = qkv_weight.shape[1]
    zero = jnp.zeros((1,), jnp.int32)
    attn_off, expert_off = zero, zero
    me = place.expert.astype(jnp.int32).reshape(1)
    attn_w, expert_w = [], []
    tables = slot_tables(place, routes, priority, experts)
    for l in range(LAYERS):
        shard = jnp.concatenate([qkv_weight[l], jnp.swapaxes(out_weight[l], 0, 1)[:, None]], axis=1)
        full = gather_attention(place, shard.reshape(rows, -1))
        attn_w.append([full[j][None] for j in range(4)])
        expert_w.append([w[None] for w in gather_experts(place, expert_in[l], expert_out[l])])
    hidden_in, hidden_mid, qkv, ctx = {}, {}, {}, {}
    base, pieces = inputs, []
    saved = None
    gain_list, router_list, in_list, out_list, attn_list = {}, {}, {}, {}, {}
    for l in range(LAYERS):
        last = l == LAYERS - 1
        hidden_in[l], hidden_mid[l], normed, qkv[l], ctx[l] = attention_forward(
            attn_off, base, pieces, [], norm_gains[l], attn_w[l]
        )
        images = exchange_rows(place, normed)
        block = expert_w[l][0].shape
        at = [(0, None)], [(1, None)]
        here = [(j, 0) for j in range(8)]
        if last:
            grads = exchange_rows(place, padded_bf16(cotangent)[None])
            plan = Plan(l, block, here, [(j + 8, 0) for j in range(8)], *at, [block] * 2, *at)
            result = expert_layer(
                plan, expert_off, me, tables, router_weight[l], images + grads, None, expert_w[l]
            )
            tail = send_rows(place, pair_rows(place, result[:2]))
            result = result[2:]
            outputs = hidden_mid[l] + sum(p.astype(f32) for p in tail)
        else:
            plan = Plan(l, block, here, None, *at, None, None, None)
            *result, sent, expert_y = expert_layer(
                plan, expert_off, me, tables, router_weight[l], images, None, expert_w[l]
            )
            base, pieces = hidden_mid[l], send_rows(place, pair_rows(place, result))
            saved = [sent, expert_y]
    base = cotangent
    for l in reversed(range(LAYERS)):
        back = send_rows(place, pair_rows(place, result[:2]))
        router_list[l], *pieces = result[2:]
        in_list[l], out_list[l] = scatter_experts(place, pieces[0][0], pieces[1][0])
        base, branch, gain_list[l], *parts = attention_backward(
            attn_off, base, back, hidden_in[l], hidden_mid[l], norm_gains[l], attn_w[l], qkv[l], ctx[l],
            ROWS if l else LEN,
        )
        if l:
            grads = exchange_rows(place, branch[None])
            plan = Plan(l - 1, block, None, here, *at, [block] * 2, *at)
            result = expert_layer(
                plan, expert_off, me, tables, router_weight[l - 1], grads, saved, expert_w[l - 1]
            )
        total = scatter_attention(place, jnp.concatenate(parts), rows)
        attn_list[l] = total.astype(f32).reshape(rows, 4, -1)
    gains = jnp.stack([gain_list[l] for l in range(LAYERS)])
    router = jnp.stack([router_list[l] for l in range(LAYERS)])
    small = jnp.concatenate([gains.reshape(-1), router.reshape(-1)]).reshape(-1, 512)
    for bit in range(place.count.bit_length() - 1):
        small = small + place.swap(small, 1 << bit)
    small = small.reshape(-1)
    gains, router = small[: gains.size].reshape(gains.shape), small[gains.size :].reshape(router.shape)
    return (
        outputs[:LEN].astype(bf16),
        base,
        gains,
        jnp.stack([attn_list[l][:, :3] for l in range(LAYERS)]),
        jnp.stack([jnp.swapaxes(attn_list[l][:, 3], 0, 1) for l in range(LAYERS)]),
        router,
        jnp.stack([in_list[l] for l in range(LAYERS)]),
        jnp.stack([out_list[l] for l in range(LAYERS)]),
    )


CORE, Y, X, NEAR, FAR = 1, 2, 4, 8, 16


def tie(*values):
    return lax.optimization_barrier(values)


def expert_blocks(place, w_in, w_out):
    order = place.expert ^ jnp.arange(w_in.shape[0])
    return jnp.stack([w_in[order], jnp.swapaxes(w_out, 1, 2)[order]])


def chip_pairs(place, blocks):
    return jnp.stack([blocks[:, 0::2], place.swap(blocks[:, 1::2], CORE)], axis=2)


def send_pairs(place, pair):
    two, chips, cores, rows, width = pair.shape
    got = [pair[:, 0]] + [place.swap(pair[:, k], 2 * k) for k in (1, 2, 3)]
    return jnp.stack(got, axis=1).reshape(two, 2, chips * cores // 2, rows, width)


def plane_blocks(place, blocks):
    return send_pairs(place, chip_pairs(place, blocks))


def mixed(place, value, even, odd):
    pairs = [(i, i ^ (odd if i & CORE else even)) for i in range(place.count)]
    return lax.ppermute(value, AXES, pairs)


def attention_shard(qkv_weight, out_weight):
    shard = jnp.concatenate([qkv_weight, jnp.swapaxes(out_weight, 0, 1)[:, None]], axis=1)
    return shard.reshape(shard.shape[0], -1)


def widen(place, held, mask):
    return jnp.concatenate([held, place.swap(held, mask)])


def halve(place, held, mask):
    half = held.shape[0] // 2
    return held[:half] + place.swap(held[half:], mask)


def send_sums(place, pair):
    return [pair[:, 0]] + [place.swap(pair[:, k], 2 * k) for k in (1, 2, 3)]


def unpack_kernel(layer, filled, me_ref, *refs):
    pieces, refs = refs[:4], refs[4 + 2 * filled :]
    in_ref, out_ref, in_buf, out_buf, sems = refs
    copies = []
    for k, piece in enumerate(pieces):
        for core in (0, 1):
            j = 2 * k + core
            expert = jnp.bitwise_xor(me_ref[0], j)
            in_buf[j] = piece[0, core].astype(f32)
            out_buf[j] = piece[1, core].astype(f32)
            copies.append(pltpu.make_async_copy(in_buf.at[j], in_ref.at[layer, expert], sems.at[0, j]))
            copies.append(pltpu.make_async_copy(out_buf.at[j], out_ref.at[layer, expert], sems.at[1, j]))
            for copy in copies[-2:]:
                copy.start()
    for copy in copies:
        copy.wait()


def unpack_sums(me, pieces, layer, layers, before=()):
    unused, cores, rows, width = pieces[0].shape
    experts = cores * len(pieces)
    shape = jax.ShapeDtypeStruct
    return pl.pallas_call(
        lambda *refs: unpack_kernel(layer, len(before) // 2, *refs),
        out_shape=(shape((layers, experts, rows, width), f32),) * 2,
        in_specs=[smem()] + [vmem()] * len(pieces) + [hbm()] * len(before),
        out_specs=(hbm(), hbm()),
        scratch_shapes=[
            pltpu.VMEM((experts, rows, width), f32),
            pltpu.VMEM((experts, rows, width), f32),
            pltpu.SemaphoreType.DMA((2, experts)),
        ],
        input_output_aliases={5: 0, 6: 1} if before else {},
        compiler_params=params(),
        cost_estimate=pl.CostEstimate(flops=1, transcendentals=0, bytes_accessed=1),
        name="unpack",
    )(me, *pieces, *before)


def per_device_plane(
    inputs,
    norm_gains,
    qkv_weight,
    out_weight,
    router_weight,
    expert_in,
    expert_out,
    routes,
    priority,
    cotangent,
):
    place = Place()
    swap = place.swap
    experts = expert_in.shape[1]
    rows = qkv_weight.shape[1]
    attn_order = [x | n * 2 | f * 4 for x in (0, 1) for n in (0, 1) for f in (0, 1)]
    attn_off = ((place.dp ^ jnp.array(attn_order, jnp.int32)) * rows).astype(jnp.int32)
    core = place.tensor & CORE
    replica = jnp.stack([jnp.zeros_like(core), 4 - 2 * core, 2 + 2 * core, 6 + 0 * core])
    expert_off = ((place.dp ^ replica[:, None] ^ jnp.arange(2)[None, :]) * rows).reshape(-1).astype(jnp.int32)
    me = place.expert.astype(jnp.int32).reshape(1)
    block = (2, place.tensor_size, rows, expert_in.shape[3])

    pair = chip_pairs(place, expert_blocks(place, expert_in[0], expert_out[0]))
    held = jnp.stack([attention_shard(qkv_weight[l], out_weight[l]) for l in (0, 1)])[None]
    pair, held = tie(pair, held)
    own0 = send_pairs(place, pair)
    held = widen(place, widen(place, held, FAR), NEAR)
    held, own0 = tie(held, own0)
    a0 = mixed(place, own0, FAR, NEAR)
    held = widen(place, held, X)
    held0, held1 = held[:, 0], held[:, 1]
    over0 = swap(held0, Y)
    tables = slot_tables(place, routes, priority, experts)
    over0, a0, blocks1, *tables = tie(over0, a0, expert_blocks(place, expert_in[1], expert_out[1]), *tables)
    b0, c0 = mixed(place, own0, NEAR, FAR), mixed(place, a0, NEAR, FAR)
    weights0 = [held0, swap(held0, CORE), over0, swap(over0, CORE)]
    own1 = plane_blocks(place, blocks1)

    hidden_in0, hidden_mid0, normed, qkv0, ctx0 = attention_forward(
        attn_off, inputs, [], [], norm_gains[0], weights0
    )
    normed, own1, held1 = tie(normed, own1, held1)
    images = exchange_rows(place, normed)
    over1 = swap(held1, Y)
    weights1 = [held1, swap(held1, CORE), over1, swap(over1, CORE)]
    tied = tie(*images, *weights1)
    images, weights1 = tied[:8], tied[8:]
    b0, c0, own1 = tie(b0, c0, own1)
    a1, b1 = mixed(place, own1, FAR, NEAR), mixed(place, own1, NEAR, FAR)
    first = [(j, 0) for j in range(8)]
    second = [(j, 1) for j in range(8)]
    parts = [[(m, io) for m in range(4)] for io in (0, 1)]
    *rows0, sent, expert_y = expert_layer(
        Plan(0, block, first, None, *parts, None, None, None),
        expert_off, me, tables, router_weight[0], images, None, [own0, a0, b0, c0],
    )
    pieces = send_rows(place, pair_rows(place, rows0))
    hidden_in1, hidden_mid1, normed, qkv1, ctx1 = attention_forward(
        attn_off, hidden_mid0, pieces, [cotangent], norm_gains[1], weights1
    )
    normed, a1 = tie(normed, a1)
    c1 = mixed(place, a1, NEAR, FAR)
    images = exchange_rows(place, normed)
    images[2], b1 = tie(images[2], b1)
    grad_shapes = [(2,) + block, (2,) + block, (2, 2) + block]
    grad_parts = [[(0, io), (1, io), (2, (0, io)), (2, (1, io))] for io in (0, 1)]
    result = expert_layer(
        Plan(1, block, first, second, *parts, grad_shapes, *grad_parts),
        expert_off, me, tables, router_weight[1], images, None, [own1, a1, b1, c1],
    )
    out_rows, back_rows, router1, (own, a, bc) = result[:2], result[2:4], result[4], result[5:]
    bc = mixed(place, bc, NEAR, FAR)
    pieces = send_rows(place, pair_rows(place, back_rows))
    grad1, branch, gains1, *parts1 = attention_backward(
        attn_off, cotangent, pieces, hidden_in1, hidden_mid1, norm_gains[1], weights1, qkv1, ctx1, ROWS
    )
    far1 = parts1[2] + swap(parts1[3], CORE)
    images = exchange_rows(place, branch[None])
    tied = tie(*images, a, bc, far1)
    images, (a, bc, far1) = tied[:8], tied[8:]
    far1 = swap(far1, Y)
    a = mixed(place, a + bc[1], FAR, NEAR)
    result = expert_layer(
        Plan(0, block, None, first, *parts, grad_shapes, *grad_parts),
        expert_off, me, tables, router_weight[0], images, [sent, expert_y], [own0, a0, b0, c0],
        flops=10**10,
    )
    back_rows, router0, (own0, a0, bc0) = result[:2], result[2], result[3:]
    *back_rows, far1 = tie(*back_rows, far1)
    bc0 = mixed(place, bc0, NEAR, FAR)
    pieces = send_rows(place, pair_rows(place, back_rows))
    pieces[3], a = tie(pieces[3], a)
    grad0, unused, gains0, *parts0 = attention_backward(
        attn_off, grad1, pieces, hidden_in0, hidden_mid0, norm_gains[0], weights0, qkv0, ctx0, LEN
    )
    gains0, a0, a, bc, own, *out_rows = tie(gains0, a0, a, bc, own, *out_rows)
    gains, router = jnp.stack([gains0, gains1]), jnp.stack([router0, router1])
    small = jnp.concatenate([gains.reshape(-1), router.reshape(-1)]).reshape(-1, 512)
    recv = [swap(v, CORE) for v in (parts0[3], parts0[1], parts1[1])]
    *recv, sum1, parts0[0], parts0[2], parts1[0] = tie(
        *recv, own + bc[0] + a, parts0[0], parts0[2], parts1[0]
    )
    far0, near0, near1 = parts0[2] + recv[0], parts0[0] + recv[1], parts1[0] + recv[2]
    far0 = swap(far0, Y)
    far0, out_rows[0], a0, bc0 = tie(far0, out_rows[0], a0, bc0)
    a0 = mixed(place, a0 + bc0[1], FAR, NEAR)
    attn_sum = [halve(place, near + far, X) for near, far in ((near0, far0), (near1, far1))]
    attn_sum = jnp.stack(attn_sum, axis=1)
    sum1 = send_sums(place, chip_pairs(place, sum1.reshape((2, -1) + sum1.shape[3:])))
    sum1[3], small, *tail = tie(sum1[3], small, *pair_rows(place, out_rows))
    tail = send_rows(place, tail)
    for mask in (CORE, X, Y):
        small = small + swap(small, mask)
    grads1 = unpack_sums(me, sum1, 1, LAYERS)
    tied = tie(attn_sum, small, a0, *grads1, *tail)
    (attn_sum, small, a0), grads1, tail = tied[:3], tied[3:5], tied[5:]
    outputs = hidden_mid1 + sum(p.astype(f32) for p in tail)
    sum0 = own0 + a0 + bc0[0]
    pair0 = chip_pairs(place, sum0.reshape((2, -1) + sum0.shape[3:]))
    pair0, attn_sum, small = tie(pair0, attn_sum, small)
    sum0 = send_sums(place, pair0)
    for mask in (NEAR, FAR):
        attn_sum = halve(place, attn_sum, mask)
        small = small + swap(small, mask)
    in_grads, out_grads = unpack_sums(me, sum0, 0, LAYERS, grads1)
    small = small.reshape(-1)
    gains, router = small[: gains.size].reshape(gains.shape), small[gains.size :].reshape(router.shape)
    attn = attn_sum.astype(f32).reshape(2, rows, 4, -1)
    return (
        outputs[:LEN].astype(bf16),
        grad0,
        gains,
        attn[:, :, :3],
        jnp.swapaxes(attn[:, :, 3], 1, 2),
        router,
        in_grads,
        jnp.swapaxes(out_grads, 2, 3),
    )


def solution(mesh):
    in_specs = (
        P(("dp", "tensor"), None),
        P(),
        P(None, "dp", None, "tensor"),
        P(None, "tensor", "dp"),
        P(),
        P(None, None, "dp", "tensor"),
        P(None, None, "tensor", "dp"),
        P(None, "dp", None),
        P(None, "dp", None),
        P(("dp", "tensor"), None),
    )
    out_specs = (
        P(("dp", "tensor"), None),
        P(("dp", "tensor"), None),
        P(),
        P(None, "dp", None, "tensor"),
        P(None, "tensor", "dp"),
        P(),
        P(None, None, "dp", "tensor"),
        P(None, None, "tensor", "dp"),
    )
    fast = mesh.shape["dp"] == 8 and mesh.shape["tensor"] == 4 and LAYERS == 2
    return jax.shard_map(
        per_device_plane if fast else per_device, mesh=mesh, in_specs=in_specs, out_specs=out_specs, check_vma=False
    )
```

```python
import jax
import jax.numpy as jnp
from jax import lax
from jax.experimental import pallas as pl
from jax.experimental.pallas import tpu as pltpu
from jax.sharding import PartitionSpec as P

HD = 64
LEN = 197
LAYERS = 2
CAP = 247
SLOTS = 256
ROWS = 200
NORM_EPS = 1e-06
f32 = jnp.float32
bf16 = jnp.bfloat16
AXES = ("dp", "tensor")


def mm(spec, *args):
    return jnp.einsum(spec, *args, preferred_element_type=f32)


class Place:
    def __init__(self):
        self.dp_size = lax.axis_size("dp")
        self.tensor_size = lax.axis_size("tensor")
        self.count = self.dp_size * self.tensor_size
        self.dp = lax.axis_index("dp")
        self.tensor = lax.axis_index("tensor")
        self.near = self.dp & 1
        self.expert = self.near * self.tensor_size + self.tensor

    def swap(self, value, mask):
        pairs = [(i, i ^ mask) for i in range(self.count)]
        return lax.ppermute(value, AXES, pairs)

    def dp_groups(self):
        return [[d for d in range(self.dp_size) if d & 1 == b] for b in (0, 1)]

    def ordered(self, mine, theirs, bit):
        return jnp.stack([jnp.where(bit, theirs, mine), jnp.where(bit, mine, theirs)])


def gather_attention(place, shard):
    rows, width = shard.shape
    bits = place.dp_size.bit_length() - 1
    held = shard
    for bit in reversed(range(bits)):
        other = place.swap(held, place.tensor_size << bit)
        held = place.ordered(held, other, (place.dp >> bit) & 1)
    held = held.reshape((2,) * bits + (rows, width))
    held = jnp.transpose(held, tuple(reversed(range(bits))) + (bits, bits + 1))
    held = held.reshape(1, place.dp_size * rows, width)
    for mask in (2, 1):
        held = jnp.stack([held, place.swap(held, mask)], axis=1 if mask == 1 else 0)
        held = held.reshape((-1,) + held.shape[2:])
    return held


def scatter_attention(place, blocks, rows):
    bits = place.dp_size.bit_length() - 1
    held = blocks.reshape((2, 2) + blocks.shape[1:])
    held = held[:, 0] + place.swap(held[:, 1], 1)
    held = held[0] + place.swap(held[1], 2)
    for bit in range(bits):
        parts = held.reshape((-1, 2, rows, held.shape[-1]))
        mine = lax.dynamic_index_in_dim(parts, (place.dp >> bit) & 1, 1, keepdims=False)
        theirs = lax.dynamic_index_in_dim(parts, 1 - ((place.dp >> bit) & 1), 1, keepdims=False)
        held = mine + place.swap(theirs, place.tensor_size << bit)
        held = held.reshape(-1, held.shape[-1])
    return held


def plane_exchange(place, blocks):
    even, odd = blocks[0::2], blocks[1::2]
    pair = jnp.stack([even, place.swap(odd, 1)], axis=1)
    got = [pair[0]] + [place.swap(pair[k], 2 * k) for k in (1, 2, 3)]
    return jnp.concatenate(got, axis=0)


def gather_experts(place, w_in, w_out):
    blocks = jnp.stack([w_in, jnp.swapaxes(w_out, 1, 2)], axis=1)
    experts, unused, rows, width = blocks.shape
    order = place.expert ^ jnp.arange(experts)
    got = plane_exchange(place, blocks[order])
    got = got.reshape((2, place.tensor_size, 2, rows, width))
    got = place.ordered(got[0], got[1], place.near)
    full = lax.all_gather(got, "dp", axis=0, tiled=False, axis_index_groups=place.dp_groups())
    full = jnp.transpose(full, (3, 2, 0, 1, 4, 5))
    full = full.reshape((2, place.tensor_size, -1, width))
    return full[0], full[1]


def scatter_experts(place, grad_in, grad_out):
    tensor, model, width = grad_in.shape
    rows = model // place.dp_size
    both = jnp.stack([grad_in, grad_out]).astype(bf16)
    both = both.reshape((2, tensor, -1, 2, rows, width))
    both = jnp.transpose(both, (2, 3, 1, 0, 4, 5))
    mine = lax.psum_scatter(
        both, "dp", scatter_dimension=0, tiled=False, axis_index_groups=place.dp_groups()
    )
    mine = place.ordered(mine[0], mine[1], place.near)
    got = plane_exchange(place, mine.reshape((-1, 2, rows, width)))
    order = place.expert ^ jnp.arange(got.shape[0])
    got = got[order].astype(f32)
    return got[:, 0], jnp.swapaxes(got[:, 1], 1, 2)


LANES = 256
SPLIT = 2


def slot_kernel(experts, mine_ref, ids, rank, mine, theirs):
    tensor = mine.shape[1]
    expert, other = mine_ref[0], mine_ref[1]
    here = mine_ref[2]
    for l in range(ids.shape[0]):
        choice = lax.broadcasted_iota(jnp.int32, (experts, tensor * LANES), 0)
        first, second = ids[l, 0:1, :] == choice, ids[l, 1:2, :] == choice
        order = rank[l : l + 1, :].astype(f32)
        column = jnp.broadcast_to(order, (8, tensor * LANES)).T[:, 0:1]
        earlier = (column < order).astype(f32).astype(bf16)
        both = jnp.concatenate([first.astype(f32), second.astype(f32)]).astype(bf16)
        counts = dot(both, earlier)
        total = jnp.sum(first.astype(f32), axis=1, keepdims=True)
        slot = jnp.where(first, counts[:experts], jnp.where(second, total + counts[experts:], -1.0))
        slot = jnp.where(slot < CAP, slot, -1.0)
        for which, target in ((expert, mine), (other, theirs)):
            row = jnp.sum(jnp.where(choice == which, slot, 0.0), axis=0, keepdims=True).astype(jnp.int32)
            for t in range(tensor):
                target[l, pl.ds(jnp.bitwise_xor(here, t), 1), :] = row[:, t * LANES : (t + 1) * LANES]


def slot_tables(place, routes, priority, experts):
    layers, count, unused = routes.shape
    spread = ((0, 0), (0, 0), (0, 0), (0, LANES - LEN))
    ids = jnp.swapaxes(routes, 1, 2).reshape(layers, 2, -1, LEN)
    ids = jnp.pad(ids, spread, constant_values=-1).reshape(layers, 2, -1)
    rank = jnp.pad(priority.reshape(layers, 1, -1, LEN), spread).reshape(layers, -1)
    where = jnp.stack([place.expert, place.expert ^ place.tensor_size, place.tensor]).astype(jnp.int32)
    shape = jax.ShapeDtypeStruct((layers, place.tensor_size, LANES), jnp.int32)
    mine, theirs = pl.pallas_call(
        lambda *refs: slot_kernel(experts, *refs),
        out_shape=(shape, shape),
        in_specs=[smem(), vmem(), vmem()],
        out_specs=(vmem(), vmem()),
        compiler_params=params(),
        cost_estimate=pl.CostEstimate(flops=1, transcendentals=0, bytes_accessed=1),
        name="slots",
    )(where, ids, rank)
    return mine, place.swap(theirs, place.tensor_size)


def exchange_rows(place, own):
    even = [own] + [place.swap(own, 2 * k) for k in (1, 2, 3)]
    odd = [place.swap(rows, 1) for rows in even]
    return [rows for pair in zip(even, odd) for rows in pair]


def add_kernel(even, odd, *sums):
    for k, target in enumerate(sums):
        target[...] = (even[k].astype(f32) + odd[k].astype(f32)).astype(bf16)


def pair_rows(place, parts, *others):
    even, odd = parts
    odd, *others = lax.optimization_barrier((place.swap(odd, 1), *others))
    return list(pl.pallas_call(
        add_kernel,
        out_shape=(jax.ShapeDtypeStruct(even.shape[1:], bf16),) * 4,
        in_specs=[vmem()] * 2,
        out_specs=(vmem(),) * 4,
        cost_estimate=pl.CostEstimate(flops=1, transcendentals=0, bytes_accessed=1),
        name="add_rows",
    )(even, odd)) + others


def send_rows(place, sums):
    return [sums[0]] + [place.swap(sums[k], 2 * k) for k in (1, 2, 3)]


def dot(a, b):
    return lax.dot_general(a, b, (((1,), (0,)), ((), ())), preferred_element_type=f32)


def dot_t(a, b):
    return lax.dot_general(a, b, (((1,), (1,)), ((), ())), preferred_element_type=f32)


def t_dot(a, b):
    return lax.dot_general(a, b, (((0,), (0,)), ((), ())), preferred_element_type=f32)


def normalized(rows):
    average = jnp.mean(rows, axis=-1, keepdims=True)
    centered = rows - average
    variance = jnp.mean(centered * centered, axis=-1, keepdims=True)
    scale = lax.rsqrt(variance + NORM_EPS)
    return centered * scale, scale


def norm_grad(rows, gain, grad):
    unit, scale = normalized(rows)
    scaled = grad * gain
    pull = scaled - jnp.mean(scaled, axis=-1, keepdims=True)
    pull = pull - unit * jnp.mean(scaled * unit, axis=-1, keepdims=True)
    return scale * pull, jnp.sum(grad * unit, axis=0, keepdims=True)


def head_masks():
    lane = lax.broadcasted_iota(jnp.int32, (1, 2 * HD), 1)
    return lane < HD, lane >= HD


def only(values, mask):
    return jnp.where(mask, values.astype(f32), 0.0).astype(bf16)


def head_probs(queries, keys, mask):
    scores = dot_t(only(queries, mask), keys) * (HD ** (-0.5))
    valid = lax.broadcasted_iota(jnp.int32, scores.shape, 1) < LEN
    scores = jnp.where(valid, scores, -1e30)
    top = jnp.max(scores, axis=-1, keepdims=True)
    weights = jnp.exp(scores - top)
    return weights / jnp.sum(weights, axis=-1, keepdims=True)


def weight_copies(off_ref, pieces, buffer, sems):
    result = []
    for j, piece in enumerate(pieces):
        count, rows, unused = piece.shape
        result.append([
            pltpu.make_async_copy(
                piece.at[i],
                buffer.at[j, pl.ds(pl.multiple_of(off_ref[i], rows), rows)],
                sems.at[j, i],
            )
            for i in range(count)
        ])
    return result


def padded_rows(ref, scratch):
    if ref.shape[0] == ROWS:
        return ref[...].astype(f32)
    scratch[...] = jnp.zeros_like(scratch)
    scratch[0 : ref.shape[0]] = ref[...].astype(f32)
    return scratch[...]


def attention_forward_kernel(piece_count, extra_count, off_ref, base, *refs):
    pieces, refs = refs[:piece_count], refs[piece_count:]
    extra, refs = refs[:extra_count], refs[extra_count:]
    gains, w0, w1, w2, w3, hidden, mid, normed, qkv, ctx, scratch, wbuf, sems = refs
    copies = weight_copies(off_ref, (w0, w1, w2, w3), wbuf, sems)
    for group in copies:
        for copy in group:
            copy.start()
    rows = padded_rows(base, scratch)
    for piece in pieces:
        rows = rows + piece[...].astype(f32)
    hidden[...] = rows
    unit, unused = normalized(rows)
    normed_a = (unit * gains[0:1]).astype(bf16)
    low, high = head_masks()
    for group in copies:
        for copy in group:
            copy.wait()
    for j in range(4):
        qkv[:, j * 6 * HD : (j + 1) * 6 * HD] = dot(normed_a, wbuf[j, :, : 6 * HD]).astype(bf16)
    probs = []
    for j in range(4):
        part = qkv[:, j * 6 * HD : (j + 1) * 6 * HD]
        probs.append([head_probs(part[:, : 2 * HD], part[:, 2 * HD : 4 * HD], m).astype(bf16) for m in (low, high)])
    total = rows
    for j in range(4):
        values = qkv[:, j * 6 * HD + 4 * HD : (j + 1) * 6 * HD]
        context = jnp.where(low, dot(probs[j][0], values), dot(probs[j][1], values)).astype(bf16)
        ctx[:, j * 2 * HD : (j + 1) * 2 * HD] = context
        total = total + dot_t(context, wbuf[j, :, 6 * HD :])
    mid[...] = total
    unit, unused = normalized(total)
    normed[0] = (unit * gains[1:2]).astype(bf16)
    for ref in extra:
        normed[1] = padded_rows(ref, scratch).astype(bf16)


def vmem():
    return pl.BlockSpec(memory_space=pltpu.VMEM)


def smem():
    return pl.BlockSpec(memory_space=pltpu.SMEM)


def hbm():
    return pl.BlockSpec(memory_space=pl.ANY)


def params():
    return pltpu.CompilerParams(vmem_limit_bytes=60 << 20)


def attention_forward(offsets, base, pieces, extra, gains, weights):
    width = base.shape[1]
    shape = jax.ShapeDtypeStruct
    return pl.pallas_call(
        lambda *refs: attention_forward_kernel(len(pieces), len(extra), *refs),
        out_shape=(
            shape((ROWS, width), f32),
            shape((ROWS, width), f32),
            shape((1 + len(extra), ROWS, width), bf16),
            shape((ROWS, 3 * width), bf16),
            shape((ROWS, width), bf16),
        ),
        in_specs=[smem(), vmem()] + [vmem()] * (len(pieces) + len(extra)) + [vmem()] + [hbm()] * 4,
        out_specs=[vmem()] * 5,
        scratch_shapes=[
            pltpu.VMEM((ROWS, width), f32),
            pltpu.VMEM((4, width, width), bf16),
            pltpu.SemaphoreType.DMA((4, weights[0].shape[0])),
        ],
        compiler_params=params(),
        cost_estimate=pl.CostEstimate(flops=1, transcendentals=0, bytes_accessed=1),
        name="attention_forward",
    )(offsets, base, *pieces, *extra, gains, *weights)


def attention_backward_kernel(
    off_ref, base, p0, p1, p2, p3, hidden_in, hidden_mid, gains, w0, w1, w2, w3, qkv, ctx,
    grad_out, branch, gain_out, g0, g1, g2, g3, scratch, wbuf, gbuf, sems, out_sems,
):
    copies = weight_copies(off_ref, (w0, w1, w2, w3), wbuf, sems)
    for group in copies:
        for copy in group:
            copy.start()
    grad = padded_rows(base, scratch)
    normed_grad = p0[...].astype(f32) + p1[...].astype(f32) + p2[...].astype(f32) + p3[...].astype(f32)
    part, gain_expert = norm_grad(hidden_mid[...], gains[1:2], normed_grad)
    grad = grad + part
    attn_grad = grad.astype(bf16)
    attn_grad_t = attn_grad.T
    rows_in = hidden_in[...]
    unit, unused = normalized(rows_in)
    normed_t = (unit * gains[0:1]).astype(bf16).T
    low, high = head_masks()
    scale = HD ** (-0.5)
    for group in copies:
        for copy in group:
            copy.wait()
    heads = [(j, mask) for j in range(4) for mask in (low, high)]
    parts = [qkv[:, j * 6 * HD : (j + 1) * 6 * HD] for j in range(4)]
    queries = [part[:, : 2 * HD] for part in parts]
    keys = [part[:, 2 * HD : 4 * HD] for part in parts]
    values = [part[:, 4 * HD :] for part in parts]
    context_grads = [dot(attn_grad, wbuf[j, :, 6 * HD :]).astype(bf16) for j in range(4)]
    probs = [head_probs(queries[j], keys[j], mask) for j, mask in heads]
    probs_grads = [dot_t(only(context_grads[j], mask), values[j]) for j, mask in heads]
    v_grads = [t_dot(probs[i].astype(bf16), context_grads[j]) for i, (j, mask) in enumerate(heads)]
    score_grads = [
        (p * (g - jnp.sum(p * g, axis=-1, keepdims=True))).astype(bf16) for p, g in zip(probs, probs_grads)
    ]
    q_grads = [dot(score_grads[i], keys[j]) * scale for i, (j, mask) in enumerate(heads)]
    k_grads = [t_dot(score_grads[i], queries[j]) * scale for i, (j, mask) in enumerate(heads)]
    normed_part = jnp.zeros_like(grad)
    sends = []
    for j, target in enumerate((g0, g1, g2, g3)):
        mixed = jnp.concatenate(
            [jnp.where(low, g[2 * j], g[2 * j + 1]).astype(bf16) for g in (q_grads, k_grads, v_grads)], axis=1
        )
        context = ctx[:, j * 2 * HD : (j + 1) * 2 * HD]
        gbuf[j, :, : 6 * HD] = dot(normed_t, mixed).astype(bf16)
        gbuf[j, :, 6 * HD :] = dot(attn_grad_t, context).astype(bf16)
        normed_part = normed_part + dot_t(mixed, wbuf[j, :, : 6 * HD])
        count, rows, unused = target.shape
        for i in range(count):
            send = pltpu.make_async_copy(
                gbuf.at[j, pl.ds(pl.multiple_of(off_ref[i], rows), rows)], target.at[i], out_sems.at[j, i]
            )
            send.start()
            sends.append(send)
    part, gain_attn = norm_grad(rows_in, gains[0:1], normed_part)
    grad = grad + part
    grad_out[...] = grad[: grad_out.shape[0]]
    branch[...] = grad.astype(bf16)
    gain_out[...] = jnp.concatenate([gain_attn, gain_expert], axis=0)
    for send in sends:
        send.wait()


def attention_backward(offsets, base, pieces, hidden_in, hidden_mid, gains, weights, qkv, ctx, out_rows):
    width = base.shape[1]
    shape = jax.ShapeDtypeStruct
    blocks = weights[0].shape
    return pl.pallas_call(
        attention_backward_kernel,
        out_shape=(
            shape((out_rows, width), f32),
            shape((ROWS, width), bf16),
            shape((2, width), f32),
        ) + (shape(blocks, bf16),) * 4,
        in_specs=[smem()] + [vmem()] * 8 + [hbm()] * 4 + [vmem()] * 2,
        out_specs=[vmem()] * 3 + [hbm()] * 4,
        scratch_shapes=[
            pltpu.VMEM((ROWS, width), f32),
            pltpu.VMEM((4, width, width), bf16),
            pltpu.VMEM((4, width, width), bf16),
            pltpu.SemaphoreType.DMA((4, blocks[0])),
            pltpu.SemaphoreType.DMA((4, blocks[0])),
        ],
        compiler_params=params(),
        cost_estimate=pl.CostEstimate(flops=1, transcendentals=0, bytes_accessed=1),
        name="attention_backward",
    )(offsets, base, *pieces, hidden_in, hidden_mid, gains, *weights, qkv, ctx)


def split(values):
    high = values.astype(bf16)
    return high, (values - high.astype(f32)).astype(bf16)


ROOT = 0.7978845608028654
CUBE = 0.044715


def expert_kernel(plan, off_ref, me_ref, mine, theirs, router, *refs):
    forward, backward = plan.images is not None, plan.grads is not None
    piece_count = len(plan.w_in)
    refs = list(refs)

    def take(count):
        taken, refs[:count] = refs[:count], []
        return taken

    tokens = take(plan.token_arrays)
    sent_in, y_in = take(2) if not forward else (None, None)
    sources = take(plan.weight_arrays)
    parts = take(2) if forward else None
    sent_out, y_out = take(2) if forward and not backward else (None, None)
    if backward:
        back_parts = take(2)
        (router_grad,) = take(1)
        targets = take(len(plan.grad_shapes))
    in_buf, out_buf, sent_buf, y_buf = take(4)
    if backward:
        slot_buf, branch_buf, slot_t, sent_t, back_buf, gbuf, out_sems = take(7)
    (sems,) = take(1)

    near, chunks, rows, width = plan.block

    def loads(c, which):
        result = []
        for m in range(piece_count):
            for n in range(near):
                at = pl.ds(pl.multiple_of(off_ref[m * near + n], rows), rows)
                index, part = (plan.w_in, plan.w_out)[which][m]
                piece = sources[index] if part is None else sources[index].at[part]
                buf = (in_buf, out_buf)[which]
                result.append(
                    pltpu.make_async_copy(piece.at[n, c], buf.at[c, at], sems.at[which, c, m * near + n])
                )
        return result

    @pl.loop(0, chunks)
    def _(c):
        for which in (0, 1):
            for copy in loads(c, which):
                copy.start()

    def hot_rows(g, t, slot):
        row = (mine, theirs)[g][plan.layer, t : t + 1, :][:, :ROWS]
        return (row == slot).astype(f32).astype(bf16)

    def gather(images):
        for g in (0, 1):
            total = None
            for t in range(4):
                j = g * 4 + t
                slot = lax.broadcasted_iota(jnp.int32, (SLOTS, ROWS), 0)
                hot = hot_rows(g, t, slot)
                index, layer = images[j]
                part = dot(hot, tokens[index][layer])
                total = part if total is None else total + part
            yield g, total

    def scatter(slot_rows, parts):
        for g in (0, 1):
            for t in range(4):
                j = g * 4 + t
                slot = lax.broadcasted_iota(jnp.int32, (SLOTS, ROWS), 0)
                part = t_dot(hot_rows(g, t, slot), slot_rows[g * SLOTS : (g + 1) * SLOTS]).astype(bf16)
                parts[j % 2][j // 2] = part

    if forward:
        for g, rows_g in gather(plan.images):
            sent_buf[g * SLOTS : (g + 1) * SLOTS] = rows_g.astype(bf16)
    else:
        sent_buf[...] = sent_in[...]
    sent = sent_buf[...]
    logits = dot_t(sent, router[plan.layer])
    top = jnp.max(logits, axis=-1, keepdims=True)
    weights = jnp.exp(logits - top)
    probs = weights / jnp.sum(weights, axis=-1, keepdims=True)
    is_mine = lax.broadcasted_iota(jnp.int32, probs.shape, 1) == me_ref[0]
    gate = jnp.sum(jnp.where(is_mine, probs, 0.0), axis=-1, keepdims=True)

    if backward:
        for g, rows_g in gather(plan.grads):
            part = slice(g * SLOTS, (g + 1) * SLOTS)
            slot_buf[part] = (gate[part] * rows_g).astype(bf16)
            branch_buf[part] = rows_g.astype(bf16)
        slot_t[...] = slot_buf[...].T
        sent_t[...] = sent.T
        back_buf[...] = jnp.zeros_like(back_buf)
    if forward:
        y_buf[...] = jnp.zeros_like(y_buf)

    def stores(c, which):
        result = []
        for m in range(piece_count):
            for n in range(near):
                at = pl.ds(pl.multiple_of(off_ref[m * near + n], rows), rows)
                index, part = (plan.grad_in, plan.grad_out)[which][m]
                piece = targets[index] if part is None else targets[index].at[part]
                result.append(
                    pltpu.make_async_copy(
                        gbuf.at[which, c, at], piece.at[n, c], out_sems.at[which, c, m * near + n]
                    )
                )
        return result

    halves = [slice(h * width // SPLIT, (h + 1) * width // SPLIT) for h in range(SPLIT)]

    @pl.loop(0, chunks)
    def _(c):
        for which in (0, 1):
            for copy in loads(c, which):
                copy.wait()
        pres = [dot(sent_buf[...], in_buf[c, :, at]) for at in halves]
        act_grads = [dot(slot_buf[...], out_buf[c, :, at]) for at in halves] if backward else None
        for h, at in enumerate(halves):
            pre = pres[h]
            square = pre * pre
            bend = jnp.tanh(pre * (ROOT + ROOT * CUBE * square))
            rise = 0.5 + 0.5 * bend
            act = pre * rise
            low_act = act.astype(bf16)
            if forward:
                y_buf[...] += dot_t(low_act, out_buf[c, :, at])
            if backward:
                gbuf[1, c, :, at] = dot(slot_t[...], low_act).astype(bf16)
                slope = rise + act * ((1.0 - bend) * (ROOT + 3.0 * ROOT * CUBE * square))
                pre_grad = (act_grads[h] * slope).astype(bf16)
                gbuf[0, c, :, at] = dot(sent_t[...], pre_grad).astype(bf16)
                back_buf[...] += dot_t(pre_grad, in_buf[c, :, at])
        if backward:
            for which in (1, 0):
                for copy in stores(c, which):
                    copy.start()

    expert_y = y_buf[...] if forward else y_in[...]
    if backward:
        gate_grad = jnp.sum(branch_buf[...].astype(f32) * expert_y, axis=-1, keepdims=True)
        logit_grad = gate_grad * gate * (is_mine.astype(f32) - probs)
        first, second = split(logit_grad)
        router_grad[...] = t_dot(first, sent) + t_dot(second, sent)
        back_buf[...] += dot(first, router[plan.layer]) + dot(second, router[plan.layer])
        scatter(back_buf[...].astype(bf16), back_parts)
    if forward:
        scatter((gate * expert_y).astype(bf16), parts)
        if not backward:
            sent_out[...] = sent
            y_out[...] = expert_y
    if backward:

        @pl.loop(0, chunks)
        def _(c):
            for which in (0, 1):
                for copy in stores(c, which):
                    copy.wait()


class Plan:
    def __init__(self, layer, block, images, grads, w_in, w_out, grad_shapes, grad_in, grad_out):
        self.layer, self.block = layer, block
        self.images, self.grads = images, grads
        self.w_in, self.w_out = w_in, w_out
        self.grad_shapes, self.grad_in, self.grad_out = grad_shapes, grad_in, grad_out


def expert_layer(plan, offsets, me, tables, router, tokens, saved, weights, flops=1):
    forward, backward = plan.images is not None, plan.grads is not None
    plan.token_arrays, plan.weight_arrays = len(tokens), len(weights)
    width = router.shape[2]
    count = len(plan.w_in)
    near, chunks, rows, hidden = plan.block
    slots = 2 * SLOTS
    shape = jax.ShapeDtypeStruct
    token_part = shape((4, ROWS, width), bf16)
    operands = [offsets, me, *tables, router, *tokens]
    in_specs = [smem(), smem()] + [vmem()] * (3 + len(tokens))
    if not forward:
        operands += saved
        in_specs += [vmem()] * 2
    operands += weights
    in_specs += [hbm()] * len(weights)
    out_shape, out_specs = [], []
    if forward:
        out_shape += [token_part] * 2
    if forward and not backward:
        out_shape += [shape((slots, width), bf16), shape((slots, width), f32)]
    if backward:
        out_shape += [token_part] * 2 + [shape(router.shape[1:], f32)]
    out_specs += [vmem()] * len(out_shape)
    if backward:
        out_shape += [shape(s, bf16) for s in plan.grad_shapes]
        out_specs += [hbm()] * len(plan.grad_shapes)
    scratch = [
        pltpu.VMEM((chunks, width, hidden), bf16),
        pltpu.VMEM((chunks, width, hidden), bf16),
        pltpu.VMEM((slots, width), bf16),
        pltpu.VMEM((slots, width), f32),
    ]
    if backward:
        scratch += [
            pltpu.VMEM((slots, width), bf16),
            pltpu.VMEM((slots, width), bf16),
            pltpu.VMEM((width, slots), bf16),
            pltpu.VMEM((width, slots), bf16),
            pltpu.VMEM((slots, width), f32),
            pltpu.VMEM((2, chunks, width, hidden), bf16),
            pltpu.SemaphoreType.DMA((2, chunks, count * near)),
        ]
    scratch += [pltpu.SemaphoreType.DMA((2, chunks, count * near))]
    return pl.pallas_call(
        lambda *refs: expert_kernel(plan, *refs),
        out_shape=tuple(out_shape),
        in_specs=in_specs,
        out_specs=tuple(out_specs),
        scratch_shapes=scratch,
        compiler_params=params(),
        cost_estimate=pl.CostEstimate(flops=flops, transcendentals=0, bytes_accessed=1),
        name="expert_layer",
    )(*operands)


def padded_bf16(rows):
    return jnp.pad(rows.astype(bf16), ((0, ROWS - LEN), (0, 0)))


def per_device(
    inputs,
    norm_gains,
    qkv_weight,
    out_weight,
    router_weight,
    expert_in,
    expert_out,
    routes,
    priority,
    cotangent,
):
    place = Place()
    experts = expert_in.shape[1]
    rows = qkv_weight.shape[1]
    zero = jnp.zeros((1,), jnp.int32)
    attn_off, expert_off = zero, zero
    me = place.expert.astype(jnp.int32).reshape(1)
    routers = jnp.swapaxes(router_weight, 1, 2)
    attn_w, expert_w = [], []
    tables = slot_tables(place, routes, priority, experts)
    for l in range(LAYERS):
        shard = jnp.concatenate([qkv_weight[l], jnp.swapaxes(out_weight[l], 0, 1)[:, None]], axis=1)
        full = gather_attention(place, shard.reshape(rows, -1))
        attn_w.append([full[j][None] for j in range(4)])
        expert_w.append([w[None] for w in gather_experts(place, expert_in[l], expert_out[l])])
    hidden_in, hidden_mid, qkv, ctx = {}, {}, {}, {}
    base, pieces = inputs, []
    saved = None
    gain_list, router_list, in_list, out_list, attn_list = {}, {}, {}, {}, {}
    for l in range(LAYERS):
        last = l == LAYERS - 1
        hidden_in[l], hidden_mid[l], normed, qkv[l], ctx[l] = attention_forward(
            attn_off, base, pieces, [], norm_gains[l], attn_w[l]
        )
        images = exchange_rows(place, normed)
        block = expert_w[l][0].shape
        at = [(0, None)], [(1, None)]
        here = [(j, 0) for j in range(8)]
        if last:
            grads = exchange_rows(place, padded_bf16(cotangent)[None])
            plan = Plan(l, block, here, [(j + 8, 0) for j in range(8)], *at, [block] * 2, *at)
            result = expert_layer(
                plan, expert_off, me, tables, routers, images + grads, None, expert_w[l]
            )
            tail = send_rows(place, pair_rows(place, result[:2]))
            result = result[2:]
            outputs = hidden_mid[l] + sum(p.astype(f32) for p in tail)
        else:
            plan = Plan(l, block, here, None, *at, None, None, None)
            *result, sent, expert_y = expert_layer(
                plan, expert_off, me, tables, routers, images, None, expert_w[l]
            )
            base, pieces = hidden_mid[l], send_rows(place, pair_rows(place, result))
            saved = [sent, expert_y]
    base = cotangent
    for l in reversed(range(LAYERS)):
        back = send_rows(place, pair_rows(place, result[:2]))
        router_list[l], *pieces = result[2:]
        in_list[l], out_list[l] = scatter_experts(place, pieces[0][0], pieces[1][0])
        base, branch, gain_list[l], *parts = attention_backward(
            attn_off, base, back, hidden_in[l], hidden_mid[l], norm_gains[l], attn_w[l], qkv[l], ctx[l],
            ROWS if l else LEN,
        )
        if l:
            grads = exchange_rows(place, branch[None])
            plan = Plan(l - 1, block, None, here, *at, [block] * 2, *at)
            result = expert_layer(
                plan, expert_off, me, tables, routers, grads, saved, expert_w[l - 1]
            )
        total = scatter_attention(place, jnp.concatenate(parts), rows)
        attn_list[l] = total.astype(f32).reshape(rows, 4, -1)
    gains = jnp.stack([gain_list[l] for l in range(LAYERS)])
    router = jnp.stack([router_list[l] for l in range(LAYERS)])
    small = jnp.concatenate([gains.reshape(-1), router.reshape(-1)]).reshape(-1, 512)
    for bit in range(place.count.bit_length() - 1):
        small = small + place.swap(small, 1 << bit)
    small = small.reshape(-1)
    gains, router = small[: gains.size].reshape(gains.shape), small[gains.size :].reshape(router.shape)
    return (
        outputs[:LEN].astype(bf16),
        base,
        gains,
        jnp.stack([attn_list[l][:, :3] for l in range(LAYERS)]),
        jnp.stack([jnp.swapaxes(attn_list[l][:, 3], 0, 1) for l in range(LAYERS)]),
        jnp.swapaxes(router, 1, 2),
        jnp.stack([in_list[l] for l in range(LAYERS)]),
        jnp.stack([out_list[l] for l in range(LAYERS)]),
    )


CORE, Y, X, NEAR, FAR = 1, 2, 4, 8, 16


def tie(*values):
    return lax.optimization_barrier(values)


def expert_blocks(place, w_in, w_out):
    order = place.expert ^ jnp.arange(w_in.shape[0])
    return jnp.stack([w_in[order], jnp.swapaxes(w_out, 1, 2)[order]])


def chip_pairs(place, blocks):
    return jnp.stack([blocks[:, 0::2], place.swap(blocks[:, 1::2], CORE)], axis=2)


def send_pairs(place, pair):
    two, chips, cores, rows, width = pair.shape
    got = [pair[:, 0]] + [place.swap(pair[:, k], 2 * k) for k in (1, 2, 3)]
    return jnp.stack(got, axis=1).reshape(two, 2, chips * cores // 2, rows, width)


def plane_blocks(place, blocks):
    return send_pairs(place, chip_pairs(place, blocks))


def mixed(place, value, even, odd):
    pairs = [(i, i ^ (odd if i & CORE else even)) for i in range(place.count)]
    return lax.ppermute(value, AXES, pairs)


def attention_shard(qkv_weight, out_weight):
    shard = jnp.concatenate([qkv_weight, jnp.swapaxes(out_weight, 0, 1)[:, None]], axis=1)
    return shard.reshape(shard.shape[0], -1)


def widen(place, held, mask):
    return jnp.concatenate([held, place.swap(held, mask)])


def halve(place, held, mask):
    half = held.shape[0] // 2
    return held[:half] + place.swap(held[half:], mask)


def send_sums(place, pair):
    return [pair[:, 0]] + [place.swap(pair[:, k], 2 * k) for k in (1, 2, 3)]


def unpack_kernel(layer, filled, me_ref, *refs):
    pieces, refs = refs[:4], refs[4 + 2 * filled :]
    in_ref, out_ref, in_buf, out_buf, sems = refs
    copies = []
    for k, piece in enumerate(pieces):
        for core in (0, 1):
            j = 2 * k + core
            expert = jnp.bitwise_xor(me_ref[0], j)
            in_buf[j] = piece[0, core].astype(f32)
            out_buf[j] = piece[1, core].astype(f32)
            copies.append(pltpu.make_async_copy(in_buf.at[j], in_ref.at[layer, expert], sems.at[0, j]))
            copies.append(pltpu.make_async_copy(out_buf.at[j], out_ref.at[layer, expert], sems.at[1, j]))
            for copy in copies[-2:]:
                copy.start()
    for copy in copies:
        copy.wait()


def unpack_sums(me, pieces, layer, layers, before=()):
    unused, cores, rows, width = pieces[0].shape
    experts = cores * len(pieces)
    shape = jax.ShapeDtypeStruct
    return pl.pallas_call(
        lambda *refs: unpack_kernel(layer, len(before) // 2, *refs),
        out_shape=(shape((layers, experts, rows, width), f32),) * 2,
        in_specs=[smem()] + [vmem()] * len(pieces) + [hbm()] * len(before),
        out_specs=(hbm(), hbm()),
        scratch_shapes=[
            pltpu.VMEM((experts, rows, width), f32),
            pltpu.VMEM((experts, rows, width), f32),
            pltpu.SemaphoreType.DMA((2, experts)),
        ],
        input_output_aliases={5: 0, 6: 1} if before else {},
        compiler_params=params(),
        cost_estimate=pl.CostEstimate(flops=1, transcendentals=0, bytes_accessed=1),
        name="unpack",
    )(me, *pieces, *before)


def per_device_plane(
    inputs,
    norm_gains,
    qkv_weight,
    out_weight,
    router_weight,
    expert_in,
    expert_out,
    routes,
    priority,
    cotangent,
):
    place = Place()
    swap = place.swap
    experts = expert_in.shape[1]
    rows = qkv_weight.shape[1]
    attn_order = [x | n * 2 | f * 4 for x in (0, 1) for n in (0, 1) for f in (0, 1)]
    attn_off = ((place.dp ^ jnp.array(attn_order, jnp.int32)) * rows).astype(jnp.int32)
    core = place.tensor & CORE
    replica = jnp.stack([jnp.zeros_like(core), 4 - 2 * core, 2 + 2 * core, 6 + 0 * core])
    expert_off = ((place.dp ^ replica[:, None] ^ jnp.arange(2)[None, :]) * rows).reshape(-1).astype(jnp.int32)
    me = place.expert.astype(jnp.int32).reshape(1)
    routers = jnp.swapaxes(router_weight, 1, 2)
    block = (2, place.tensor_size, rows, expert_in.shape[3])

    pair = chip_pairs(place, expert_blocks(place, expert_in[0], expert_out[0]))
    held = jnp.stack([attention_shard(qkv_weight[l], out_weight[l]) for l in (0, 1)])[None]
    pair, held = tie(pair, held)
    own0 = send_pairs(place, pair)
    held = widen(place, widen(place, held, FAR), NEAR)
    held, own0 = tie(held, own0)
    a0 = mixed(place, own0, FAR, NEAR)
    held = widen(place, held, X)
    held0, held1 = held[:, 0], held[:, 1]
    over0 = swap(held0, Y)
    tables = slot_tables(place, routes, priority, experts)
    over0, a0, blocks1, me, expert_off, *tables = tie(
        over0, a0, expert_blocks(place, expert_in[1], expert_out[1]), me, expert_off, *tables
    )
    b0, c0 = mixed(place, own0, NEAR, FAR), mixed(place, a0, NEAR, FAR)
    weights0 = [held0, swap(held0, CORE), over0, swap(over0, CORE)]
    own1 = plane_blocks(place, blocks1)

    hidden_in0, hidden_mid0, normed, qkv0, ctx0 = attention_forward(
        attn_off, inputs, [], [], norm_gains[0], weights0
    )
    normed, own1, held1 = tie(normed, own1, held1)
    images = exchange_rows(place, normed)
    over1 = swap(held1, Y)
    weights1 = [held1, swap(held1, CORE), over1, swap(over1, CORE)]
    tied = tie(*images, *weights1)
    images, weights1 = tied[:8], tied[8:]
    b0, c0, own1 = tie(b0, c0, own1)
    a1, b1 = mixed(place, own1, FAR, NEAR), mixed(place, own1, NEAR, FAR)
    first = [(j, 0) for j in range(8)]
    second = [(j, 1) for j in range(8)]
    parts = [[(m, io) for m in range(4)] for io in (0, 1)]
    *rows0, sent, expert_y = expert_layer(
        Plan(0, block, first, None, *parts, None, None, None),
        expert_off, me, tables, routers, images, None, [own0, a0, b0, c0],
    )
    pieces = send_rows(place, pair_rows(place, rows0))
    hidden_in1, hidden_mid1, normed, qkv1, ctx1 = attention_forward(
        attn_off, hidden_mid0, pieces, [cotangent], norm_gains[1], weights1
    )
    normed, a1 = tie(normed, a1)
    c1 = mixed(place, a1, NEAR, FAR)
    images = exchange_rows(place, normed)
    images[2], b1 = tie(images[2], b1)
    grad_shapes = [(2,) + block, (2,) + block, (2, 2) + block]
    grad_parts = [[(0, io), (1, io), (2, (0, io)), (2, (1, io))] for io in (0, 1)]
    result = expert_layer(
        Plan(1, block, first, second, *parts, grad_shapes, *grad_parts),
        expert_off, me, tables, routers, images, None, [own1, a1, b1, c1],
    )
    out_rows, back_rows, router1, (own, a, bc) = result[:2], result[2:4], result[4], result[5:]
    bc = mixed(place, bc, NEAR, FAR)
    pieces = send_rows(place, pair_rows(place, back_rows))
    grad1, branch, gains1, *parts1 = attention_backward(
        attn_off, cotangent, pieces, hidden_in1, hidden_mid1, norm_gains[1], weights1, qkv1, ctx1, ROWS
    )
    far1 = parts1[2] + swap(parts1[3], CORE)
    images = exchange_rows(place, branch[None])
    tied = tie(*images, a, bc, far1)
    images, (a, bc, far1) = tied[:8], tied[8:]
    far1 = swap(far1, Y)
    a = mixed(place, a + bc[1], FAR, NEAR)
    result = expert_layer(
        Plan(0, block, None, first, *parts, grad_shapes, *grad_parts),
        expert_off, me, tables, routers, images, [sent, expert_y], [own0, a0, b0, c0],
        flops=10**10,
    )
    back_rows, router0, (own0, a0, bc0) = result[:2], result[2], result[3:]
    *back_rows, far1 = tie(*back_rows, far1)
    bc0 = mixed(place, bc0, NEAR, FAR)
    pieces = send_rows(place, pair_rows(place, back_rows))
    pieces[3], a = tie(pieces[3], a)
    grad0, unused, gains0, *parts0 = attention_backward(
        attn_off, grad1, pieces, hidden_in0, hidden_mid0, norm_gains[0], weights0, qkv0, ctx0, LEN
    )
    gains0, a0, a, bc, own, *out_rows = tie(gains0, a0, a, bc, own, *out_rows)
    gains, router = jnp.stack([gains0, gains1]), jnp.stack([router0, router1])
    small = jnp.concatenate([gains.reshape(-1), router.reshape(-1)]).reshape(-1, 512)
    recv = [swap(v, CORE) for v in (parts0[3], parts0[1], parts1[1])]
    *recv, sum1, parts0[0], parts0[2], parts1[0] = tie(
        *recv, own + bc[0] + a, parts0[0], parts0[2], parts1[0]
    )
    far0, near0, near1 = parts0[2] + recv[0], parts0[0] + recv[1], parts1[0] + recv[2]
    far0 = swap(far0, Y)
    sum1 = send_sums(place, chip_pairs(place, sum1.reshape((2, -1) + sum1.shape[3:])))
    attn_sum = [halve(place, near + far, X) for near, far in ((near0, far0), (near1, far1))]
    attn_sum = jnp.stack(attn_sum, axis=1)
    tied = tie(*sum1, bc0, a0, small, *out_rows)
    sum1, (bc0, a0, small), out_rows = tied[:4], tied[4:7], tied[7:]
    a0 = mixed(place, a0 + bc0[1], FAR, NEAR)
    tail = send_rows(place, pair_rows(place, out_rows))
    for mask in (CORE, X, Y):
        small = small + swap(small, mask)
    grads1 = unpack_sums(me, sum1, 1, LAYERS)
    tied = tie(attn_sum, small, a0, *grads1, *tail)
    (attn_sum, small, a0), grads1, tail = tied[:3], tied[3:5], tied[5:]
    outputs = hidden_mid1 + sum(p.astype(f32) for p in tail)
    sum0 = own0 + a0 + bc0[0]
    pair0 = chip_pairs(place, sum0.reshape((2, -1) + sum0.shape[3:]))
    pair0, attn_sum, small = tie(pair0, attn_sum, small)
    sum0 = send_sums(place, pair0)
    for mask in (NEAR, FAR):
        attn_sum = halve(place, attn_sum, mask)
        small = small + swap(small, mask)
    in_grads, out_grads = unpack_sums(me, sum0, 0, LAYERS, grads1)
    small = small.reshape(-1)
    gains, router = small[: gains.size].reshape(gains.shape), small[gains.size :].reshape(router.shape)
    attn = attn_sum.astype(f32).reshape(2, rows, 4, -1)
    return (
        outputs[:LEN].astype(bf16),
        grad0,
        gains,
        attn[:, :, :3],
        jnp.swapaxes(attn[:, :, 3], 1, 2),
        jnp.swapaxes(router, 1, 2),
        in_grads,
        jnp.swapaxes(out_grads, 2, 3),
    )


def solution(mesh):
    in_specs = (
        P(("dp", "tensor"), None),
        P(),
        P(None, "dp", None, "tensor"),
        P(None, "tensor", "dp"),
        P(),
        P(None, None, "dp", "tensor"),
        P(None, None, "tensor", "dp"),
        P(None, "dp", None),
        P(None, "dp", None),
        P(("dp", "tensor"), None),
    )
    out_specs = (
        P(("dp", "tensor"), None),
        P(("dp", "tensor"), None),
        P(),
        P(None, "dp", None, "tensor"),
        P(None, "tensor", "dp"),
        P(),
        P(None, None, "dp", "tensor"),
        P(None, None, "tensor", "dp"),
    )
    fast = mesh.shape["dp"] == 8 and mesh.shape["tensor"] == 4 and LAYERS == 2
    return jax.shard_map(
        per_device_plane if fast else per_device, mesh=mesh, in_specs=in_specs, out_specs=out_specs, check_vma=False
    )
```

```python
import jax
import jax.numpy as jnp
from jax import lax
from jax.experimental import pallas as pl
from jax.experimental.pallas import tpu as pltpu
from jax.sharding import PartitionSpec as P

HD = 64
LEN = 197
LAYERS = 2
CAP = 247
SLOTS = 256
ROWS = 200
NORM_EPS = 1e-06
f32 = jnp.float32
bf16 = jnp.bfloat16
AXES = ("dp", "tensor")


def mm(spec, *args):
    return jnp.einsum(spec, *args, preferred_element_type=f32)


class Place:
    def __init__(self):
        self.dp_size = lax.axis_size("dp")
        self.tensor_size = lax.axis_size("tensor")
        self.count = self.dp_size * self.tensor_size
        self.dp = lax.axis_index("dp")
        self.tensor = lax.axis_index("tensor")
        self.near = self.dp & 1
        self.expert = self.near * self.tensor_size + self.tensor

    def swap(self, value, mask):
        pairs = [(i, i ^ mask) for i in range(self.count)]
        return lax.ppermute(value, AXES, pairs)

    def dp_groups(self):
        return [[d for d in range(self.dp_size) if d & 1 == b] for b in (0, 1)]

    def ordered(self, mine, theirs, bit):
        return jnp.stack([jnp.where(bit, theirs, mine), jnp.where(bit, mine, theirs)])


def gather_attention(place, shard):
    rows, width = shard.shape
    bits = place.dp_size.bit_length() - 1
    held = shard
    for bit in reversed(range(bits)):
        other = place.swap(held, place.tensor_size << bit)
        held = place.ordered(held, other, (place.dp >> bit) & 1)
    held = held.reshape((2,) * bits + (rows, width))
    held = jnp.transpose(held, tuple(reversed(range(bits))) + (bits, bits + 1))
    held = held.reshape(1, place.dp_size * rows, width)
    for mask in (2, 1):
        held = jnp.stack([held, place.swap(held, mask)], axis=1 if mask == 1 else 0)
        held = held.reshape((-1,) + held.shape[2:])
    return held


def scatter_attention(place, blocks, rows):
    bits = place.dp_size.bit_length() - 1
    held = blocks.reshape((2, 2) + blocks.shape[1:])
    held = held[:, 0] + place.swap(held[:, 1], 1)
    held = held[0] + place.swap(held[1], 2)
    for bit in range(bits):
        parts = held.reshape((-1, 2, rows, held.shape[-1]))
        mine = lax.dynamic_index_in_dim(parts, (place.dp >> bit) & 1, 1, keepdims=False)
        theirs = lax.dynamic_index_in_dim(parts, 1 - ((place.dp >> bit) & 1), 1, keepdims=False)
        held = mine + place.swap(theirs, place.tensor_size << bit)
        held = held.reshape(-1, held.shape[-1])
    return held


def plane_exchange(place, blocks):
    even, odd = blocks[0::2], blocks[1::2]
    pair = jnp.stack([even, place.swap(odd, 1)], axis=1)
    got = [pair[0]] + [place.swap(pair[k], 2 * k) for k in (1, 2, 3)]
    return jnp.concatenate(got, axis=0)


def gather_experts(place, w_in, w_out):
    blocks = jnp.stack([w_in, jnp.swapaxes(w_out, 1, 2)], axis=1)
    experts, unused, rows, width = blocks.shape
    order = place.expert ^ jnp.arange(experts)
    got = plane_exchange(place, blocks[order])
    got = got.reshape((2, place.tensor_size, 2, rows, width))
    got = place.ordered(got[0], got[1], place.near)
    full = lax.all_gather(got, "dp", axis=0, tiled=False, axis_index_groups=place.dp_groups())
    full = jnp.transpose(full, (3, 2, 0, 1, 4, 5))
    full = full.reshape((2, place.tensor_size, -1, width))
    return full[0], full[1]


def scatter_experts(place, grad_in, grad_out):
    tensor, model, width = grad_in.shape
    rows = model // place.dp_size
    both = jnp.stack([grad_in, grad_out]).astype(bf16)
    both = both.reshape((2, tensor, -1, 2, rows, width))
    both = jnp.transpose(both, (2, 3, 1, 0, 4, 5))
    mine = lax.psum_scatter(
        both, "dp", scatter_dimension=0, tiled=False, axis_index_groups=place.dp_groups()
    )
    mine = place.ordered(mine[0], mine[1], place.near)
    got = plane_exchange(place, mine.reshape((-1, 2, rows, width)))
    order = place.expert ^ jnp.arange(got.shape[0])
    got = got[order].astype(f32)
    return got[:, 0], jnp.swapaxes(got[:, 1], 1, 2)


LANES = 256
SPLIT = 1


def slot_kernel(experts, mine_ref, ids, rank, mine, theirs):
    tensor = mine.shape[1]
    expert, other = mine_ref[0], mine_ref[1]
    here = mine_ref[2]
    for l in range(ids.shape[0]):
        choice = lax.broadcasted_iota(jnp.int32, (experts, tensor * LANES), 0)
        first, second = ids[l, 0:1, :] == choice, ids[l, 1:2, :] == choice
        order = rank[l : l + 1, :].astype(f32)
        column = jnp.broadcast_to(order, (8, tensor * LANES)).T[:, 0:1]
        earlier = (column < order).astype(f32).astype(bf16)
        both = jnp.concatenate([first.astype(f32), second.astype(f32)]).astype(bf16)
        counts = dot(both, earlier)
        total = jnp.sum(first.astype(f32), axis=1, keepdims=True)
        slot = jnp.where(first, counts[:experts], jnp.where(second, total + counts[experts:], -1.0))
        slot = jnp.where(slot < CAP, slot, -1.0)
        for which, target in ((expert, mine), (other, theirs)):
            row = jnp.sum(jnp.where(choice == which, slot, 0.0), axis=0, keepdims=True).astype(jnp.int32)
            for t in range(tensor):
                target[l, pl.ds(jnp.bitwise_xor(here, t), 1), :] = row[:, t * LANES : (t + 1) * LANES]


def slot_tables(place, routes, priority, experts):
    layers, count, unused = routes.shape
    spread = ((0, 0), (0, 0), (0, 0), (0, LANES - LEN))
    ids = jnp.swapaxes(routes, 1, 2).reshape(layers, 2, -1, LEN)
    ids = jnp.pad(ids, spread, constant_values=-1).reshape(layers, 2, -1)
    rank = jnp.pad(priority.reshape(layers, 1, -1, LEN), spread).reshape(layers, -1)
    where = jnp.stack([place.expert, place.expert ^ place.tensor_size, place.tensor]).astype(jnp.int32)
    shape = jax.ShapeDtypeStruct((layers, place.tensor_size, LANES), jnp.int32)
    mine, theirs = pl.pallas_call(
        lambda *refs: slot_kernel(experts, *refs),
        out_shape=(shape, shape),
        in_specs=[smem(), vmem(), vmem()],
        out_specs=(vmem(), vmem()),
        compiler_params=params(),
        cost_estimate=pl.CostEstimate(flops=1, transcendentals=0, bytes_accessed=1),
        name="slots",
    )(where, ids, rank)
    return mine, place.swap(theirs, place.tensor_size)


def exchange_rows(place, own):
    even = [own] + [place.swap(own, 2 * k) for k in (1, 2, 3)]
    odd = [place.swap(rows, 1) for rows in even]
    return [rows for pair in zip(even, odd) for rows in pair]


def add_kernel(even, odd, *sums):
    for k, target in enumerate(sums):
        target[...] = (even[k].astype(f32) + odd[k].astype(f32)).astype(bf16)


def pair_rows(place, parts, *others):
    even, odd = parts
    odd, *others = lax.optimization_barrier((place.swap(odd, 1), *others))
    return list(pl.pallas_call(
        add_kernel,
        out_shape=(jax.ShapeDtypeStruct(even.shape[1:], bf16),) * 4,
        in_specs=[vmem()] * 2,
        out_specs=(vmem(),) * 4,
        cost_estimate=pl.CostEstimate(flops=1, transcendentals=0, bytes_accessed=1),
        name="add_rows",
    )(even, odd)) + others


def send_rows(place, sums):
    return [sums[0]] + [place.swap(sums[k], 2 * k) for k in (1, 2, 3)]


def dot(a, b):
    return lax.dot_general(a, b, (((1,), (0,)), ((), ())), preferred_element_type=f32)


def dot_t(a, b):
    return lax.dot_general(a, b, (((1,), (1,)), ((), ())), preferred_element_type=f32)


def t_dot(a, b):
    return lax.dot_general(a, b, (((0,), (0,)), ((), ())), preferred_element_type=f32)


def normalized(rows):
    average = jnp.mean(rows, axis=-1, keepdims=True)
    centered = rows - average
    variance = jnp.mean(centered * centered, axis=-1, keepdims=True)
    scale = lax.rsqrt(variance + NORM_EPS)
    return centered * scale, scale


def norm_grad(rows, gain, grad):
    unit, scale = normalized(rows)
    scaled = grad * gain
    pull = scaled - jnp.mean(scaled, axis=-1, keepdims=True)
    pull = pull - unit * jnp.mean(scaled * unit, axis=-1, keepdims=True)
    return scale * pull, jnp.sum(grad * unit, axis=0, keepdims=True)


def head_masks():
    lane = lax.broadcasted_iota(jnp.int32, (1, 2 * HD), 1)
    return lane < HD, lane >= HD


def only(values, mask):
    return jnp.where(mask, values.astype(f32), 0.0).astype(bf16)


def head_probs(queries, keys, mask):
    scores = dot_t(only(queries, mask), keys) * (HD ** (-0.5))
    valid = lax.broadcasted_iota(jnp.int32, scores.shape, 1) < LEN
    scores = jnp.where(valid, scores, -1e30)
    top = jnp.max(scores, axis=-1, keepdims=True)
    weights = jnp.exp(scores - top)
    return weights / jnp.sum(weights, axis=-1, keepdims=True)


def weight_copies(off_ref, pieces, buffer, sems):
    result = []
    for j, piece in enumerate(pieces):
        count, rows, unused = piece.shape
        result.append([
            pltpu.make_async_copy(
                piece.at[i],
                buffer.at[j, pl.ds(pl.multiple_of(off_ref[i], rows), rows)],
                sems.at[j, i],
            )
            for i in range(count)
        ])
    return result


def padded_rows(ref, scratch):
    if ref.shape[0] == ROWS:
        return ref[...].astype(f32)
    scratch[...] = jnp.zeros_like(scratch)
    scratch[0 : ref.shape[0]] = ref[...].astype(f32)
    return scratch[...]


def attention_forward_kernel(piece_count, extra_count, off_ref, base, *refs):
    pieces, refs = refs[:piece_count], refs[piece_count:]
    extra, refs = refs[:extra_count], refs[extra_count:]
    gains, w0, w1, w2, w3, hidden, mid, normed, qkv, ctx, scratch, wbuf, sems = refs
    copies = weight_copies(off_ref, (w0, w1, w2, w3), wbuf, sems)
    for group in copies:
        for copy in group:
            copy.start()
    rows = padded_rows(base, scratch)
    for piece in pieces:
        rows = rows + piece[...].astype(f32)
    hidden[...] = rows
    unit, unused = normalized(rows)
    normed_a = (unit * gains[0:1]).astype(bf16)
    low, high = head_masks()
    for group in copies:
        for copy in group:
            copy.wait()

    @pl.loop(0, 4)
    def _(j):
        qkv[:, pl.ds(pl.multiple_of(j * 6 * HD, 6 * HD), 6 * HD)] = dot(normed_a, wbuf[j, :, : 6 * HD]).astype(bf16)

    probs = []
    for j in range(4):
        part = qkv[:, j * 6 * HD : (j + 1) * 6 * HD]
        probs.append([head_probs(part[:, : 2 * HD], part[:, 2 * HD : 4 * HD], m).astype(bf16) for m in (low, high)])
    total = rows
    for j in range(4):
        values = qkv[:, j * 6 * HD + 4 * HD : (j + 1) * 6 * HD]
        context = jnp.where(low, dot(probs[j][0], values), dot(probs[j][1], values)).astype(bf16)
        ctx[:, j * 2 * HD : (j + 1) * 2 * HD] = context
        total = total + dot_t(context, wbuf[j, :, 6 * HD :])
    mid[...] = total
    unit, unused = normalized(total)
    normed[0] = (unit * gains[1:2]).astype(bf16)
    for ref in extra:
        normed[1] = padded_rows(ref, scratch).astype(bf16)


def vmem():
    return pl.BlockSpec(memory_space=pltpu.VMEM)


def smem():
    return pl.BlockSpec(memory_space=pltpu.SMEM)


def hbm():
    return pl.BlockSpec(memory_space=pl.ANY)


def params():
    return pltpu.CompilerParams(vmem_limit_bytes=60 << 20)


def attention_forward(offsets, base, pieces, extra, gains, weights):
    width = base.shape[1]
    shape = jax.ShapeDtypeStruct
    return pl.pallas_call(
        lambda *refs: attention_forward_kernel(len(pieces), len(extra), *refs),
        out_shape=(
            shape((ROWS, width), f32),
            shape((ROWS, width), f32),
            shape((1 + len(extra), ROWS, width), bf16),
            shape((ROWS, 3 * width), bf16),
            shape((ROWS, width), bf16),
        ),
        in_specs=[smem(), vmem()] + [vmem()] * (len(pieces) + len(extra)) + [vmem()] + [hbm()] * 4,
        out_specs=[vmem()] * 5,
        scratch_shapes=[
            pltpu.VMEM((ROWS, width), f32),
            pltpu.VMEM((4, width, width), bf16),
            pltpu.SemaphoreType.DMA((4, weights[0].shape[0])),
        ],
        compiler_params=params(),
        cost_estimate=pl.CostEstimate(flops=1, transcendentals=0, bytes_accessed=1),
        name="attention_forward",
    )(offsets, base, *pieces, *extra, gains, *weights)


def attention_backward_kernel(
    off_ref, base, p0, p1, p2, p3, hidden_in, hidden_mid, gains, w0, w1, w2, w3, qkv, ctx,
    grad_out, branch, gain_out, g0, g1, g2, g3, scratch, wbuf, gbuf, mixed_buf, back_buf, sems, out_sems,
):
    copies = weight_copies(off_ref, (w0, w1, w2, w3), wbuf, sems)
    for group in copies:
        for copy in group:
            copy.start()
    grad = padded_rows(base, scratch)
    normed_grad = p0[...].astype(f32) + p1[...].astype(f32) + p2[...].astype(f32) + p3[...].astype(f32)
    part, gain_expert = norm_grad(hidden_mid[...], gains[1:2], normed_grad)
    grad = grad + part
    attn_grad = grad.astype(bf16)
    attn_grad_t = attn_grad.T
    rows_in = hidden_in[...]
    unit, unused = normalized(rows_in)
    normed_t = (unit * gains[0:1]).astype(bf16).T
    low, high = head_masks()
    scale = HD ** (-0.5)
    for group in copies:
        for copy in group:
            copy.wait()
    heads = [(j, mask) for j in range(4) for mask in (low, high)]
    parts = [qkv[:, j * 6 * HD : (j + 1) * 6 * HD] for j in range(4)]
    queries = [part[:, : 2 * HD] for part in parts]
    keys = [part[:, 2 * HD : 4 * HD] for part in parts]
    values = [part[:, 4 * HD :] for part in parts]

    @pl.loop(0, 4)
    def _(j):
        back_buf[j] = dot(attn_grad, wbuf[j, :, 6 * HD :]).astype(bf16)

    context_grads = [back_buf[j] for j in range(4)]
    probs = [head_probs(queries[j], keys[j], mask) for j, mask in heads]
    probs_grads = [dot_t(only(context_grads[j], mask), values[j]) for j, mask in heads]
    v_grads = [t_dot(probs[i].astype(bf16), context_grads[j]) for i, (j, mask) in enumerate(heads)]
    score_grads = [
        (p * (g - jnp.sum(p * g, axis=-1, keepdims=True))).astype(bf16) for p, g in zip(probs, probs_grads)
    ]
    q_grads = [dot(score_grads[i], keys[j]) * scale for i, (j, mask) in enumerate(heads)]
    k_grads = [t_dot(score_grads[i], queries[j]) * scale for i, (j, mask) in enumerate(heads)]
    for j in range(4):
        mixed_buf[j] = jnp.concatenate(
            [jnp.where(low, g[2 * j], g[2 * j + 1]).astype(bf16) for g in (q_grads, k_grads, v_grads)], axis=1
        )
    scratch[...] = jnp.zeros_like(scratch)

    @pl.loop(0, 4)
    def _(j):
        mixed = mixed_buf[j]
        context = ctx[:, pl.ds(pl.multiple_of(j * 2 * HD, 2 * HD), 2 * HD)]
        gbuf[j, :, : 6 * HD] = dot(normed_t, mixed).astype(bf16)
        gbuf[j, :, 6 * HD :] = dot(attn_grad_t, context).astype(bf16)
        scratch[...] += dot_t(mixed, wbuf[j, :, : 6 * HD])

    normed_part = scratch[...]
    sends = []
    for j, target in enumerate((g0, g1, g2, g3)):
        count, rows, unused = target.shape
        for i in range(count):
            send = pltpu.make_async_copy(
                gbuf.at[j, pl.ds(pl.multiple_of(off_ref[i], rows), rows)], target.at[i], out_sems.at[j, i]
            )
            send.start()
            sends.append(send)
    part, gain_attn = norm_grad(rows_in, gains[0:1], normed_part)
    grad = grad + part
    grad_out[...] = grad[: grad_out.shape[0]]
    branch[...] = grad.astype(bf16)
    gain_out[...] = jnp.concatenate([gain_attn, gain_expert], axis=0)
    for send in sends:
        send.wait()


def attention_backward(offsets, base, pieces, hidden_in, hidden_mid, gains, weights, qkv, ctx, out_rows):
    width = base.shape[1]
    shape = jax.ShapeDtypeStruct
    blocks = weights[0].shape
    return pl.pallas_call(
        attention_backward_kernel,
        out_shape=(
            shape((out_rows, width), f32),
            shape((ROWS, width), bf16),
            shape((2, width), f32),
        ) + (shape(blocks, bf16),) * 4,
        in_specs=[smem()] + [vmem()] * 8 + [hbm()] * 4 + [vmem()] * 2,
        out_specs=[vmem()] * 3 + [hbm()] * 4,
        scratch_shapes=[
            pltpu.VMEM((ROWS, width), f32),
            pltpu.VMEM((4, width, width), bf16),
            pltpu.VMEM((4, width, width), bf16),
            pltpu.VMEM((4, ROWS, 6 * HD), bf16),
            pltpu.VMEM((4, ROWS, 2 * HD), bf16),
            pltpu.SemaphoreType.DMA((4, blocks[0])),
            pltpu.SemaphoreType.DMA((4, blocks[0])),
        ],
        compiler_params=params(),
        cost_estimate=pl.CostEstimate(flops=1, transcendentals=0, bytes_accessed=1),
        name="attention_backward",
    )(offsets, base, *pieces, hidden_in, hidden_mid, gains, *weights, qkv, ctx)


def split(values):
    high = values.astype(bf16)
    return high, (values - high.astype(f32)).astype(bf16)


ROOT = 0.7978845608028654
CUBE = 0.044715


def expert_kernel(plan, off_ref, me_ref, mine, theirs, router, *refs):
    forward, backward = plan.images is not None, plan.grads is not None
    piece_count = len(plan.w_in)
    refs = list(refs)

    def take(count):
        taken, refs[:count] = refs[:count], []
        return taken

    tokens = take(plan.token_arrays)
    sent_in, y_in = take(2) if not forward else (None, None)
    sources = take(plan.weight_arrays)
    parts = take(2) if forward else None
    sent_out, y_out = take(2) if forward and not backward else (None, None)
    if backward:
        back_parts = take(2)
        (router_grad,) = take(1)
        targets = take(len(plan.grad_shapes))
    in_buf, out_buf, sent_buf, y_buf = take(4)
    if backward:
        slot_buf, branch_buf, slot_t, sent_t, back_buf, gbuf, out_sems = take(7)
    (sems,) = take(1)

    near, chunks, rows, width = plan.block

    def loads(c, which):
        result = []
        for m in range(piece_count):
            for n in range(near):
                at = pl.ds(pl.multiple_of(off_ref[m * near + n], rows), rows)
                index, part = (plan.w_in, plan.w_out)[which][m]
                piece = sources[index] if part is None else sources[index].at[part]
                buf = (in_buf, out_buf)[which]
                result.append(
                    pltpu.make_async_copy(piece.at[n, c], buf.at[c, at], sems.at[which, c, m * near + n])
                )
        return result

    @pl.loop(0, chunks)
    def _(c):
        for which in (0, 1):
            for copy in loads(c, which):
                copy.start()

    def hot_rows(g, t, slot):
        row = (mine, theirs)[g][plan.layer, t : t + 1, :][:, :ROWS]
        return (row == slot).astype(f32).astype(bf16)

    def gather(images):
        for g in (0, 1):
            total = None
            for t in range(4):
                j = g * 4 + t
                slot = lax.broadcasted_iota(jnp.int32, (SLOTS, ROWS), 0)
                hot = hot_rows(g, t, slot)
                index, layer = images[j]
                part = dot(hot, tokens[index][layer])
                total = part if total is None else total + part
            yield g, total

    def scatter(slot_rows, parts):
        for g in (0, 1):
            for t in range(4):
                j = g * 4 + t
                slot = lax.broadcasted_iota(jnp.int32, (SLOTS, ROWS), 0)
                part = t_dot(hot_rows(g, t, slot), slot_rows[g * SLOTS : (g + 1) * SLOTS]).astype(bf16)
                parts[j % 2][j // 2] = part

    if forward:
        for g, rows_g in gather(plan.images):
            sent_buf[g * SLOTS : (g + 1) * SLOTS] = rows_g.astype(bf16)
    else:
        sent_buf[...] = sent_in[...]
    sent = sent_buf[...]
    logits = dot_t(sent, router[plan.layer])
    top = jnp.max(logits, axis=-1, keepdims=True)
    weights = jnp.exp(logits - top)
    probs = weights / jnp.sum(weights, axis=-1, keepdims=True)
    is_mine = lax.broadcasted_iota(jnp.int32, probs.shape, 1) == me_ref[0]
    gate = jnp.sum(jnp.where(is_mine, probs, 0.0), axis=-1, keepdims=True)

    if backward:
        for g, rows_g in gather(plan.grads):
            part = slice(g * SLOTS, (g + 1) * SLOTS)
            slot_buf[part] = (gate[part] * rows_g).astype(bf16)
            branch_buf[part] = rows_g.astype(bf16)
        slot_t[...] = slot_buf[...].T
        sent_t[...] = sent.T
        back_buf[...] = jnp.zeros_like(back_buf)
    if forward:
        y_buf[...] = jnp.zeros_like(y_buf)

    def stores(c, which):
        result = []
        for m in range(piece_count):
            for n in range(near):
                at = pl.ds(pl.multiple_of(off_ref[m * near + n], rows), rows)
                index, part = (plan.grad_in, plan.grad_out)[which][m]
                piece = targets[index] if part is None else targets[index].at[part]
                result.append(
                    pltpu.make_async_copy(
                        gbuf.at[which, c, at], piece.at[n, c], out_sems.at[which, c, m * near + n]
                    )
                )
        return result

    halves = [slice(h * width // SPLIT, (h + 1) * width // SPLIT) for h in range(SPLIT)]

    @pl.loop(0, chunks)
    def _(c):
        for which in (0, 1):
            for copy in loads(c, which):
                copy.wait()
        pres = [dot(sent_buf[...], in_buf[c, :, at]) for at in halves]
        act_grads = [dot(slot_buf[...], out_buf[c, :, at]) for at in halves] if backward else None
        for h, at in enumerate(halves):
            pre = pres[h]
            square = pre * pre
            bend = jnp.tanh(pre * (ROOT + ROOT * CUBE * square))
            rise = 0.5 + 0.5 * bend
            act = pre * rise
            low_act = act.astype(bf16)
            if forward:
                y_buf[...] += dot_t(low_act, out_buf[c, :, at])
            if backward:
                gbuf[1, c, :, at] = dot(slot_t[...], low_act).astype(bf16)
                slope = rise + act * ((1.0 - bend) * (ROOT + 3.0 * ROOT * CUBE * square))
                pre_grad = (act_grads[h] * slope).astype(bf16)
                gbuf[0, c, :, at] = dot(sent_t[...], pre_grad).astype(bf16)
                back_buf[...] += dot_t(pre_grad, in_buf[c, :, at])
        if backward:
            for which in (1, 0):
                for copy in stores(c, which):
                    copy.start()

    expert_y = y_buf[...] if forward else y_in[...]
    if backward:
        gate_grad = jnp.sum(branch_buf[...].astype(f32) * expert_y, axis=-1, keepdims=True)
        logit_grad = gate_grad * gate * (is_mine.astype(f32) - probs)
        first, second = split(logit_grad)
        router_grad[...] = t_dot(first, sent) + t_dot(second, sent)
        back_buf[...] += dot(first, router[plan.layer]) + dot(second, router[plan.layer])
        scatter(back_buf[...].astype(bf16), back_parts)
    if forward:
        scatter((gate * expert_y).astype(bf16), parts)
        if not backward:
            sent_out[...] = sent
            y_out[...] = expert_y
    if backward:

        @pl.loop(0, chunks)
        def _(c):
            for which in (0, 1):
                for copy in stores(c, which):
                    copy.wait()


class Plan:
    def __init__(self, layer, block, images, grads, w_in, w_out, grad_shapes, grad_in, grad_out):
        self.layer, self.block = layer, block
        self.images, self.grads = images, grads
        self.w_in, self.w_out = w_in, w_out
        self.grad_shapes, self.grad_in, self.grad_out = grad_shapes, grad_in, grad_out


def expert_layer(plan, offsets, me, tables, router, tokens, saved, weights, flops=1):
    forward, backward = plan.images is not None, plan.grads is not None
    plan.token_arrays, plan.weight_arrays = len(tokens), len(weights)
    width = router.shape[2]
    count = len(plan.w_in)
    near, chunks, rows, hidden = plan.block
    slots = 2 * SLOTS
    shape = jax.ShapeDtypeStruct
    token_part = shape((4, ROWS, width), bf16)
    operands = [offsets, me, *tables, router, *tokens]
    in_specs = [smem(), smem()] + [vmem()] * (3 + len(tokens))
    if not forward:
        operands += saved
        in_specs += [vmem()] * 2
    operands += weights
    in_specs += [hbm()] * len(weights)
    out_shape, out_specs = [], []
    if forward:
        out_shape += [token_part] * 2
    if forward and not backward:
        out_shape += [shape((slots, width), bf16), shape((slots, width), f32)]
    if backward:
        out_shape += [token_part] * 2 + [shape(router.shape[1:], f32)]
    out_specs += [vmem()] * len(out_shape)
    if backward:
        out_shape += [shape(s, bf16) for s in plan.grad_shapes]
        out_specs += [hbm()] * len(plan.grad_shapes)
    scratch = [
        pltpu.VMEM((chunks, width, hidden), bf16),
        pltpu.VMEM((chunks, width, hidden), bf16),
        pltpu.VMEM((slots, width), bf16),
        pltpu.VMEM((slots, width), f32),
    ]
    if backward:
        scratch += [
            pltpu.VMEM((slots, width), bf16),
            pltpu.VMEM((slots, width), bf16),
            pltpu.VMEM((width, slots), bf16),
            pltpu.VMEM((width, slots), bf16),
            pltpu.VMEM((slots, width), f32),
            pltpu.VMEM((2, chunks, width, hidden), bf16),
            pltpu.SemaphoreType.DMA((2, chunks, count * near)),
        ]
    scratch += [pltpu.SemaphoreType.DMA((2, chunks, count * near))]
    return pl.pallas_call(
        lambda *refs: expert_kernel(plan, *refs),
        out_shape=tuple(out_shape),
        in_specs=in_specs,
        out_specs=tuple(out_specs),
        scratch_shapes=scratch,
        compiler_params=params(),
        cost_estimate=pl.CostEstimate(flops=flops, transcendentals=0, bytes_accessed=1),
        name="expert_layer",
    )(*operands)


def padded_bf16(rows):
    return jnp.pad(rows.astype(bf16), ((0, ROWS - LEN), (0, 0)))


def per_device(
    inputs,
    norm_gains,
    qkv_weight,
    out_weight,
    router_weight,
    expert_in,
    expert_out,
    routes,
    priority,
    cotangent,
):
    place = Place()
    experts = expert_in.shape[1]
    rows = qkv_weight.shape[1]
    zero = jnp.zeros((1,), jnp.int32)
    attn_off, expert_off = zero, zero
    me = place.expert.astype(jnp.int32).reshape(1)
    routers = jnp.swapaxes(router_weight, 1, 2)
    attn_w, expert_w = [], []
    tables = slot_tables(place, routes, priority, experts)
    for l in range(LAYERS):
        shard = jnp.concatenate([qkv_weight[l], jnp.swapaxes(out_weight[l], 0, 1)[:, None]], axis=1)
        full = gather_attention(place, shard.reshape(rows, -1))
        attn_w.append([full[j][None] for j in range(4)])
        expert_w.append([w[None] for w in gather_experts(place, expert_in[l], expert_out[l])])
    hidden_in, hidden_mid, qkv, ctx = {}, {}, {}, {}
    base, pieces = inputs, []
    saved = None
    gain_list, router_list, in_list, out_list, attn_list = {}, {}, {}, {}, {}
    for l in range(LAYERS):
        last = l == LAYERS - 1
        hidden_in[l], hidden_mid[l], normed, qkv[l], ctx[l] = attention_forward(
            attn_off, base, pieces, [], norm_gains[l], attn_w[l]
        )
        images = exchange_rows(place, normed)
        block = expert_w[l][0].shape
        at = [(0, None)], [(1, None)]
        here = [(j, 0) for j in range(8)]
        if last:
            grads = exchange_rows(place, padded_bf16(cotangent)[None])
            plan = Plan(l, block, here, [(j + 8, 0) for j in range(8)], *at, [block] * 2, *at)
            result = expert_layer(
                plan, expert_off, me, tables, routers, images + grads, None, expert_w[l]
            )
            tail = send_rows(place, pair_rows(place, result[:2]))
            result = result[2:]
            outputs = hidden_mid[l] + sum(p.astype(f32) for p in tail)
        else:
            plan = Plan(l, block, here, None, *at, None, None, None)
            *result, sent, expert_y = expert_layer(
                plan, expert_off, me, tables, routers, images, None, expert_w[l]
            )
            base, pieces = hidden_mid[l], send_rows(place, pair_rows(place, result))
            saved = [sent, expert_y]
    base = cotangent
    for l in reversed(range(LAYERS)):
        back = send_rows(place, pair_rows(place, result[:2]))
        router_list[l], *pieces = result[2:]
        in_list[l], out_list[l] = scatter_experts(place, pieces[0][0], pieces[1][0])
        base, branch, gain_list[l], *parts = attention_backward(
            attn_off, base, back, hidden_in[l], hidden_mid[l], norm_gains[l], attn_w[l], qkv[l], ctx[l],
            ROWS if l else LEN,
        )
        if l:
            grads = exchange_rows(place, branch[None])
            plan = Plan(l - 1, block, None, here, *at, [block] * 2, *at)
            result = expert_layer(
                plan, expert_off, me, tables, routers, grads, saved, expert_w[l - 1]
            )
        total = scatter_attention(place, jnp.concatenate(parts), rows)
        attn_list[l] = total.astype(f32).reshape(rows, 4, -1)
    gains = jnp.stack([gain_list[l] for l in range(LAYERS)])
    router = jnp.stack([router_list[l] for l in range(LAYERS)])
    small = jnp.concatenate([gains.reshape(-1), router.reshape(-1)]).reshape(-1, 512)
    for bit in range(place.count.bit_length() - 1):
        small = small + place.swap(small, 1 << bit)
    small = small.reshape(-1)
    gains, router = small[: gains.size].reshape(gains.shape), small[gains.size :].reshape(router.shape)
    return (
        outputs[:LEN].astype(bf16),
        base,
        gains,
        jnp.stack([attn_list[l][:, :3] for l in range(LAYERS)]),
        jnp.stack([jnp.swapaxes(attn_list[l][:, 3], 0, 1) for l in range(LAYERS)]),
        jnp.swapaxes(router, 1, 2),
        jnp.stack([in_list[l] for l in range(LAYERS)]),
        jnp.stack([out_list[l] for l in range(LAYERS)]),
    )


CORE, Y, X, NEAR, FAR = 1, 2, 4, 8, 16


def tie(*values):
    return lax.optimization_barrier(values)


def expert_blocks(place, w_in, w_out):
    order = place.expert ^ jnp.arange(w_in.shape[0])
    return jnp.stack([w_in[order], jnp.swapaxes(w_out, 1, 2)[order]])


def chip_pairs(place, blocks):
    return jnp.stack([blocks[:, 0::2], place.swap(blocks[:, 1::2], CORE)], axis=2)


def send_pairs(place, pair):
    two, chips, cores, rows, width = pair.shape
    got = [pair[:, 0]] + [place.swap(pair[:, k], 2 * k) for k in (1, 2, 3)]
    return jnp.stack(got, axis=1).reshape(two, 2, chips * cores // 2, rows, width)


def plane_blocks(place, blocks):
    return send_pairs(place, chip_pairs(place, blocks))


def mixed(place, value, even, odd):
    pairs = [(i, i ^ (odd if i & CORE else even)) for i in range(place.count)]
    return lax.ppermute(value, AXES, pairs)


def attention_shard(qkv_weight, out_weight):
    shard = jnp.concatenate([qkv_weight, jnp.swapaxes(out_weight, 0, 1)[:, None]], axis=1)
    return shard.reshape(shard.shape[0], -1)


def widen(place, held, mask):
    return jnp.concatenate([held, place.swap(held, mask)])


def halve(place, held, mask):
    half = held.shape[0] // 2
    return held[:half] + place.swap(held[half:], mask)


def send_sums(place, pair):
    return [pair[:, 0]] + [place.swap(pair[:, k], 2 * k) for k in (1, 2, 3)]


def unpack_kernel(layer, filled, me_ref, *refs):
    pieces, refs = refs[:4], refs[4 + 2 * filled :]
    in_ref, out_ref, in_buf, out_buf, sems = refs
    copies = []
    for k, piece in enumerate(pieces):
        for core in (0, 1):
            j = 2 * k + core
            expert = jnp.bitwise_xor(me_ref[0], j)
            in_buf[j] = piece[0, core].astype(f32)
            out_buf[j] = piece[1, core].astype(f32)
            copies.append(pltpu.make_async_copy(in_buf.at[j], in_ref.at[layer, expert], sems.at[0, j]))
            copies.append(pltpu.make_async_copy(out_buf.at[j], out_ref.at[layer, expert], sems.at[1, j]))
            for copy in copies[-2:]:
                copy.start()
    for copy in copies:
        copy.wait()


def unpack_sums(me, pieces, layer, layers, before=()):
    unused, cores, rows, width = pieces[0].shape
    experts = cores * len(pieces)
    shape = jax.ShapeDtypeStruct
    return pl.pallas_call(
        lambda *refs: unpack_kernel(layer, len(before) // 2, *refs),
        out_shape=(shape((layers, experts, rows, width), f32),) * 2,
        in_specs=[smem()] + [vmem()] * len(pieces) + [hbm()] * len(before),
        out_specs=(hbm(), hbm()),
        scratch_shapes=[
            pltpu.VMEM((experts, rows, width), f32),
            pltpu.VMEM((experts, rows, width), f32),
            pltpu.SemaphoreType.DMA((2, experts)),
        ],
        input_output_aliases={5: 0, 6: 1} if before else {},
        compiler_params=params(),
        cost_estimate=pl.CostEstimate(flops=1, transcendentals=0, bytes_accessed=1),
        name="unpack",
    )(me, *pieces, *before)


def per_device_plane(
    inputs,
    norm_gains,
    qkv_weight,
    out_weight,
    router_weight,
    expert_in,
    expert_out,
    routes,
    priority,
    cotangent,
):
    place = Place()
    swap = place.swap
    experts = expert_in.shape[1]
    rows = qkv_weight.shape[1]
    attn_order = [x | n * 2 | f * 4 for x in (0, 1) for n in (0, 1) for f in (0, 1)]
    attn_off = ((place.dp ^ jnp.array(attn_order, jnp.int32)) * rows).astype(jnp.int32)
    core = place.tensor & CORE
    replica = jnp.stack([jnp.zeros_like(core), 4 - 2 * core, 2 + 2 * core, 6 + 0 * core])
    expert_off = ((place.dp ^ replica[:, None] ^ jnp.arange(2)[None, :]) * rows).reshape(-1).astype(jnp.int32)
    me = place.expert.astype(jnp.int32).reshape(1)
    routers = jnp.swapaxes(router_weight, 1, 2)
    block = (2, place.tensor_size, rows, expert_in.shape[3])

    pair = chip_pairs(place, expert_blocks(place, expert_in[0], expert_out[0]))
    held = jnp.stack([attention_shard(qkv_weight[l], out_weight[l]) for l in (0, 1)])[None]
    pair, held = tie(pair, held)
    own0 = send_pairs(place, pair)
    held = widen(place, widen(place, held, FAR), NEAR)
    held, own0 = tie(held, own0)
    a0 = mixed(place, own0, FAR, NEAR)
    held = widen(place, held, X)
    held0, held1 = held[:, 0], held[:, 1]
    over0 = swap(held0, Y)
    tables = slot_tables(place, routes, priority, experts)
    over0, a0, blocks1, me, expert_off, *tables = tie(
        over0, a0, expert_blocks(place, expert_in[1], expert_out[1]), me, expert_off, *tables
    )
    b0, c0 = mixed(place, own0, NEAR, FAR), mixed(place, a0, NEAR, FAR)
    weights0 = [held0, swap(held0, CORE), over0, swap(over0, CORE)]
    own1 = plane_blocks(place, blocks1)

    hidden_in0, hidden_mid0, normed, qkv0, ctx0 = attention_forward(
        attn_off, inputs, [], [], norm_gains[0], weights0
    )
    normed, own1, held1 = tie(normed, own1, held1)
    images = exchange_rows(place, normed)
    over1 = swap(held1, Y)
    weights1 = [held1, swap(held1, CORE), over1, swap(over1, CORE)]
    tied = tie(*images, *weights1)
    images, weights1 = tied[:8], tied[8:]
    b0, c0, own1 = tie(b0, c0, own1)
    a1, b1 = mixed(place, own1, FAR, NEAR), mixed(place, own1, NEAR, FAR)
    first = [(j, 0) for j in range(8)]
    second = [(j, 1) for j in range(8)]
    parts = [[(m, io) for m in range(4)] for io in (0, 1)]
    *rows0, sent, expert_y = expert_layer(
        Plan(0, block, first, None, *parts, None, None, None),
        expert_off, me, tables, routers, images, None, [own0, a0, b0, c0],
    )
    pieces = send_rows(place, pair_rows(place, rows0))
    hidden_in1, hidden_mid1, normed, qkv1, ctx1 = attention_forward(
        attn_off, hidden_mid0, pieces, [cotangent], norm_gains[1], weights1
    )
    normed, a1 = tie(normed, a1)
    c1 = mixed(place, a1, NEAR, FAR)
    images = exchange_rows(place, normed)
    images[2], b1 = tie(images[2], b1)
    grad_shapes = [(2,) + block, (2,) + block, (2, 2) + block]
    grad_parts = [[(0, io), (1, io), (2, (0, io)), (2, (1, io))] for io in (0, 1)]
    result = expert_layer(
        Plan(1, block, first, second, *parts, grad_shapes, *grad_parts),
        expert_off, me, tables, routers, images, None, [own1, a1, b1, c1],
    )
    out_rows, back_rows, router1, (own, a, bc) = result[:2], result[2:4], result[4], result[5:]
    bc = mixed(place, bc, NEAR, FAR)
    pieces = send_rows(place, pair_rows(place, back_rows))
    grad1, branch, gains1, *parts1 = attention_backward(
        attn_off, cotangent, pieces, hidden_in1, hidden_mid1, norm_gains[1], weights1, qkv1, ctx1, ROWS
    )
    far1 = parts1[2] + swap(parts1[3], CORE)
    images = exchange_rows(place, branch[None])
    tied = tie(*images, a, bc, far1)
    images, (a, bc, far1) = tied[:8], tied[8:]
    far1 = swap(far1, Y)
    a = mixed(place, a + bc[1], FAR, NEAR)
    result = expert_layer(
        Plan(0, block, None, first, *parts, grad_shapes, *grad_parts),
        expert_off, me, tables, routers, images, [sent, expert_y], [own0, a0, b0, c0],
        flops=10**10,
    )
    back_rows, router0, (own0, a0, bc0) = result[:2], result[2], result[3:]
    *back_rows, far1 = tie(*back_rows, far1)
    bc0 = mixed(place, bc0, NEAR, FAR)
    pieces = send_rows(place, pair_rows(place, back_rows))
    pieces[3], a = tie(pieces[3], a)
    grad0, unused, gains0, *parts0 = attention_backward(
        attn_off, grad1, pieces, hidden_in0, hidden_mid0, norm_gains[0], weights0, qkv0, ctx0, LEN
    )
    gains0, a0, a, bc, own, *out_rows = tie(gains0, a0, a, bc, own, *out_rows)
    gains, router = jnp.stack([gains0, gains1]), jnp.stack([router0, router1])
    small = jnp.concatenate([gains.reshape(-1), router.reshape(-1)]).reshape(-1, 512)
    recv = [swap(v, CORE) for v in (parts0[3], parts0[1], parts1[1])]
    *recv, sum1, parts0[0], parts0[2], parts1[0] = tie(
        *recv, own + bc[0] + a, parts0[0], parts0[2], parts1[0]
    )
    far0, near0, near1 = parts0[2] + recv[0], parts0[0] + recv[1], parts1[0] + recv[2]
    far0 = swap(far0, Y)
    sum1 = send_sums(place, chip_pairs(place, sum1.reshape((2, -1) + sum1.shape[3:])))
    attn_sum = [halve(place, near + far, X) for near, far in ((near0, far0), (near1, far1))]
    attn_sum = jnp.stack(attn_sum, axis=1)
    tied = tie(*sum1, bc0, a0, small, *out_rows)
    sum1, (bc0, a0, small), out_rows = tied[:4], tied[4:7], tied[7:]
    a0 = mixed(place, a0 + bc0[1], FAR, NEAR)
    tail = send_rows(place, pair_rows(place, out_rows))
    for mask in (CORE, X, Y):
        small = small + swap(small, mask)
    grads1 = unpack_sums(me, sum1, 1, LAYERS)
    tied = tie(attn_sum, small, a0, *grads1, *tail)
    (attn_sum, small, a0), grads1, tail = tied[:3], tied[3:5], tied[5:]
    outputs = hidden_mid1 + sum(p.astype(f32) for p in tail)
    sum0 = own0 + a0 + bc0[0]
    pair0 = chip_pairs(place, sum0.reshape((2, -1) + sum0.shape[3:]))
    pair0, attn_sum, small = tie(pair0, attn_sum, small)
    sum0 = send_sums(place, pair0)
    for mask in (NEAR, FAR):
        attn_sum = halve(place, attn_sum, mask)
        small = small + swap(small, mask)
    in_grads, out_grads = unpack_sums(me, sum0, 0, LAYERS, grads1)
    small = small.reshape(-1)
    gains, router = small[: gains.size].reshape(gains.shape), small[gains.size :].reshape(router.shape)
    attn = attn_sum.astype(f32).reshape(2, rows, 4, -1)
    return (
        outputs[:LEN].astype(bf16),
        grad0,
        gains,
        attn[:, :, :3],
        jnp.swapaxes(attn[:, :, 3], 1, 2),
        jnp.swapaxes(router, 1, 2),
        in_grads,
        jnp.swapaxes(out_grads, 2, 3),
    )


def solution(mesh):
    in_specs = (
        P(("dp", "tensor"), None),
        P(),
        P(None, "dp", None, "tensor"),
        P(None, "tensor", "dp"),
        P(),
        P(None, None, "dp", "tensor"),
        P(None, None, "tensor", "dp"),
        P(None, "dp", None),
        P(None, "dp", None),
        P(("dp", "tensor"), None),
    )
    out_specs = (
        P(("dp", "tensor"), None),
        P(("dp", "tensor"), None),
        P(),
        P(None, "dp", None, "tensor"),
        P(None, "tensor", "dp"),
        P(),
        P(None, None, "dp", "tensor"),
        P(None, None, "tensor", "dp"),
    )
    fast = mesh.shape["dp"] == 8 and mesh.shape["tensor"] == 4 and LAYERS == 2
    return jax.shard_map(
        per_device_plane if fast else per_device, mesh=mesh, in_specs=in_specs, out_specs=out_specs, check_vma=False
    )
```

```python
import jax
import jax.numpy as jnp
from jax import lax
from jax.experimental import pallas as pl
from jax.experimental.pallas import tpu as pltpu
from jax.sharding import PartitionSpec as P

HD = 64
LEN = 197
LAYERS = 2
CAP = 247
SLOTS = 256
ROWS = 200
NORM_EPS = 1e-06
f32 = jnp.float32
bf16 = jnp.bfloat16
AXES = ("dp", "tensor")


def mm(spec, *args):
    return jnp.einsum(spec, *args, preferred_element_type=f32)


class Place:
    def __init__(self):
        self.dp_size = lax.axis_size("dp")
        self.tensor_size = lax.axis_size("tensor")
        self.count = self.dp_size * self.tensor_size
        self.dp = lax.axis_index("dp")
        self.tensor = lax.axis_index("tensor")
        self.near = self.dp & 1
        self.expert = self.near * self.tensor_size + self.tensor

    def swap(self, value, mask):
        pairs = [(i, i ^ mask) for i in range(self.count)]
        return lax.ppermute(value, AXES, pairs)

    def dp_groups(self):
        return [[d for d in range(self.dp_size) if d & 1 == b] for b in (0, 1)]

    def ordered(self, mine, theirs, bit):
        return jnp.stack([jnp.where(bit, theirs, mine), jnp.where(bit, mine, theirs)])


def gather_attention(place, shard):
    rows, width = shard.shape
    bits = place.dp_size.bit_length() - 1
    held = shard
    for bit in reversed(range(bits)):
        other = place.swap(held, place.tensor_size << bit)
        held = place.ordered(held, other, (place.dp >> bit) & 1)
    held = held.reshape((2,) * bits + (rows, width))
    held = jnp.transpose(held, tuple(reversed(range(bits))) + (bits, bits + 1))
    held = held.reshape(1, place.dp_size * rows, width)
    for mask in (2, 1):
        held = jnp.stack([held, place.swap(held, mask)], axis=1 if mask == 1 else 0)
        held = held.reshape((-1,) + held.shape[2:])
    return held


def scatter_attention(place, blocks, rows):
    bits = place.dp_size.bit_length() - 1
    held = blocks.reshape((2, 2) + blocks.shape[1:])
    held = held[:, 0] + place.swap(held[:, 1], 1)
    held = held[0] + place.swap(held[1], 2)
    for bit in range(bits):
        parts = held.reshape((-1, 2, rows, held.shape[-1]))
        mine = lax.dynamic_index_in_dim(parts, (place.dp >> bit) & 1, 1, keepdims=False)
        theirs = lax.dynamic_index_in_dim(parts, 1 - ((place.dp >> bit) & 1), 1, keepdims=False)
        held = mine + place.swap(theirs, place.tensor_size << bit)
        held = held.reshape(-1, held.shape[-1])
    return held


def plane_exchange(place, blocks):
    even, odd = blocks[0::2], blocks[1::2]
    pair = jnp.stack([even, place.swap(odd, 1)], axis=1)
    got = [pair[0]] + [place.swap(pair[k], 2 * k) for k in (1, 2, 3)]
    return jnp.concatenate(got, axis=0)


def gather_experts(place, w_in, w_out):
    blocks = jnp.stack([w_in, jnp.swapaxes(w_out, 1, 2)], axis=1)
    experts, unused, rows, width = blocks.shape
    order = place.expert ^ jnp.arange(experts)
    got = plane_exchange(place, blocks[order])
    got = got.reshape((2, place.tensor_size, 2, rows, width))
    got = place.ordered(got[0], got[1], place.near)
    full = lax.all_gather(got, "dp", axis=0, tiled=False, axis_index_groups=place.dp_groups())
    full = jnp.transpose(full, (3, 2, 0, 1, 4, 5))
    full = full.reshape((2, place.tensor_size, -1, width))
    return full[0], full[1]


def scatter_experts(place, grad_in, grad_out):
    tensor, model, width = grad_in.shape
    rows = model // place.dp_size
    both = jnp.stack([grad_in, grad_out]).astype(bf16)
    both = both.reshape((2, tensor, -1, 2, rows, width))
    both = jnp.transpose(both, (2, 3, 1, 0, 4, 5))
    mine = lax.psum_scatter(
        both, "dp", scatter_dimension=0, tiled=False, axis_index_groups=place.dp_groups()
    )
    mine = place.ordered(mine[0], mine[1], place.near)
    got = plane_exchange(place, mine.reshape((-1, 2, rows, width)))
    order = place.expert ^ jnp.arange(got.shape[0])
    got = got[order].astype(f32)
    return got[:, 0], jnp.swapaxes(got[:, 1], 1, 2)


LANES = 256
SPLIT = 1


def slot_kernel(experts, mine_ref, ids, rank, mine, theirs):
    tensor = mine.shape[1]
    expert, other = mine_ref[0], mine_ref[1]
    here = mine_ref[2]
    for l in range(ids.shape[0]):
        choice = lax.broadcasted_iota(jnp.int32, (experts, tensor * LANES), 0)
        first, second = ids[l, 0:1, :] == choice, ids[l, 1:2, :] == choice
        order = rank[l : l + 1, :].astype(f32)
        column = jnp.broadcast_to(order, (8, tensor * LANES)).T[:, 0:1]
        earlier = (column < order).astype(f32).astype(bf16)
        both = jnp.concatenate([first.astype(f32), second.astype(f32)]).astype(bf16)
        counts = dot(both, earlier)
        total = jnp.sum(first.astype(f32), axis=1, keepdims=True)
        slot = jnp.where(first, counts[:experts], jnp.where(second, total + counts[experts:], -1.0))
        slot = jnp.where(slot < CAP, slot, -1.0)
        for which, target in ((expert, mine), (other, theirs)):
            row = jnp.sum(jnp.where(choice == which, slot, 0.0), axis=0, keepdims=True).astype(jnp.int32)
            for t in range(tensor):
                target[l, pl.ds(jnp.bitwise_xor(here, t), 1), :] = row[:, t * LANES : (t + 1) * LANES]


def slot_tables(place, routes, priority, experts):
    layers, count, unused = routes.shape
    spread = ((0, 0), (0, 0), (0, 0), (0, LANES - LEN))
    ids = jnp.swapaxes(routes, 1, 2).reshape(layers, 2, -1, LEN)
    ids = jnp.pad(ids, spread, constant_values=-1).reshape(layers, 2, -1)
    rank = jnp.pad(priority.reshape(layers, 1, -1, LEN), spread).reshape(layers, -1)
    where = jnp.stack([place.expert, place.expert ^ place.tensor_size, place.tensor]).astype(jnp.int32)
    shape = jax.ShapeDtypeStruct((layers, place.tensor_size, LANES), jnp.int32)
    mine, theirs = pl.pallas_call(
        lambda *refs: slot_kernel(experts, *refs),
        out_shape=(shape, shape),
        in_specs=[smem(), vmem(), vmem()],
        out_specs=(vmem(), vmem()),
        compiler_params=params(),
        cost_estimate=pl.CostEstimate(flops=1, transcendentals=0, bytes_accessed=1),
        name="slots",
    )(where, ids, rank)
    return mine, place.swap(theirs, place.tensor_size)


def exchange_rows(place, own):
    even = [own] + [place.swap(own, 2 * k) for k in (1, 2, 3)]
    odd = [place.swap(rows, 1) for rows in even]
    return [rows for pair in zip(even, odd) for rows in pair]


def add_kernel(even, odd, *sums):
    for k, target in enumerate(sums):
        target[...] = (even[k].astype(f32) + odd[k].astype(f32)).astype(bf16)


def pair_rows(place, parts, *others):
    even, odd = parts
    odd, *others = lax.optimization_barrier((place.swap(odd, 1), *others))
    return list(pl.pallas_call(
        add_kernel,
        out_shape=(jax.ShapeDtypeStruct(even.shape[1:], bf16),) * 4,
        in_specs=[vmem()] * 2,
        out_specs=(vmem(),) * 4,
        cost_estimate=pl.CostEstimate(flops=1, transcendentals=0, bytes_accessed=1),
        name="add_rows",
    )(even, odd)) + others


def send_rows(place, sums):
    return [sums[0]] + [place.swap(sums[k], 2 * k) for k in (1, 2, 3)]


def dot(a, b):
    return lax.dot_general(a, b, (((1,), (0,)), ((), ())), preferred_element_type=f32)


def dot_t(a, b):
    return lax.dot_general(a, b, (((1,), (1,)), ((), ())), preferred_element_type=f32)


def t_dot(a, b):
    return lax.dot_general(a, b, (((0,), (0,)), ((), ())), preferred_element_type=f32)


def normalized(rows):
    average = jnp.mean(rows, axis=-1, keepdims=True)
    centered = rows - average
    variance = jnp.mean(centered * centered, axis=-1, keepdims=True)
    scale = lax.rsqrt(variance + NORM_EPS)
    return centered * scale, scale


def norm_grad(rows, gain, grad):
    unit, scale = normalized(rows)
    scaled = grad * gain
    pull = scaled - jnp.mean(scaled, axis=-1, keepdims=True)
    pull = pull - unit * jnp.mean(scaled * unit, axis=-1, keepdims=True)
    return scale * pull, jnp.sum(grad * unit, axis=0, keepdims=True)


def head_masks():
    lane = lax.broadcasted_iota(jnp.int32, (1, 2 * HD), 1)
    return lane < HD, lane >= HD


def only(values, mask):
    return jnp.where(mask, values.astype(f32), 0.0).astype(bf16)


def head_probs(queries, keys, mask):
    scores = dot_t(only(queries, mask), keys) * (HD ** (-0.5))
    valid = lax.broadcasted_iota(jnp.int32, scores.shape, 1) < LEN
    scores = jnp.where(valid, scores, -1e30)
    top = jnp.max(scores, axis=-1, keepdims=True)
    weights = jnp.exp(scores - top)
    return weights / jnp.sum(weights, axis=-1, keepdims=True)


def weight_copies(off_ref, pieces, buffer, sems):
    result = []
    for j, piece in enumerate(pieces):
        count, rows, unused = piece.shape
        result.append([
            pltpu.make_async_copy(
                piece.at[i],
                buffer.at[j, pl.ds(pl.multiple_of(off_ref[i], rows), rows)],
                sems.at[j, i],
            )
            for i in range(count)
        ])
    return result


def padded_rows(ref, scratch):
    if ref.shape[0] == ROWS:
        return ref[...].astype(f32)
    scratch[...] = jnp.zeros_like(scratch)
    scratch[0 : ref.shape[0]] = ref[...].astype(f32)
    return scratch[...]


def attention_forward_kernel(piece_count, extra_count, off_ref, base, *refs):
    pieces, refs = refs[:piece_count], refs[piece_count:]
    extra, refs = refs[:extra_count], refs[extra_count:]
    gains, w0, w1, w2, w3, hidden, mid, normed, qkv, ctx, scratch, wbuf, sems = refs
    copies = weight_copies(off_ref, (w0, w1, w2, w3), wbuf, sems)
    for group in copies:
        for copy in group:
            copy.start()
    rows = padded_rows(base, scratch)
    for piece in pieces:
        rows = rows + piece[...].astype(f32)
    hidden[...] = rows
    unit, unused = normalized(rows)
    normed_a = (unit * gains[0:1]).astype(bf16)
    low, high = head_masks()
    for group in copies:
        for copy in group:
            copy.wait()

    @pl.loop(0, 4)
    def _(j):
        qkv[:, pl.ds(pl.multiple_of(j * 6 * HD, 6 * HD), 6 * HD)] = dot(normed_a, wbuf[j, :, : 6 * HD]).astype(bf16)

    probs = []
    for j in range(4):
        part = qkv[:, j * 6 * HD : (j + 1) * 6 * HD]
        probs.append([head_probs(part[:, : 2 * HD], part[:, 2 * HD : 4 * HD], m).astype(bf16) for m in (low, high)])
    total = rows
    for j in range(4):
        values = qkv[:, j * 6 * HD + 4 * HD : (j + 1) * 6 * HD]
        context = jnp.where(low, dot(probs[j][0], values), dot(probs[j][1], values)).astype(bf16)
        ctx[:, j * 2 * HD : (j + 1) * 2 * HD] = context
        total = total + dot_t(context, wbuf[j, :, 6 * HD :])
    mid[...] = total
    unit, unused = normalized(total)
    normed[0] = (unit * gains[1:2]).astype(bf16)
    for ref in extra:
        normed[1] = padded_rows(ref, scratch).astype(bf16)


def vmem():
    return pl.BlockSpec(memory_space=pltpu.VMEM)


def smem():
    return pl.BlockSpec(memory_space=pltpu.SMEM)


def hbm():
    return pl.BlockSpec(memory_space=pl.ANY)


def params():
    return pltpu.CompilerParams(vmem_limit_bytes=60 << 20)


def attention_forward(offsets, base, pieces, extra, gains, weights):
    width = base.shape[1]
    shape = jax.ShapeDtypeStruct
    return pl.pallas_call(
        lambda *refs: attention_forward_kernel(len(pieces), len(extra), *refs),
        out_shape=(
            shape((ROWS, width), f32),
            shape((ROWS, width), f32),
            shape((1 + len(extra), ROWS, width), bf16),
            shape((ROWS, 3 * width), bf16),
            shape((ROWS, width), bf16),
        ),
        in_specs=[smem(), vmem()] + [vmem()] * (len(pieces) + len(extra)) + [vmem()] + [hbm()] * 4,
        out_specs=[vmem()] * 5,
        scratch_shapes=[
            pltpu.VMEM((ROWS, width), f32),
            pltpu.VMEM((4, width, width), bf16),
            pltpu.SemaphoreType.DMA((4, weights[0].shape[0])),
        ],
        compiler_params=params(),
        cost_estimate=pl.CostEstimate(flops=1, transcendentals=0, bytes_accessed=1),
        name="attention_forward",
    )(offsets, base, *pieces, *extra, gains, *weights)


def attention_backward_kernel(
    off_ref, base, p0, p1, p2, p3, hidden_in, hidden_mid, gains, w0, w1, w2, w3, qkv, ctx,
    grad_out, branch, gain_out, g0, g1, g2, g3, scratch, wbuf, gbuf, mixed_buf, back_buf, sems, out_sems,
):
    copies = weight_copies(off_ref, (w0, w1, w2, w3), wbuf, sems)
    for group in copies:
        for copy in group:
            copy.start()
    grad = padded_rows(base, scratch)
    normed_grad = p0[...].astype(f32) + p1[...].astype(f32) + p2[...].astype(f32) + p3[...].astype(f32)
    part, gain_expert = norm_grad(hidden_mid[...], gains[1:2], normed_grad)
    grad = grad + part
    attn_grad = grad.astype(bf16)
    attn_grad_t = attn_grad.T
    rows_in = hidden_in[...]
    unit, unused = normalized(rows_in)
    normed_t = (unit * gains[0:1]).astype(bf16).T
    low, high = head_masks()
    scale = HD ** (-0.5)
    for group in copies:
        for copy in group:
            copy.wait()
    heads = [(j, mask) for j in range(4) for mask in (low, high)]
    parts = [qkv[:, j * 6 * HD : (j + 1) * 6 * HD] for j in range(4)]
    queries = [part[:, : 2 * HD] for part in parts]
    keys = [part[:, 2 * HD : 4 * HD] for part in parts]
    values = [part[:, 4 * HD :] for part in parts]

    @pl.loop(0, 4)
    def _(j):
        back_buf[j] = dot(attn_grad, wbuf[j, :, 6 * HD :]).astype(bf16)

    context_grads = [back_buf[j] for j in range(4)]
    probs = [head_probs(queries[j], keys[j], mask) for j, mask in heads]
    probs_grads = [dot_t(only(context_grads[j], mask), values[j]) for j, mask in heads]
    v_grads = [t_dot(probs[i].astype(bf16), context_grads[j]) for i, (j, mask) in enumerate(heads)]
    score_grads = [
        (p * (g - jnp.sum(p * g, axis=-1, keepdims=True))).astype(bf16) for p, g in zip(probs, probs_grads)
    ]
    q_grads = [dot(score_grads[i], keys[j]) * scale for i, (j, mask) in enumerate(heads)]
    k_grads = [t_dot(score_grads[i], queries[j]) * scale for i, (j, mask) in enumerate(heads)]
    for j in range(4):
        mixed_buf[j] = jnp.concatenate(
            [jnp.where(low, g[2 * j], g[2 * j + 1]).astype(bf16) for g in (q_grads, k_grads, v_grads)], axis=1
        )
    scratch[...] = jnp.zeros_like(scratch)

    @pl.loop(0, 4)
    def _(j):
        mixed = mixed_buf[j]
        context = ctx[:, pl.ds(pl.multiple_of(j * 2 * HD, 2 * HD), 2 * HD)]
        gbuf[j, :, : 6 * HD] = dot(normed_t, mixed).astype(bf16)
        gbuf[j, :, 6 * HD :] = dot(attn_grad_t, context).astype(bf16)
        scratch[...] += dot_t(mixed, wbuf[j, :, : 6 * HD])

    normed_part = scratch[...]
    sends = []
    for j, target in enumerate((g0, g1, g2, g3)):
        count, rows, unused = target.shape
        for i in range(count):
            send = pltpu.make_async_copy(
                gbuf.at[j, pl.ds(pl.multiple_of(off_ref[i], rows), rows)], target.at[i], out_sems.at[j, i]
            )
            send.start()
            sends.append(send)
    part, gain_attn = norm_grad(rows_in, gains[0:1], normed_part)
    grad = grad + part
    grad_out[...] = grad[: grad_out.shape[0]]
    branch[...] = grad.astype(bf16)
    gain_out[...] = jnp.concatenate([gain_attn, gain_expert], axis=0)
    for send in sends:
        send.wait()


def attention_backward(offsets, base, pieces, hidden_in, hidden_mid, gains, weights, qkv, ctx, out_rows):
    width = base.shape[1]
    shape = jax.ShapeDtypeStruct
    blocks = weights[0].shape
    return pl.pallas_call(
        attention_backward_kernel,
        out_shape=(
            shape((out_rows, width), f32),
            shape((ROWS, width), bf16),
            shape((2, width), f32),
        ) + (shape(blocks, bf16),) * 4,
        in_specs=[smem()] + [vmem()] * 8 + [hbm()] * 4 + [vmem()] * 2,
        out_specs=[vmem()] * 3 + [hbm()] * 4,
        scratch_shapes=[
            pltpu.VMEM((ROWS, width), f32),
            pltpu.VMEM((4, width, width), bf16),
            pltpu.VMEM((4, width, width), bf16),
            pltpu.VMEM((4, ROWS, 6 * HD), bf16),
            pltpu.VMEM((4, ROWS, 2 * HD), bf16),
            pltpu.SemaphoreType.DMA((4, blocks[0])),
            pltpu.SemaphoreType.DMA((4, blocks[0])),
        ],
        compiler_params=params(),
        cost_estimate=pl.CostEstimate(flops=1, transcendentals=0, bytes_accessed=1),
        name="attention_backward",
    )(offsets, base, *pieces, hidden_in, hidden_mid, gains, *weights, qkv, ctx)


def split(values):
    high = values.astype(bf16)
    return high, (values - high.astype(f32)).astype(bf16)


ROOT = 0.7978845608028654
CUBE = 0.044715


def expert_kernel(plan, off_ref, me_ref, mine, theirs, router, *refs):
    forward, backward = plan.images is not None, plan.grads is not None
    piece_count = len(plan.w_in)
    refs = list(refs)

    def take(count):
        taken, refs[:count] = refs[:count], []
        return taken

    tokens = take(plan.token_arrays)
    sent_in, y_in = take(2) if not forward else (None, None)
    sources = take(plan.weight_arrays)
    parts = take(1 if backward else 2) if forward else None
    sent_out, y_out = take(2) if forward and not backward else (None, None)
    if backward:
        back_parts = take(2)
        (router_grad,) = take(1)
        targets = take(len(plan.grad_shapes))
    in_buf, out_buf, sent_buf, y_buf = take(4)
    if backward:
        slot_buf, branch_buf, slot_t, sent_t, back_buf, gbuf, out_sems = take(7)
    (sems,) = take(1)

    near, chunks, rows, width = plan.block

    def loads(c, which):
        result = []
        for m in range(piece_count):
            for n in range(near):
                at = pl.ds(pl.multiple_of(off_ref[m * near + n], rows), rows)
                index, part = (plan.w_in, plan.w_out)[which][m]
                piece = sources[index] if part is None else sources[index].at[part]
                buf = (in_buf, out_buf)[which]
                result.append(
                    pltpu.make_async_copy(piece.at[n, c], buf.at[c, at], sems.at[which, c, m * near + n])
                )
        return result

    @pl.loop(0, chunks)
    def _(c):
        for which in (0, 1):
            for copy in loads(c, which):
                copy.start()

    def hot_rows(g, t, slot):
        row = (mine, theirs)[g][plan.layer, t : t + 1, :][:, :ROWS]
        return (row == slot).astype(f32).astype(bf16)

    def gather(images):
        for g in (0, 1):
            total = None
            for t in range(4):
                j = g * 4 + t
                slot = lax.broadcasted_iota(jnp.int32, (SLOTS, ROWS), 0)
                hot = hot_rows(g, t, slot)
                index, layer = images[j]
                part = dot(hot, tokens[index][layer])
                total = part if total is None else total + part
            yield g, total

    def scatter(slot_rows, parts):
        for g in (0, 1):
            for t in range(4):
                j = g * 4 + t
                slot = lax.broadcasted_iota(jnp.int32, (SLOTS, ROWS), 0)
                part = t_dot(hot_rows(g, t, slot), slot_rows[g * SLOTS : (g + 1) * SLOTS]).astype(bf16)
                parts[j % 2][j // 2] = part

    if forward:
        for g, rows_g in gather(plan.images):
            sent_buf[g * SLOTS : (g + 1) * SLOTS] = rows_g.astype(bf16)
    else:
        sent_buf[...] = sent_in[...]
    sent = sent_buf[...]
    logits = dot_t(sent, router[plan.layer])
    top = jnp.max(logits, axis=-1, keepdims=True)
    weights = jnp.exp(logits - top)
    probs = weights / jnp.sum(weights, axis=-1, keepdims=True)
    is_mine = lax.broadcasted_iota(jnp.int32, probs.shape, 1) == me_ref[0]
    gate = jnp.sum(jnp.where(is_mine, probs, 0.0), axis=-1, keepdims=True)

    if backward:
        for g, rows_g in gather(plan.grads):
            part = slice(g * SLOTS, (g + 1) * SLOTS)
            slot_buf[part] = (gate[part] * rows_g).astype(bf16)
            branch_buf[part] = rows_g.astype(bf16)
        slot_t[...] = slot_buf[...].T
        sent_t[...] = sent.T
        back_buf[...] = jnp.zeros_like(back_buf)
    if forward:
        y_buf[...] = jnp.zeros_like(y_buf)

    def stores(c, which):
        result = []
        for m in range(piece_count):
            for n in range(near):
                at = pl.ds(pl.multiple_of(off_ref[m * near + n], rows), rows)
                index, part = (plan.grad_in, plan.grad_out)[which][m]
                piece = targets[index] if part is None else targets[index].at[part]
                result.append(
                    pltpu.make_async_copy(
                        gbuf.at[which, c, at], piece.at[n, c], out_sems.at[which, c, m * near + n]
                    )
                )
        return result

    halves = [slice(h * width // SPLIT, (h + 1) * width // SPLIT) for h in range(SPLIT)]

    @pl.loop(0, chunks)
    def _(c):
        for which in (0, 1):
            for copy in loads(c, which):
                copy.wait()
        pres = [dot(sent_buf[...], in_buf[c, :, at]) for at in halves]
        act_grads = [dot(slot_buf[...], out_buf[c, :, at]) for at in halves] if backward else None
        for h, at in enumerate(halves):
            pre = pres[h]
            square = pre * pre
            bend = jnp.tanh(pre * (ROOT + ROOT * CUBE * square))
            rise = 0.5 + 0.5 * bend
            act = pre * rise
            low_act = act.astype(bf16)
            if forward:
                y_buf[...] += dot_t(low_act, out_buf[c, :, at])
            if backward:
                gbuf[1, c, :, at] = dot(slot_t[...], low_act).astype(bf16)
                slope = rise + act * ((1.0 - bend) * (ROOT + 3.0 * ROOT * CUBE * square))
                pre_grad = (act_grads[h] * slope).astype(bf16)
                gbuf[0, c, :, at] = dot(sent_t[...], pre_grad).astype(bf16)
                back_buf[...] += dot_t(pre_grad, in_buf[c, :, at])
        if backward:
            for which in (1, 0):
                for copy in stores(c, which):
                    copy.start()

    expert_y = y_buf[...] if forward else y_in[...]
    if backward:
        gate_grad = jnp.sum(branch_buf[...].astype(f32) * expert_y, axis=-1, keepdims=True)
        logit_grad = gate_grad * gate * (is_mine.astype(f32) - probs)
        first, second = split(logit_grad)
        router_grad[...] = t_dot(first, sent) + t_dot(second, sent)
        back_buf[...] += dot(first, router[plan.layer]) + dot(second, router[plan.layer])
        scatter(back_buf[...].astype(bf16), back_parts)
    if forward:
        if backward:
            parts[0][...] = (gate * expert_y).astype(bf16)
        else:
            scatter((gate * expert_y).astype(bf16), parts)
            sent_out[...] = sent
            y_out[...] = expert_y
    if backward:

        @pl.loop(0, chunks)
        def _(c):
            for which in (0, 1):
                for copy in stores(c, which):
                    copy.wait()


def place_kernel(layer, mine, theirs, rows, even, odd, tables):
    tables[0] = mine[layer]
    tables[1] = theirs[layer]

    @pl.loop(0, 2)
    def _(g):
        slot = lax.broadcasted_iota(jnp.int32, (SLOTS, ROWS), 0)
        group = rows[pl.ds(pl.multiple_of(g * SLOTS, SLOTS), SLOTS)]
        for t in range(4):
            hot = (tables[g, t : t + 1, :][:, :ROWS] == slot).astype(f32).astype(bf16)
            (even, odd)[t % 2][g * 2 + t // 2] = t_dot(hot, group).astype(bf16)


def place_rows(layer, tables, rows):
    part = jax.ShapeDtypeStruct((4, ROWS, rows.shape[1]), bf16)
    return pl.pallas_call(
        lambda *refs: place_kernel(layer, *refs),
        out_shape=(part, part),
        in_specs=[vmem()] * 3,
        out_specs=(vmem(), vmem()),
        scratch_shapes=[pltpu.VMEM((2, 4, LANES), jnp.int32)],
        compiler_params=params(),
        cost_estimate=pl.CostEstimate(flops=1, transcendentals=0, bytes_accessed=1),
        name="place_rows",
    )(*tables, rows)


class Plan:
    def __init__(self, layer, block, images, grads, w_in, w_out, grad_shapes, grad_in, grad_out):
        self.layer, self.block = layer, block
        self.images, self.grads = images, grads
        self.w_in, self.w_out = w_in, w_out
        self.grad_shapes, self.grad_in, self.grad_out = grad_shapes, grad_in, grad_out


def expert_layer(plan, offsets, me, tables, router, tokens, saved, weights, flops=1):
    forward, backward = plan.images is not None, plan.grads is not None
    plan.token_arrays, plan.weight_arrays = len(tokens), len(weights)
    width = router.shape[2]
    count = len(plan.w_in)
    near, chunks, rows, hidden = plan.block
    slots = 2 * SLOTS
    shape = jax.ShapeDtypeStruct
    token_part = shape((4, ROWS, width), bf16)
    operands = [offsets, me, *tables, router, *tokens]
    in_specs = [smem(), smem()] + [vmem()] * (3 + len(tokens))
    if not forward:
        operands += saved
        in_specs += [vmem()] * 2
    operands += weights
    in_specs += [hbm()] * len(weights)
    out_shape, out_specs = [], []
    if forward:
        out_shape += [shape((slots, width), bf16)] if backward else [token_part] * 2
    if forward and not backward:
        out_shape += [shape((slots, width), bf16), shape((slots, width), f32)]
    if backward:
        out_shape += [token_part] * 2 + [shape(router.shape[1:], f32)]
    out_specs += [vmem()] * len(out_shape)
    if backward:
        out_shape += [shape(s, bf16) for s in plan.grad_shapes]
        out_specs += [hbm()] * len(plan.grad_shapes)
    scratch = [
        pltpu.VMEM((chunks, width, hidden), bf16),
        pltpu.VMEM((chunks, width, hidden), bf16),
        pltpu.VMEM((slots, width), bf16),
        pltpu.VMEM((slots, width), f32),
    ]
    if backward:
        scratch += [
            pltpu.VMEM((slots, width), bf16),
            pltpu.VMEM((slots, width), bf16),
            pltpu.VMEM((width, slots), bf16),
            pltpu.VMEM((width, slots), bf16),
            pltpu.VMEM((slots, width), f32),
            pltpu.VMEM((2, chunks, width, hidden), bf16),
            pltpu.SemaphoreType.DMA((2, chunks, count * near)),
        ]
    scratch += [pltpu.SemaphoreType.DMA((2, chunks, count * near))]
    return pl.pallas_call(
        lambda *refs: expert_kernel(plan, *refs),
        out_shape=tuple(out_shape),
        in_specs=in_specs,
        out_specs=tuple(out_specs),
        scratch_shapes=scratch,
        compiler_params=params(),
        cost_estimate=pl.CostEstimate(flops=flops, transcendentals=0, bytes_accessed=1),
        name="expert_layer",
    )(*operands)


def padded_bf16(rows):
    return jnp.pad(rows.astype(bf16), ((0, ROWS - LEN), (0, 0)))


def per_device(
    inputs,
    norm_gains,
    qkv_weight,
    out_weight,
    router_weight,
    expert_in,
    expert_out,
    routes,
    priority,
    cotangent,
):
    place = Place()
    experts = expert_in.shape[1]
    rows = qkv_weight.shape[1]
    zero = jnp.zeros((1,), jnp.int32)
    attn_off, expert_off = zero, zero
    me = place.expert.astype(jnp.int32).reshape(1)
    routers = jnp.swapaxes(router_weight, 1, 2)
    attn_w, expert_w = [], []
    tables = slot_tables(place, routes, priority, experts)
    for l in range(LAYERS):
        shard = jnp.concatenate([qkv_weight[l], jnp.swapaxes(out_weight[l], 0, 1)[:, None]], axis=1)
        full = gather_attention(place, shard.reshape(rows, -1))
        attn_w.append([full[j][None] for j in range(4)])
        expert_w.append([w[None] for w in gather_experts(place, expert_in[l], expert_out[l])])
    hidden_in, hidden_mid, qkv, ctx = {}, {}, {}, {}
    base, pieces = inputs, []
    saved = None
    gain_list, router_list, in_list, out_list, attn_list = {}, {}, {}, {}, {}
    for l in range(LAYERS):
        last = l == LAYERS - 1
        hidden_in[l], hidden_mid[l], normed, qkv[l], ctx[l] = attention_forward(
            attn_off, base, pieces, [], norm_gains[l], attn_w[l]
        )
        images = exchange_rows(place, normed)
        block = expert_w[l][0].shape
        at = [(0, None)], [(1, None)]
        here = [(j, 0) for j in range(8)]
        if last:
            grads = exchange_rows(place, padded_bf16(cotangent)[None])
            plan = Plan(l, block, here, [(j + 8, 0) for j in range(8)], *at, [block] * 2, *at)
            result = expert_layer(
                plan, expert_off, me, tables, routers, images + grads, None, expert_w[l]
            )
            tail = send_rows(place, pair_rows(place, place_rows(l, tables, result[0])))
            result = result[1:]
            outputs = hidden_mid[l] + sum(p.astype(f32) for p in tail)
        else:
            plan = Plan(l, block, here, None, *at, None, None, None)
            *result, sent, expert_y = expert_layer(
                plan, expert_off, me, tables, routers, images, None, expert_w[l]
            )
            base, pieces = hidden_mid[l], send_rows(place, pair_rows(place, result))
            saved = [sent, expert_y]
    base = cotangent
    for l in reversed(range(LAYERS)):
        back = send_rows(place, pair_rows(place, result[:2]))
        router_list[l], *pieces = result[2:]
        in_list[l], out_list[l] = scatter_experts(place, pieces[0][0], pieces[1][0])
        base, branch, gain_list[l], *parts = attention_backward(
            attn_off, base, back, hidden_in[l], hidden_mid[l], norm_gains[l], attn_w[l], qkv[l], ctx[l],
            ROWS if l else LEN,
        )
        if l:
            grads = exchange_rows(place, branch[None])
            plan = Plan(l - 1, block, None, here, *at, [block] * 2, *at)
            result = expert_layer(
                plan, expert_off, me, tables, routers, grads, saved, expert_w[l - 1]
            )
        total = scatter_attention(place, jnp.concatenate(parts), rows)
        attn_list[l] = total.astype(f32).reshape(rows, 4, -1)
    gains = jnp.stack([gain_list[l] for l in range(LAYERS)])
    router = jnp.stack([router_list[l] for l in range(LAYERS)])
    small = jnp.concatenate([gains.reshape(-1), router.reshape(-1)]).reshape(-1, 512)
    for bit in range(place.count.bit_length() - 1):
        small = small + place.swap(small, 1 << bit)
    small = small.reshape(-1)
    gains, router = small[: gains.size].reshape(gains.shape), small[gains.size :].reshape(router.shape)
    return (
        outputs[:LEN].astype(bf16),
        base,
        gains,
        jnp.stack([attn_list[l][:, :3] for l in range(LAYERS)]),
        jnp.stack([jnp.swapaxes(attn_list[l][:, 3], 0, 1) for l in range(LAYERS)]),
        jnp.swapaxes(router, 1, 2),
        jnp.stack([in_list[l] for l in range(LAYERS)]),
        jnp.stack([out_list[l] for l in range(LAYERS)]),
    )


CORE, Y, X, NEAR, FAR = 1, 2, 4, 8, 16


def tie(*values):
    return lax.optimization_barrier(values)


def expert_blocks(place, w_in, w_out):
    order = place.expert ^ jnp.arange(w_in.shape[0])
    return jnp.stack([w_in[order], jnp.swapaxes(w_out, 1, 2)[order]])


def chip_pairs(place, blocks):
    return jnp.stack([blocks[:, 0::2], place.swap(blocks[:, 1::2], CORE)], axis=2)


def send_pairs(place, pair):
    two, chips, cores, rows, width = pair.shape
    got = [pair[:, 0]] + [place.swap(pair[:, k], 2 * k) for k in (1, 2, 3)]
    return jnp.stack(got, axis=1).reshape(two, 2, chips * cores // 2, rows, width)


def plane_blocks(place, blocks):
    return send_pairs(place, chip_pairs(place, blocks))


def mixed(place, value, even, odd):
    pairs = [(i, i ^ (odd if i & CORE else even)) for i in range(place.count)]
    return lax.ppermute(value, AXES, pairs)


def attention_shard(qkv_weight, out_weight):
    shard = jnp.concatenate([qkv_weight, jnp.swapaxes(out_weight, 0, 1)[:, None]], axis=1)
    return shard.reshape(shard.shape[0], -1)


def widen(place, held, mask):
    return jnp.concatenate([held, place.swap(held, mask)])


def halve(place, held, mask):
    half = held.shape[0] // 2
    return held[:half] + place.swap(held[half:], mask)


def send_sums(place, pair):
    return [pair[:, 0]] + [place.swap(pair[:, k], 2 * k) for k in (1, 2, 3)]


def unpack_kernel(layer, filled, me_ref, *refs):
    pieces, refs = refs[:4], refs[4 + 2 * filled :]
    in_ref, out_ref, in_buf, out_buf, sems = refs
    copies = []
    for k, piece in enumerate(pieces):
        for core in (0, 1):
            j = 2 * k + core
            expert = jnp.bitwise_xor(me_ref[0], j)
            in_buf[j] = piece[0, core].astype(f32)
            out_buf[j] = piece[1, core].astype(f32)
            copies.append(pltpu.make_async_copy(in_buf.at[j], in_ref.at[layer, expert], sems.at[0, j]))
            copies.append(pltpu.make_async_copy(out_buf.at[j], out_ref.at[layer, expert], sems.at[1, j]))
            for copy in copies[-2:]:
                copy.start()
    for copy in copies:
        copy.wait()


def unpack_sums(me, pieces, layer, layers, before=()):
    unused, cores, rows, width = pieces[0].shape
    experts = cores * len(pieces)
    shape = jax.ShapeDtypeStruct
    return pl.pallas_call(
        lambda *refs: unpack_kernel(layer, len(before) // 2, *refs),
        out_shape=(shape((layers, experts, rows, width), f32),) * 2,
        in_specs=[smem()] + [vmem()] * len(pieces) + [hbm()] * len(before),
        out_specs=(hbm(), hbm()),
        scratch_shapes=[
            pltpu.VMEM((experts, rows, width), f32),
            pltpu.VMEM((experts, rows, width), f32),
            pltpu.SemaphoreType.DMA((2, experts)),
        ],
        input_output_aliases={5: 0, 6: 1} if before else {},
        compiler_params=params(),
        cost_estimate=pl.CostEstimate(flops=1, transcendentals=0, bytes_accessed=1),
        name="unpack",
    )(me, *pieces, *before)


def per_device_plane(
    inputs,
    norm_gains,
    qkv_weight,
    out_weight,
    router_weight,
    expert_in,
    expert_out,
    routes,
    priority,
    cotangent,
):
    place = Place()
    swap = place.swap
    experts = expert_in.shape[1]
    rows = qkv_weight.shape[1]
    attn_order = [x | n * 2 | f * 4 for x in (0, 1) for n in (0, 1) for f in (0, 1)]
    attn_off = ((place.dp ^ jnp.array(attn_order, jnp.int32)) * rows).astype(jnp.int32)
    core = place.tensor & CORE
    replica = jnp.stack([jnp.zeros_like(core), 4 - 2 * core, 2 + 2 * core, 6 + 0 * core])
    expert_off = ((place.dp ^ replica[:, None] ^ jnp.arange(2)[None, :]) * rows).reshape(-1).astype(jnp.int32)
    me = place.expert.astype(jnp.int32).reshape(1)
    routers = jnp.swapaxes(router_weight, 1, 2)
    block = (2, place.tensor_size, rows, expert_in.shape[3])

    pair = chip_pairs(place, expert_blocks(place, expert_in[0], expert_out[0]))
    held = jnp.stack([attention_shard(qkv_weight[l], out_weight[l]) for l in (0, 1)])[None]
    pair, held = tie(pair, held)
    own0 = send_pairs(place, pair)
    held = widen(place, widen(place, held, FAR), NEAR)
    held, own0 = tie(held, own0)
    a0 = mixed(place, own0, FAR, NEAR)
    held = widen(place, held, X)
    held0, held1 = held[:, 0], held[:, 1]
    over0 = swap(held0, Y)
    tables = slot_tables(place, routes, priority, experts)
    over0, a0, blocks1, me, expert_off, *tables = tie(
        over0, a0, expert_blocks(place, expert_in[1], expert_out[1]), me, expert_off, *tables
    )
    b0, c0 = mixed(place, own0, NEAR, FAR), mixed(place, a0, NEAR, FAR)
    weights0 = [held0, swap(held0, CORE), over0, swap(over0, CORE)]
    own1 = plane_blocks(place, blocks1)

    hidden_in0, hidden_mid0, normed, qkv0, ctx0 = attention_forward(
        attn_off, inputs, [], [], norm_gains[0], weights0
    )
    normed, own1, held1 = tie(normed, own1, held1)
    images = exchange_rows(place, normed)
    over1 = swap(held1, Y)
    weights1 = [held1, swap(held1, CORE), over1, swap(over1, CORE)]
    tied = tie(*images, *weights1)
    images, weights1 = tied[:8], tied[8:]
    b0, c0, own1 = tie(b0, c0, own1)
    a1, b1 = mixed(place, own1, FAR, NEAR), mixed(place, own1, NEAR, FAR)
    first = [(j, 0) for j in range(8)]
    second = [(j, 1) for j in range(8)]
    parts = [[(m, io) for m in range(4)] for io in (0, 1)]
    *rows0, sent, expert_y = expert_layer(
        Plan(0, block, first, None, *parts, None, None, None),
        expert_off, me, tables, routers, images, None, [own0, a0, b0, c0],
    )
    pieces = send_rows(place, pair_rows(place, rows0))
    hidden_in1, hidden_mid1, normed, qkv1, ctx1 = attention_forward(
        attn_off, hidden_mid0, pieces, [cotangent], norm_gains[1], weights1
    )
    normed, a1 = tie(normed, a1)
    c1 = mixed(place, a1, NEAR, FAR)
    images = exchange_rows(place, normed)
    images[2], b1 = tie(images[2], b1)
    grad_shapes = [(2,) + block, (2,) + block, (2, 2) + block]
    grad_parts = [[(0, io), (1, io), (2, (0, io)), (2, (1, io))] for io in (0, 1)]
    result = expert_layer(
        Plan(1, block, first, second, *parts, grad_shapes, *grad_parts),
        expert_off, me, tables, routers, images, None, [own1, a1, b1, c1],
    )
    out_rows, back_rows, router1, (own, a, bc) = result[0], result[1:3], result[3], result[4:]
    bc = mixed(place, bc, NEAR, FAR)
    pieces = send_rows(place, pair_rows(place, back_rows))
    grad1, branch, gains1, *parts1 = attention_backward(
        attn_off, cotangent, pieces, hidden_in1, hidden_mid1, norm_gains[1], weights1, qkv1, ctx1, ROWS
    )
    far1 = parts1[2] + swap(parts1[3], CORE)
    images = exchange_rows(place, branch[None])
    tied = tie(*images, a, bc, far1)
    images, (a, bc, far1) = tied[:8], tied[8:]
    far1 = swap(far1, Y)
    a = mixed(place, a + bc[1], FAR, NEAR)
    result = expert_layer(
        Plan(0, block, None, first, *parts, grad_shapes, *grad_parts),
        expert_off, me, tables, routers, images, [sent, expert_y], [own0, a0, b0, c0],
        flops=10**10,
    )
    back_rows, router0, (own0, a0, bc0) = result[:2], result[2], result[3:]
    *back_rows, far1 = tie(*back_rows, far1)
    bc0 = mixed(place, bc0, NEAR, FAR)
    pieces = send_rows(place, pair_rows(place, back_rows))
    pieces[3], a = tie(pieces[3], a)
    grad0, unused, gains0, *parts0 = attention_backward(
        attn_off, grad1, pieces, hidden_in0, hidden_mid0, norm_gains[0], weights0, qkv0, ctx0, LEN
    )
    gains0, a0, a, bc, own, out_rows = tie(gains0, a0, a, bc, own, out_rows)
    out_rows = place_rows(1, tables, out_rows)
    gains, router = jnp.stack([gains0, gains1]), jnp.stack([router0, router1])
    small = jnp.concatenate([gains.reshape(-1), router.reshape(-1)]).reshape(-1, 512)
    small = jnp.pad(small, ((0, -small.shape[0] % 8), (0, 0)))
    recv = [swap(v, CORE) for v in (parts0[3], parts0[1], parts1[1])]
    *recv, sum1, parts0[0], parts0[2], parts1[0] = tie(
        *recv, own + bc[0] + a, parts0[0], parts0[2], parts1[0]
    )
    far0, near0, near1 = parts0[2] + recv[0], parts0[0] + recv[1], parts1[0] + recv[2]
    far0 = swap(far0, Y)
    sum1 = send_sums(place, chip_pairs(place, sum1.reshape((2, -1) + sum1.shape[3:])))
    attn_sum = [halve(place, near + far, X) for near, far in ((near0, far0), (near1, far1))]
    attn_sum = jnp.stack(attn_sum, axis=1)
    tied = tie(*sum1, bc0, a0, small, *out_rows)
    sum1, (bc0, a0, small), out_rows = tied[:4], tied[4:7], tied[7:]
    a0 = mixed(place, a0 + bc0[1], FAR, NEAR)
    tail = send_rows(place, pair_rows(place, out_rows))
    for mask in (CORE, X, Y):
        small = small + swap(small, mask)
    grads1 = unpack_sums(me, sum1, 1, LAYERS)
    tied = tie(attn_sum, small, a0, *grads1, *tail)
    (attn_sum, small, a0), grads1, tail = tied[:3], tied[3:5], tied[5:]
    outputs = hidden_mid1 + sum(p.astype(f32) for p in tail)
    sum0 = own0 + a0 + bc0[0]
    pair0 = chip_pairs(place, sum0.reshape((2, -1) + sum0.shape[3:]))
    pair0, attn_sum, small = tie(pair0, attn_sum, small)
    sum0 = send_sums(place, pair0)
    shape = attn_sum.shape
    attn_sum = attn_sum.reshape(-1, shape[-1])
    for mask in (NEAR, FAR):
        keep, count = attn_sum.shape[0] // 2, small.shape[0]
        got = swap(jnp.concatenate([attn_sum[keep:], *split(small)]), mask)
        attn_sum = attn_sum[:keep] + got[:keep]
        small = small + got[keep : keep + count].astype(f32) + got[keep + count :].astype(f32)
    in_grads, out_grads = unpack_sums(me, sum0, 0, LAYERS, grads1)
    small = small.reshape(-1)
    gains, router = small[: gains.size].reshape(gains.shape), small[gains.size : gains.size + router.size].reshape(router.shape)
    attn = attn_sum.astype(f32).reshape(2, rows, 4, -1)
    return (
        outputs[:LEN].astype(bf16),
        grad0,
        gains,
        attn[:, :, :3],
        jnp.swapaxes(attn[:, :, 3], 1, 2),
        jnp.swapaxes(router, 1, 2),
        in_grads,
        jnp.swapaxes(out_grads, 2, 3),
    )


def solution(mesh):
    in_specs = (
        P(("dp", "tensor"), None),
        P(),
        P(None, "dp", None, "tensor"),
        P(None, "tensor", "dp"),
        P(),
        P(None, None, "dp", "tensor"),
        P(None, None, "tensor", "dp"),
        P(None, "dp", None),
        P(None, "dp", None),
        P(("dp", "tensor"), None),
    )
    out_specs = (
        P(("dp", "tensor"), None),
        P(("dp", "tensor"), None),
        P(),
        P(None, "dp", None, "tensor"),
        P(None, "tensor", "dp"),
        P(),
        P(None, None, "dp", "tensor"),
        P(None, None, "tensor", "dp"),
    )
    fast = mesh.shape["dp"] == 8 and mesh.shape["tensor"] == 4 and LAYERS == 2
    return jax.shard_map(
        per_device_plane if fast else per_device, mesh=mesh, in_specs=in_specs, out_specs=out_specs, check_vma=False
    )
```
